32 devices in a mesh: rep: 2 (over y), shard: 16 (over z, x, core).
Axes of the slice: x: 2, y: 2, z: 4, core: 2. Of those that a mesh axis runs over, the one named last changes fastest.
Arguments:
- tokens: bfloat16 [65536, 768], P(('rep', 'shard')), may hold values from -6 to 6
- segment_ids: int32 [32, 2048], P(('rep', 'shard')), may hold values from 0 to 7, never falling along the last dimension, each value on 1 to 1024 neighbouring positions
- query_weight: bfloat16 [768, 768], P('shard'), may hold values from -0.21875 to 0.21875
- key_weight: bfloat16 [768, 768], P('shard'), may hold values from -0.21875 to 0.21875
- value_weight: bfloat16 [768, 768], P('shard'), may hold values from -0.21875 to 0.21875
- output_weight: bfloat16 [768, 768], P('shard'), may hold values from -0.875 to 0.875
- relative_table: bfloat16 [32, 768], P(None, 'shard'), may hold values from -6 to 6
- order_table: bfloat16 [2, 768], P(None, 'shard'), may hold values from -6 to 6
- content_bias: bfloat16 [768], P('shard'), may hold values from -3 to 3
- position_bias: bfloat16 [768], P('shard'), may hold values from -3 to 3
- order_bias: bfloat16 [768], P('shard'), may hold values from -3 to 3
- first_gain: bfloat16 [768], P('shard'), may hold values from 0.5 to 1.5
- first_shift: bfloat16 [768], P('shard'), may hold values from -2 to 2
- inner_weight: bfloat16 [768, 3072], P('shard'), may hold values from -0.21875 to 0.21875
- inner_bias: bfloat16 [3072], P('shard'), may hold values from -3 to 3
- outer_weight: bfloat16 [3072, 768], P('shard'), may hold values from -0.21875 to 0.21875
- outer_bias: bfloat16 [768], P('shard'), may hold values from -2 to 2
- second_gain: bfloat16 [768], P('shard'), may hold values from 0.5 to 1.5
- second_shift: bfloat16 [768], P('shard'), may hold values from -2 to 2
- cotangent: bfloat16 [32768, 768], P(('rep', 'shard')), may hold values from -6 to 6
Outputs:
- layer_out: bfloat16 [32768, 768], P(('rep', 'shard'))
- tokens_grad: float32 [65536, 768], P(('rep', 'shard'))
- query_weight_grad: float32 [768, 768], P('shard')
- key_weight_grad: float32 [768, 768], P('shard')
- value_weight_grad: float32 [768, 768], P('shard')
- output_weight_grad: float32 [768, 768], P('shard')
- relative_table_grad: float32 [32, 768], P(None, 'shard')
- order_table_grad: float32 [2, 768], P(None, 'shard')
- content_bias_grad: float32 [768], P('shard')
- position_bias_grad: float32 [768], P('shard')
- order_bias_grad: float32 [768], P('shard')
- first_gain_grad: float32 [768], P('shard')
- first_shift_grad: float32 [768], P('shard')
- inner_weight_grad: float32 [768, 3072], P('shard')
- inner_bias_grad: float32 [3072], P('shard')
- outer_weight_grad: float32 [3072, 768], P('shard')
- outer_bias_grad: float32 [768], P('shard')
- second_gain_grad: float32 [768], P('shard')
- second_shift_grad: float32 [768], P('shard')
The draws below stay inside these ranges and needn't reach their ends.
Inputs may be any that keep to these rules, and one draw needn't show every extreme that they name: `segment_ids`: each row holds the document numbers of one sequence: never falling, each document 1 to 1024 positions, one of exactly 1024.
All inputs are finite; a program needn't handle non-finite values.
Results may differ from the reference program's by a relative error of at most 0.02.
Values may be sent and summed in bfloat16 or wider, within the bound.
A program may use at most 192 MiB of HBM per device.

```python
import math
import jax
import jax.numpy as jnp
import numpy as np
from jax import lax

D = 768
H = 12
DH = 64
FF = 3072
NB = 32
DOCS = 8
SEQ = 2048
TOKENS = 65536
SEQUENCES = 32


def shard_levels(key, shape, shards, smallest, high):
    factor_of, own = 1.0, jax.random.fold_in(key, 6)
    for dim, parts in shards:
        draws = jnp.exp(jax.random.uniform(jax.random.fold_in(own, dim), (parts,), jnp.float32, smallest / len(shards), high / len(shards)))
        factor_of = factor_of * jnp.repeat(draws, shape[dim] // parts).reshape([-1 if axis == dim else 1 for axis in range(len(shape))])
    return factor_of


def split_up(number_of, total, bound, slope):
    portions = [(1 << 20) // math.isqrt(standing ** slope) + 1 for standing in range(2, number_of + 1)]
    surplus, given = total - bound - (number_of - 1), [1] * (number_of - 1)
    while surplus > 0:
        free = [i for i in range(number_of - 1) if given[i] < bound]
        mass, left = sum([portions[i] for i in free]), surplus
        for i in free:
            extra = min(bound - given[i], max(1, left * portions[i] // mass), surplus)
            given[i] = given[i] + extra
            surplus = surplus - extra
    return np.array([bound] + given)


def ragged(key, count, total, most, lean):
    if count == 2:
        one = jax.random.randint(key, (), max(1, total - most), min(most, total - 1) + 1)
        return jnp.stack([one, total - one])
    lengths = jnp.asarray(split_up(count, total, most, lean), jnp.int32)
    pairs = (count - 1) // 2
    source_of, sink = lengths[1:1 + 2 * pairs:2], lengths[2:2 + 2 * pairs:2]
    room = jnp.minimum(source_of - 1, most - sink)
    shifted = jax.random.randint(jax.random.fold_in(key, 1), (pairs,), 0, 1 << 20) % (room + 1)
    lengths = lengths.at[1:1 + 2 * pairs:2].set(source_of - shifted).at[2:2 + 2 * pairs:2].set(sink + shifted)
    return lengths[jax.random.permutation(jax.random.fold_in(key, 2), count)]


def bell_draw(stream_key, shape, deviation, most, cuts=(), kind=jnp.bfloat16):
    level = shard_levels(stream_key, shape, cuts, -0.22, 0.18) if cuts else 1.0
    drawn = jax.random.normal(stream_key, shape, jnp.float32) * deviation * level
    return jnp.minimum(jnp.maximum(drawn, -most), most).astype(kind)


def setup_inputs(seed: int = 0) -> dict:
    streams_of = jax.random.split(jax.random.key(seed), 21)
    tokens = bell_draw(streams_of[0], (TOKENS, D), 1.0, 6.0, ((0, 32),))
    segment_ids = jax.vmap(lambda own: jnp.searchsorted(jnp.cumsum(ragged(own, DOCS, SEQ, SEQ // 2, 2)), jnp.arange(SEQ), side="right"))(jax.random.split(streams_of[1], SEQUENCES)).reshape((SEQUENCES, SEQ)).astype(jnp.int32)
    query_weight = bell_draw(streams_of[2], (D, D), D ** -0.5, 0.21875, ((0, 16),))
    key_weight = bell_draw(streams_of[3], (D, D), D ** -0.5, 0.21875, ((0, 16),))
    value_weight = bell_draw(streams_of[4], (D, D), D ** -0.5, 0.21875, ((0, 16),))
    output_weight = bell_draw(streams_of[5], (D, D), (D // 16) ** -0.5, 0.875, ((0, 16),))
    relative_table = bell_draw(streams_of[6], (NB, D), 1.0, 6.0, ((1, 16),))
    order_table = bell_draw(streams_of[7], (2, D), 1.0, 6.0, ((1, 16),))
    content_bias = bell_draw(streams_of[8], (D,), 0.5, 3.0, ((0, 16),))
    position_bias = bell_draw(streams_of[9], (D,), 0.5, 3.0, ((0, 16),))
    order_bias = bell_draw(streams_of[10], (D,), 0.5, 3.0, ((0, 16),))
    first_gain = jnp.clip(1.0 + 0.1 * jax.random.normal(streams_of[11], (D,), jnp.float32), 0.5, 1.5).astype(jnp.bfloat16)
    first_shift = bell_draw(streams_of[12], (D,), 0.3, 2.0, ((0, 16),))
    inner_weight = bell_draw(streams_of[13], (D, FF), D ** -0.5, 0.21875, ((0, 16),))
    inner_bias = bell_draw(streams_of[14], (FF,), 0.5, 3.0, ((0, 16),))
    outer_weight = bell_draw(streams_of[15], (FF, D), (FF // 4) ** -0.5, 0.21875, ((0, 16),))
    outer_bias = bell_draw(streams_of[16], (D,), 0.3, 2.0, ((0, 16),))
    second_gain = jnp.clip(1.0 + 0.1 * jax.random.normal(streams_of[17], (D,), jnp.float32), 0.5, 1.5).astype(jnp.bfloat16)
    second_shift = bell_draw(streams_of[18], (D,), 0.3, 2.0, ((0, 16),))
    cotangent = bell_draw(streams_of[19], (TOKENS // 2, D), 1.0, 6.0, ((0, 32),))
    return dict(tokens=tokens, segment_ids=segment_ids, query_weight=query_weight, key_weight=key_weight, value_weight=value_weight, output_weight=output_weight, relative_table=relative_table, order_table=order_table, content_bias=content_bias, position_bias=position_bias, order_bias=order_bias, first_gain=first_gain, first_shift=first_shift, inner_weight=inner_weight, inner_bias=inner_bias, outer_weight=outer_weight, outer_bias=outer_bias, second_gain=second_gain, second_shift=second_shift, cotangent=cotangent)


@jax.custom_vjp
def low(v):
    return lax.optimization_barrier(v.astype(jnp.bfloat16)).astype(jnp.float32)

@jax.custom_vjp
def low_back(v):
    return v

def low_keep(v):
    return (low(v), None)

def low_pass(kept, grad):
    return (grad,)

def back_keep(v):
    return (v, None)

def back_low(kept, grad):
    return (low(grad),)
low.defvjp(low_keep, low_pass)
low_back.defvjp(back_keep, back_low)
LIMITS = (1, 2, 3, 4, 5, 6, 7, 8, 12, 16, 24, 32, 48, 64, 128)

def precise(left, right):
    return jnp.dot(left, right, precision=lax.Precision.HIGHEST, preferred_element_type=jnp.float32)

def bucket_table(length):
    query_pos = jnp.arange(length // 2, dtype=jnp.int32) * 2
    key_pos = jnp.arange(length, dtype=jnp.int32)
    offset = key_pos[None, :] - query_pos[:, None]
    distance = jnp.abs(offset)
    passed = jnp.zeros(offset.shape, jnp.int32)
    for limit in LIMITS:
        passed = passed + (distance >= limit).astype(jnp.int32)
    behind = offset < 0
    farther = (distance >= 256).astype(jnp.int32)
    return (jnp.where(behind, 15 + passed + farther, passed), behind)

def normalize(values, gain, shift):
    centered = values - lax.optimization_barrier(jnp.mean(values, axis=1, keepdims=True))
    inverse = lax.rsqrt(lax.optimization_barrier(jnp.mean(centered * centered, axis=1, keepdims=True)) + 1e-05)
    return centered * inverse * gain + shift

def sequence_forward(params, tokens, segments, bucket, behind):
    query_weight, key_weight, value_weight, output_weight, relative_table, order_table, content_bias, position_bias, order_bias, first_gain, first_shift, inner_weight, inner_bias, outer_weight, outer_bias, second_gain, second_shift = params
    length, width = tokens.shape
    half = length // 2
    scale = 1.0 / math.sqrt(DH)
    pairs = tokens.reshape(half, 2, width)
    query_seg = segments[0::2]
    joined = (query_seg == segments[1::2]).astype(jnp.float32)[:, None]
    pooled = (pairs[:, 0] + joined * pairs[:, 1]) / (1.0 + joined)
    queries = low_back(precise(low(pooled), query_weight))
    keys = low(low_back(precise(tokens, key_weight)))
    values = low(low_back(precise(tokens, value_weight)))
    content = low(queries + content_bias)
    position = low(queries + position_bias)
    ordering = low(queries + order_bias)
    same = query_seg[:, None] == segments[None, :]

    def split(array):
        return array.reshape(array.shape[0], H, DH).transpose(1, 0, 2)

    def attend(inputs):
        content_h, keys_h, values_h, position_h, order_h, relative_h, orders_h = inputs
        table = low_back(precise(position_h, relative_h.T))
        placed = jnp.take_along_axis(table, bucket, axis=1)
        ranked = low_back(precise(order_h, orders_h.T))
        ordered = jnp.where(behind, ranked[:, 1:2], ranked[:, 0:1])
        scores = low_back((precise(content_h, keys_h.T) + placed + ordered) * scale)
        scores = jnp.where(same, scores, -1e+30)
        probs = jax.nn.softmax(scores, axis=1)
        return precise(low(probs), values_h)
    relative_heads = relative_table.reshape(relative_table.shape[0], H, DH).transpose(1, 0, 2)
    order_heads = order_table.reshape(2, H, DH).transpose(1, 0, 2)
    heads_out = lax.map(jax.checkpoint(attend), (split(content), split(keys), split(values), split(position), split(ordering), relative_heads, order_heads))
    context = low(low_back(heads_out.transpose(1, 0, 2).reshape(half, width)))
    attended = low_back(precise(context, output_weight))
    first = normalize(pooled + attended, first_gain, first_shift)
    inner = low_back(precise(low(first), inner_weight) + inner_bias)
    outer = low_back(precise(low(jax.nn.gelu(inner, approximate=False)), outer_weight) + outer_bias)
    return normalize(first + outer, second_gain, second_shift)

def reference(tokens, segment_ids, query_weight, key_weight, value_weight, output_weight, relative_table, order_table, content_bias, position_bias, order_bias, first_gain, first_shift, inner_weight, inner_bias, outer_weight, outer_bias, second_gain, second_shift, cotangent):
    params = tuple((array.astype(jnp.float32) for array in (query_weight, key_weight, value_weight, output_weight, relative_table, order_table, content_bias, position_bias, order_bias, first_gain, first_shift, inner_weight, inner_bias, outer_weight, outer_bias, second_gain, second_shift)))
    bucket, behind = bucket_table(SEQ)
    blocks = tokens.astype(jnp.float32).reshape(-1, SEQ, D)
    incoming_all = cotangent.astype(jnp.float32).reshape(-1, SEQ // 2, D)

    def one_sequence(totals, inputs):
        pieces, segments, incoming = inputs

        def forward(weights, rows):
            return sequence_forward(weights, rows, segments, bucket, behind)
        result, pullback = jax.vjp(forward, params, pieces)
        weight_grads, row_grads = pullback(incoming)
        return (jax.tree.map(jnp.add, totals, weight_grads), (result.astype(jnp.bfloat16), row_grads))
    start = tuple((jnp.zeros_like(array) for array in params))
    totals, (results, row_grads) = lax.scan(one_sequence, start, (blocks, segment_ids, incoming_all))
    return (results.reshape(-1, D), row_grads.reshape(-1, D), totals[0], totals[1], totals[2], totals[3], totals[4], totals[5], totals[6], totals[7], totals[8], totals[9], totals[10], totals[11], totals[12], totals[13], totals[14], totals[15], totals[16])
```

```python
import math
import jax
import jax.numpy as jnp
import numpy as np
from jax import lax
from jax.experimental import pallas as pl
from jax.experimental.pallas import tpu as pltpu
from jax.sharding import PartitionSpec as P

LIMITS = (1, 2, 3, 4, 5, 6, 7, 8, 12, 16, 24, 32, 48, 64, 128)
BQ = 128
NEAR = 640
CHUNK = 256
LOG2E = math.log2(math.e)
LN2 = math.log(2.0)
BIG = 1e30
f32 = jnp.float32
bf16 = jnp.bfloat16


def bucket_of(offset):
    distance = np.abs(offset)
    passed = sum((distance >= limit).astype(np.int32) for limit in LIMITS)
    return np.where(offset < 0, 15 + passed + (distance >= 256), passed).astype(np.int32)


def near_index():
    row = np.arange(BQ)[None, :, None]
    tile = np.arange(-2, 3)[:, None, None]
    lane = np.arange(128)[None, None, :]
    return bucket_of(128 * tile + lane - 2 * row)


def bucket_onehot():
    out = np.zeros((7 * 128, 128), np.float32)
    offsets = np.concatenate([np.full(256, -300), np.arange(-256, 128), np.full(256, 300)])
    out[np.arange(896), bucket_of(offsets)] = 1
    out[:, 32] = offsets >= 0
    out[:, 33] = offsets < 0
    return out


def nt(left, right):
    return lax.dot_general(left, right, (((1,), (1,)), ((), ())), preferred_element_type=f32)


def nn(left, right):
    return lax.dot_general(left, right, (((1,), (0,)), ((), ())), preferred_element_type=f32)


def tn(left, right):
    return lax.dot_general(left, right, (((0,), (0,)), ((), ())), preferred_element_type=f32)


def halves(array):
    low = lax.broadcasted_iota(jnp.int32, array.shape, 1) < 64
    zero = jnp.zeros_like(array)
    return jnp.where(low, array, zero), jnp.where(low, zero, array)


def pick(array):
    half = array.shape[0] // 2
    low = lax.broadcasted_iota(jnp.int32, (half, 128), 1) < 64
    return jnp.where(low, array[:half], array[half:])


def take(table, index):
    return jnp.take_along_axis(table, index, axis=1, mode="promise_in_bounds")


def forward_kernel(
    behind_ref, ahead_ref, content_ref, position_ref, ordering_ref, key_ref, value_ref,
    relative_ref, order_ref, away_ref, document_ref, index_ref,
    probs_ref, context_ref, mixed_ref, inverse_ref,
    keys, values, table, scores, peak, total,
):
    step = pl.program_id(1)
    length = key_ref.shape[0]

    @pl.when(step == 0)
    def _():
        keys[: 256, :128] = jnp.zeros((256, 128), bf16)
        keys[256 + length :, :128] = jnp.zeros((256, 128), bf16)
        keys[256 : 256 + length, :128] = key_ref[...]
        keys[:, 128:] = away_ref[...]
        values[: 256, :128] = jnp.zeros((256, 128), bf16)
        values[256 + length :, :128] = jnp.zeros((256, 128), bf16)
        values[256 : 256 + length, :128] = value_ref[...]
        values[:, 128:] = jnp.ones((length + 512, 128), bf16)
        table[...] = jnp.zeros((256, 256), bf16)
        even, odd = halves(relative_ref[...])
        after = lax.broadcasted_iota(jnp.int32, (32, 128), 0) < 16
        orders = jnp.where(after, order_ref[0:1, :].astype(f32), order_ref[1:2, :].astype(f32))
        even_order, odd_order = halves(orders)
        table[0:32, :128] = even
        table[128:160, :128] = odd
        table[0:32, 128:] = even_order.astype(bf16)
        table[128:160, 128:] = odd_order.astype(bf16)

    even, odd = halves(content_ref[...])
    document = document_ref[...]
    query = jnp.concatenate(
        [jnp.concatenate([even, document], 1), jnp.concatenate([odd, document], 1)], 0
    )
    places = nt(jnp.concatenate([position_ref[...], ordering_ref[...]], 1), table[...]) * (0.125 * LOG2E)
    place = (places[:, :128], places[:, 128:])
    near = pl.multiple_of(step * 256, 256)
    near_scores = nt(query, keys[pl.ds(near, NEAR), :])
    best = None
    for tile in range(5):
        index = index_ref[tile]
        bias = jnp.concatenate([take(place[0], index), take(place[1], index)], 0)
        part = near_scores[:, tile * 128 : tile * 128 + 128] + bias
        scores[:, pl.ds(near + tile * 128, 128)] = part
        best = part if best is None else jnp.maximum(best, part)
    peak[...] = best
    behind, ahead = behind_ref[step], ahead_ref[step]

    def far_scores(start, bias):
        part = nt(query, keys[pl.ds(start, CHUNK), :]) + bias
        scores[:, pl.ds(start, CHUNK)] = part
        peak[...] = jnp.maximum(peak[...], jnp.maximum(part[:, :128], part[:, 128:]))

    @pl.when(behind > 0)
    def _():
        bias = jnp.concatenate([place[0][:, 31:32], place[1][:, 31:32]], 0)

        @pl.loop(0, behind)
        def _(chunk):
            far_scores(pl.multiple_of(near - 256 * (chunk + 1), 128), bias)

    @pl.when(ahead > 0)
    def _():
        bias = jnp.concatenate([place[0][:, 15:16], place[1][:, 15:16]], 0)

        @pl.loop(0, ahead)
        def _(chunk):
            far_scores(pl.multiple_of(near + NEAR + 256 * chunk, 128), bias)

    top = jnp.max(peak[...], axis=1, keepdims=True)
    probs = jnp.exp2(scores[:, pl.ds(near, NEAR)] - top).astype(bf16)
    probs_ref[0, 0, :, pl.ds(near, NEAR)] = probs
    total[...] = nn(probs, values[pl.ds(near, NEAR), :])

    def far_total(start):
        probs = jnp.exp2(scores[:, pl.ds(start, CHUNK)] - top).astype(bf16)
        probs_ref[0, 0, :, pl.ds(start, CHUNK)] = probs
        total[...] += nn(probs, values[pl.ds(start, CHUNK), :])

    @pl.loop(0, behind)
    def _(chunk):
        far_total(pl.multiple_of(near - 256 * (chunk + 1), 128))

    @pl.loop(0, ahead)
    def _(chunk):
        far_total(pl.multiple_of(near + NEAR + 256 * chunk, 128))

    inverse = 1.0 / total[:, 128:]
    mixed = pick(total[:, :128] * inverse)
    inverse_ref[...] = pick(inverse)
    mixed_ref[...] = mixed
    context_ref[...] = mixed.astype(bf16)


def backward_kernel(
    behind_ref, ahead_ref, probs_ref, grad_ref, mixed_ref, inverse_ref, content_ref, position_ref, ordering_ref,
    key_ref, value_ref, relative_ref, order_ref, turn_ref, onehot_ref,
    query_ref, key_low_ref, value_low_ref, relative_out, order_out, sums_out,
    keys, values, table, key_total, value_total, query_total, far_behind, far_ahead, bucket, table_total, sums,
):
    step = pl.program_id(1)
    length = key_ref.shape[0]

    @pl.when(step == 0)
    def _():
        for scratch, ref in ((keys, key_ref), (values, value_ref)):
            scratch[:256, :] = jnp.zeros((256, 128), bf16)
            scratch[256 + length :, :] = jnp.zeros((256, 128), bf16)
            scratch[256 : 256 + length, :] = ref[...]
        table[...] = jnp.zeros((256, 256), bf16)
        even, odd = halves(relative_ref[...])
        table[0:32, :128] = even
        table[128:160, :128] = odd
        slot = lax.broadcasted_iota(jnp.int32, (32, 128), 0)
        orders = jnp.where(slot == 0, order_ref[0:1, :].astype(f32), order_ref[1:2, :].astype(f32))
        even, odd = halves(jnp.where(slot < 2, orders, 0.0))
        table[32:64, 128:] = even.astype(bf16)
        table[160:192, 128:] = odd.astype(bf16)
        key_total[...] = jnp.zeros(key_total.shape, f32)
        value_total[...] = jnp.zeros(value_total.shape, f32)
        table_total[...] = jnp.zeros(table_total.shape, f32)
        sums[...] = jnp.zeros(sums.shape, f32)

    scaled = (grad_ref[...].astype(f32) * inverse_ref[...]).astype(bf16)
    even, odd = halves(scaled)
    grads = jnp.concatenate([even, odd], 0)
    even, odd = halves(scaled.astype(f32) * mixed_ref[...])
    delta = jnp.concatenate(
        [jnp.sum(even, axis=1, keepdims=True), jnp.sum(odd, axis=1, keepdims=True)], 0
    )
    even, odd = halves(content_ref[...])
    content = jnp.concatenate([even, odd], 0)
    grads_t = grads.T
    content_t = content.T
    near = pl.multiple_of(step * 256, 256)

    def visit(start, size):
        probs = probs_ref[0, 0, :, pl.ds(start, size)]
        prob_grad = nt(grads, values[pl.ds(start, size), :])
        score = probs.astype(f32) * (prob_grad - delta)
        score_low = score.astype(bf16)
        value_total[:, pl.ds(start, size)] += nn(grads_t, probs)
        key_total[:, pl.ds(start, size)] += nn(content_t, score_low)
        return score, nn(score_low, keys[pl.ds(start, size), :])

    score, query_part = visit(near, NEAR)
    query_total[...] = query_part
    parts = [score[:, 128 * t : 128 * t + 128] for t in range(5)]
    turn = turn_ref[...]
    turns = jnp.concatenate([turn, turn], 0)
    tiles = [take(part, turns) for part in parts]
    lane = lax.broadcasted_iota(jnp.int32, (64, 128), 1)
    row = lax.broadcasted_iota(jnp.int32, (64, 128), 0)
    first = lane + 2 * row < 128
    zero = jnp.zeros((64, 128), f32)
    for quarter in range(4):
        rows = slice(64 * quarter, 64 * quarter + 64)
        own = [tile[rows] for tile in tiles]
        if quarter % 2 == 0:
            near_parts = [jnp.where(first, own[t], own[t + 1]) for t in range(3)]
            far_behind[rows] = jnp.where(first, zero, own[0])
            far_ahead[rows] = jnp.where(first, own[3], zero) + parts[4][rows]
        else:
            near_parts = [jnp.where(first, own[t + 1], own[t + 2]) for t in range(3)]
            far_behind[rows] = parts[0][rows] + jnp.where(first, zero, own[1])
            far_ahead[rows] = jnp.where(first, own[4], zero)
        for t in range(3):
            bucket[rows, 256 + 128 * t : 384 + 128 * t] = near_parts[t].astype(bf16)

    @pl.loop(0, behind_ref[step])
    def _(chunk):
        score, part = visit(pl.multiple_of(near - 256 * (chunk + 1), 128), CHUNK)
        query_total[...] += part
        far_behind[...] += score[:, :128] + score[:, 128:]

    @pl.loop(0, ahead_ref[step])
    def _(chunk):
        score, part = visit(pl.multiple_of(near + NEAR + 256 * chunk, 128), CHUNK)
        query_total[...] += part
        far_ahead[...] += score[:, :128] + score[:, 128:]

    for ref, place in ((far_behind, 0), (far_ahead, 640)):
        whole = ref[...]
        coarse = whole.astype(bf16)
        bucket[:, place : place + 128] = coarse
        bucket[:, place + 128 : place + 256] = (whole - coarse.astype(f32)).astype(bf16)
    low = (nn(bucket[...], onehot_ref[...]) * 0.125).astype(bf16)
    low = jnp.concatenate([low[:BQ], low[BQ:]], 1)
    placed = nn(low, table[...])
    content_grad = pick(query_total[...]) * 0.125
    query_ref[...] = (content_grad + placed[:, :128] + placed[:, 128:]).astype(bf16)
    table_total[...] += tn(low, jnp.concatenate([position_ref[...], ordering_ref[...]], 1))
    sums[0:1, :] += jnp.sum(content_grad, axis=0, keepdims=True)
    sums[1:2, :] += jnp.sum(placed[:, :128], axis=0, keepdims=True)
    sums[2:3, :] += jnp.sum(placed[:, 128:], axis=0, keepdims=True)

    @pl.when(step == pl.num_programs(1) - 1)
    def _():
        key_low_ref[...] = (key_total[:, 256 : 256 + length] * LN2).T.astype(bf16)
        value_low_ref[...] = value_total[:, 256 : 256 + length].T.astype(bf16)
        low_lane = lax.broadcasted_iota(jnp.int32, (32, 128), 1) < 64
        relative_out[...] = jnp.where(low_lane, table_total[0:32, :128], table_total[128:160, :128])
        order_out[...] = jnp.where(low_lane[:8], table_total[32:40, 128:], table_total[160:168, 128:])
        sums_out[...] = sums[...]


def ranges(segments):
    length = segments.shape[1]
    own = segments[0]
    blocks = length // (2 * BQ)
    start = 2 * BQ * jnp.arange(blocks, dtype=jnp.int32)
    first = jnp.sum((own[None, :] < own[start][:, None]).astype(jnp.int32), axis=1)
    last = jnp.sum((own[None, :] <= own[start + 2 * BQ - 2][:, None]).astype(jnp.int32), axis=1)
    behind = jnp.maximum(start - 256 - first + CHUNK - 1, 0) // CHUNK
    ahead = jnp.maximum(last - (start - 256 + NEAR) + CHUNK - 1, 0) // CHUNK
    return behind, ahead


def documents(segments):
    length = segments.shape[1]
    lane = jnp.arange(128, dtype=jnp.int32)[None, :]
    same = segments[0][:, None] == lane
    query = same[0::2].astype(bf16)
    away = jnp.where((lane < 8) & ~same, -BIG, 0.0).astype(bf16)
    pad = jnp.broadcast_to(jnp.where(lane < 8, -BIG, 0.0).astype(bf16), (256, 128))
    return query, jnp.concatenate([pad, away, pad], 0)


def attend(behind, ahead, content, position, ordering, keys, values, relative, order, away, document):
    rows, width = content.shape
    length = keys.shape[0]
    padded = length + 512
    pairs, blocks = width // 128, rows // BQ
    tile = pl.BlockSpec((BQ, 128), lambda p, i, *_: (i, p))
    whole = pl.BlockSpec((length, 128), lambda p, i, *_: (0, p))
    return pl.pallas_call(
        forward_kernel,
        name="attend",
        out_shape=(
            jax.ShapeDtypeStruct((pairs, blocks, 2 * BQ, padded), bf16),
            jax.ShapeDtypeStruct((rows, width), bf16),
            jax.ShapeDtypeStruct((rows, width), f32),
            jax.ShapeDtypeStruct((rows, width), f32),
        ),
        grid_spec=pltpu.PrefetchScalarGridSpec(
            num_scalar_prefetch=2,
            grid=(pairs, blocks),
            in_specs=[
                tile, tile, tile, whole, whole,
                pl.BlockSpec((32, 128), lambda p, i, *_: (0, p)),
                pl.BlockSpec((2, 128), lambda p, i, *_: (0, p)),
                pl.BlockSpec((padded, 128), lambda p, i, *_: (0, 0)),
                pl.BlockSpec((BQ, 128), lambda p, i, *_: (i, 0)),
                pl.BlockSpec((5, BQ, 128), lambda p, i, *_: (0, 0, 0)),
            ],
            out_specs=[pl.BlockSpec((1, 1, 2 * BQ, padded), lambda p, i, *_: (p, i, 0, 0)), tile, tile, tile],
            scratch_shapes=[
                pltpu.VMEM((padded, 256), bf16),
                pltpu.VMEM((padded, 256), bf16),
                pltpu.VMEM((256, 256), bf16),
                pltpu.VMEM((2 * BQ, padded), f32),
                pltpu.VMEM((2 * BQ, 128), f32),
                pltpu.VMEM((2 * BQ, 256), f32),
            ],
        ),
        compiler_params=pltpu.CompilerParams(dimension_semantics=("arbitrary", "arbitrary"), vmem_limit_bytes=48 << 20),
        cost_estimate=pl.CostEstimate(flops=40 * 10**9, bytes_accessed=70 * 10**6, transcendentals=10**7),
    )(behind, ahead, content, position, ordering, keys, values, relative, order, away, document, jnp.asarray(near_index()))


def attend_back(behind, ahead, probs, grad, mixed, inverse, content, position, ordering, keys, values, relative, order):
    rows, width = content.shape
    length = keys.shape[0]
    padded = length + 512
    pairs, blocks = width // 128, rows // BQ
    tile = pl.BlockSpec((BQ, 128), lambda p, i, *_: (i, p))
    whole = pl.BlockSpec((length, 128), lambda p, i, *_: (0, p))
    small = lambda n: pl.BlockSpec((n, 128), lambda p, i, *_: (0, p))
    fixed = lambda n: pl.BlockSpec((n, 128), lambda p, i, *_: (0, 0))
    turn = (np.arange(128)[None, :] + 2 * np.arange(BQ)[:, None]) % 128
    return pl.pallas_call(
        backward_kernel,
        name="attend_back",
        out_shape=(
            jax.ShapeDtypeStruct((rows, width), bf16),
            jax.ShapeDtypeStruct((length, width), bf16),
            jax.ShapeDtypeStruct((length, width), bf16),
            jax.ShapeDtypeStruct((32, width), f32),
            jax.ShapeDtypeStruct((8, width), f32),
            jax.ShapeDtypeStruct((8, width), f32),
        ),
        grid_spec=pltpu.PrefetchScalarGridSpec(
            num_scalar_prefetch=2,
            grid=(pairs, blocks),
            in_specs=[
                pl.BlockSpec((1, 1, 2 * BQ, padded), lambda p, i, *_: (p, i, 0, 0)),
                tile, tile, tile, tile, tile, tile, whole, whole, small(32), small(2), fixed(BQ), fixed(896),
            ],
            out_specs=[tile, whole, whole, small(32), small(8), small(8)],
            scratch_shapes=[
                pltpu.VMEM((padded, 128), bf16),
                pltpu.VMEM((padded, 128), bf16),
                pltpu.VMEM((256, 256), bf16),
                pltpu.VMEM((128, padded), f32),
                pltpu.VMEM((128, padded), f32),
                pltpu.VMEM((2 * BQ, 128), f32),
                pltpu.VMEM((2 * BQ, 128), f32),
                pltpu.VMEM((2 * BQ, 128), f32),
                pltpu.VMEM((2 * BQ, 896), bf16),
                pltpu.VMEM((256, 256), f32),
                pltpu.VMEM((8, 128), f32),
            ],
        ),
        compiler_params=pltpu.CompilerParams(dimension_semantics=("arbitrary", "arbitrary"), vmem_limit_bytes=48 << 20),
        cost_estimate=pl.CostEstimate(flops=80 * 10**9, bytes_accessed=70 * 10**6, transcendentals=0),
    )(behind, ahead, probs, grad, mixed, inverse, content, position, ordering, keys, values, relative, order,
      jnp.asarray(turn, jnp.int32), jnp.asarray(bucket_onehot(), bf16))


def matmul(left, right):
    return jnp.dot(left, right, preferred_element_type=jnp.float32)


def normalize(values):
    centered = values - jnp.mean(values, axis=1, keepdims=True)
    inverse = lax.rsqrt(jnp.mean(centered * centered, axis=1, keepdims=True) + 1e-05)
    return (centered * inverse, inverse)


def norm_back(grad, normed, inverse):
    return inverse * (
        grad
        - jnp.mean(grad, axis=1, keepdims=True)
        - normed * jnp.mean(grad * normed, axis=1, keepdims=True)
    )


def gelu_slope(values):
    return 0.5 * (1.0 + lax.erf(values * math.sqrt(0.5))) + values * jnp.exp(
        -0.5 * values * values
    ) / math.sqrt(2.0 * math.pi)


def body(
    tokens,
    segment_ids,
    query_weight,
    key_weight,
    value_weight,
    output_weight,
    relative_table,
    order_table,
    content_bias,
    position_bias,
    order_bias,
    first_gain,
    first_shift,
    inner_weight,
    inner_bias,
    outer_weight,
    outer_bias,
    second_gain,
    second_shift,
    cotangent,
):
    full = (
        lax.all_gather(query_weight, "shard", axis=0, tiled=True),
        lax.all_gather(key_weight, "shard", axis=0, tiled=True),
        lax.all_gather(value_weight, "shard", axis=0, tiled=True),
        lax.all_gather(output_weight, "shard", axis=0, tiled=True),
        lax.all_gather(relative_table, "shard", axis=1, tiled=True),
        lax.all_gather(order_table, "shard", axis=1, tiled=True),
        lax.all_gather(content_bias, "shard", axis=0, tiled=True),
        lax.all_gather(position_bias, "shard", axis=0, tiled=True),
        lax.all_gather(order_bias, "shard", axis=0, tiled=True),
        lax.all_gather(first_gain, "shard", axis=0, tiled=True),
        lax.all_gather(first_shift, "shard", axis=0, tiled=True),
        lax.all_gather(inner_weight, "shard", axis=0, tiled=True),
        lax.all_gather(inner_bias, "shard", axis=0, tiled=True),
        lax.all_gather(outer_weight, "shard", axis=0, tiled=True),
        lax.all_gather(outer_bias, "shard", axis=0, tiled=True),
        lax.all_gather(second_gain, "shard", axis=0, tiled=True),
        lax.all_gather(second_shift, "shard", axis=0, tiled=True),
    )
    (
        weight_query,
        weight_key,
        weight_value,
        weight_output,
        weight_relative,
        weight_order,
        bias_content,
        bias_position,
        bias_order,
        gain_first,
        shift_first,
        weight_inner,
        bias_inner,
        weight_outer,
        bias_outer,
        gain_second,
        shift_second,
    ) = full
    count, length = segment_ids.shape
    half = length // 2
    width = tokens.shape[1]
    pairs = tokens.astype(f32).reshape(count, half, 2, width)
    query_seg = segment_ids[:, 0::2]
    joined = (query_seg == segment_ids[:, 1::2]).astype(f32)[:, :, None]
    pooled = ((pairs[:, :, 0] + joined * pairs[:, :, 1]) / (1.0 + joined)).reshape(
        count * half, width
    )
    pooled_low = pooled.astype(bf16)
    queries = matmul(pooled_low, weight_query)
    keys = matmul(tokens, weight_key).astype(bf16)
    values = matmul(tokens, weight_value).astype(bf16)
    content = ((queries + bias_content.astype(f32)) * (0.125 * LOG2E)).astype(bf16)
    position = (queries + bias_position.astype(f32)).astype(bf16)
    ordering = (queries + bias_order.astype(f32)).astype(bf16)
    behind, ahead = ranges(segment_ids)
    document, away = documents(segment_ids)
    probs, context, mixed, inverse = attend(
        behind, ahead, content, position, ordering, keys, values, weight_relative, weight_order, away, document
    )
    attended = matmul(context, weight_output)
    first_norm, first_inverse = normalize(pooled + attended)
    first = first_norm * gain_first.astype(f32) + shift_first.astype(f32)
    first_low = first.astype(bf16)
    inner = matmul(first_low, weight_inner) + bias_inner.astype(f32)
    act_low = jax.nn.gelu(inner, approximate=False).astype(bf16)
    outer = matmul(act_low, weight_outer) + bias_outer.astype(f32)
    second_norm, second_inverse = normalize(first + outer)
    layer_out = (second_norm * gain_second.astype(f32) + shift_second.astype(f32)).astype(bf16)
    grad_out = cotangent.astype(f32)
    second_gain_grad = jnp.sum(grad_out * second_norm, axis=0)
    second_shift_grad = jnp.sum(grad_out, axis=0)
    mid_grad = norm_back(grad_out * gain_second.astype(f32), second_norm, second_inverse)
    outer_low = mid_grad.astype(bf16)
    outer_weight_grad = matmul(act_low.T, outer_low)
    outer_bias_grad = jnp.sum(outer_low.astype(f32), axis=0)
    inner_low = (matmul(outer_low, weight_outer.T) * gelu_slope(inner)).astype(bf16)
    inner_weight_grad = matmul(first_low.T, inner_low)
    inner_bias_grad = jnp.sum(inner_low.astype(f32), axis=0)
    first_grad = matmul(inner_low, weight_inner.T) + mid_grad
    first_gain_grad = jnp.sum(first_grad * first_norm, axis=0)
    first_shift_grad = jnp.sum(first_grad, axis=0)
    sum_grad = norm_back(first_grad * gain_first.astype(f32), first_norm, first_inverse)
    attended_low = sum_grad.astype(bf16)
    output_weight_grad = matmul(context.T, attended_low)
    context_grad = matmul(attended_low, weight_output.T).astype(bf16)
    query_low, key_low, value_low, relative_table_grad, order_table_grad, bias_sums = attend_back(
        behind, ahead, probs, context_grad, mixed, inverse, content, position, ordering,
        keys, values, weight_relative, weight_order,
    )
    order_table_grad = order_table_grad[:2]
    content_bias_grad, position_bias_grad, order_bias_grad = bias_sums[0], bias_sums[1], bias_sums[2]
    query_weight_grad = matmul(pooled_low.T, query_low)
    key_weight_grad = matmul(tokens.T, key_low)
    value_weight_grad = matmul(tokens.T, value_low)
    pooled_grad = (sum_grad + matmul(query_low, weight_query.T)).reshape(count, half, 1, width)
    shared = joined[:, :, :, None]
    spread = jnp.concatenate(
        [pooled_grad / (1.0 + shared), shared * pooled_grad / (1.0 + shared)], axis=2
    ).reshape(count * length, width)
    tokens_grad = matmul(key_low, weight_key.T) + matmul(value_low, weight_value.T) + spread
    owned = (
        lax.psum_scatter(query_weight_grad, "shard", scatter_dimension=0, tiled=True),
        lax.psum_scatter(key_weight_grad, "shard", scatter_dimension=0, tiled=True),
        lax.psum_scatter(value_weight_grad, "shard", scatter_dimension=0, tiled=True),
        lax.psum_scatter(output_weight_grad, "shard", scatter_dimension=0, tiled=True),
        lax.psum_scatter(relative_table_grad, "shard", scatter_dimension=1, tiled=True),
        lax.psum_scatter(order_table_grad, "shard", scatter_dimension=1, tiled=True),
        lax.psum_scatter(content_bias_grad, "shard", scatter_dimension=0, tiled=True),
        lax.psum_scatter(position_bias_grad, "shard", scatter_dimension=0, tiled=True),
        lax.psum_scatter(order_bias_grad, "shard", scatter_dimension=0, tiled=True),
        lax.psum_scatter(first_gain_grad, "shard", scatter_dimension=0, tiled=True),
        lax.psum_scatter(first_shift_grad, "shard", scatter_dimension=0, tiled=True),
        lax.psum_scatter(inner_weight_grad, "shard", scatter_dimension=0, tiled=True),
        lax.psum_scatter(inner_bias_grad, "shard", scatter_dimension=0, tiled=True),
        lax.psum_scatter(outer_weight_grad, "shard", scatter_dimension=0, tiled=True),
        lax.psum_scatter(outer_bias_grad, "shard", scatter_dimension=0, tiled=True),
        lax.psum_scatter(second_gain_grad, "shard", scatter_dimension=0, tiled=True),
        lax.psum_scatter(second_shift_grad, "shard", scatter_dimension=0, tiled=True),
    )
    summed = lax.psum(
        (
            owned[0],
            owned[1],
            owned[2],
            owned[3],
            owned[4],
            owned[5],
            owned[6],
            owned[7],
            owned[8],
            owned[9],
            owned[10],
            owned[11],
            owned[12],
            owned[13],
            owned[14],
            owned[15],
            owned[16],
        ),
        "rep",
    )
    return (layer_out, tokens_grad) + tuple(summed)


def solution(mesh):
    placed = (
        P(("rep", "shard"), None),
        P(("rep", "shard"), None),
        P("shard", None),
        P("shard", None),
        P("shard", None),
        P("shard", None),
        P(None, "shard"),
        P(None, "shard"),
        P("shard"),
        P("shard"),
        P("shard"),
        P("shard"),
        P("shard"),
        P("shard", None),
        P("shard"),
        P("shard", None),
        P("shard"),
        P("shard"),
        P("shard"),
        P(("rep", "shard"), None),
    )
    return jax.shard_map(
        body,
        mesh=mesh,
        in_specs=placed,
        out_specs=(
            P(("rep", "shard"), None),
            P(("rep", "shard"), None),
            P("shard", None),
            P("shard", None),
            P("shard", None),
            P("shard", None),
            P(None, "shard"),
            P(None, "shard"),
            P("shard"),
            P("shard"),
            P("shard"),
            P("shard"),
            P("shard"),
            P("shard", None),
            P("shard"),
            P("shard", None),
            P("shard"),
            P("shard"),
            P("shard"),
        ),
        check_vma=False,
    )
```

```python
import functools
import math

import jax
import jax.numpy as jnp
import numpy as np
from jax import lax
from jax.experimental import pallas as pl
from jax.experimental.pallas import tpu as pltpu
from jax.sharding import PartitionSpec as P

LIMITS = (1, 2, 3, 4, 5, 6, 7, 8, 12, 16, 24, 32, 48, 64, 128)
BQ = 128
NEAR = 640
CHUNK = 256
LOG2E = math.log2(math.e)
LN2 = math.log(2.0)
BIG = 1e30
f32 = jnp.float32
bf16 = jnp.bfloat16


def bucket_of(offset):
    distance = np.abs(offset)
    passed = sum((distance >= limit).astype(np.int32) for limit in LIMITS)
    return np.where(offset < 0, 15 + passed + (distance >= 256), passed).astype(np.int32)


def near_index():
    row = np.arange(BQ)[None, :, None]
    tile = np.arange(-2, 3)[:, None, None]
    lane = np.arange(128)[None, None, :]
    return bucket_of(128 * tile + lane - 2 * row)


def bucket_onehot():
    out = np.zeros((4 * 128, 128), np.float32)
    offsets = np.concatenate([np.arange(-256, 128), np.full(64, -300), np.full(64, 300)])
    out[np.arange(512), bucket_of(offsets)] = 1
    out[:, 32] = offsets >= 0
    out[:, 33] = offsets < 0
    return out


def nt(left, right):
    return lax.dot_general(left, right, (((1,), (1,)), ((), ())), preferred_element_type=f32)


def nn(left, right):
    return lax.dot_general(left, right, (((1,), (0,)), ((), ())), preferred_element_type=f32)


def tn(left, right):
    return lax.dot_general(left, right, (((0,), (0,)), ((), ())), preferred_element_type=f32)


def halves(array):
    low = lax.broadcasted_iota(jnp.int32, array.shape, 1) < 64
    zero = jnp.zeros_like(array)
    return jnp.where(low, array, zero), jnp.where(low, zero, array)


def pick(array):
    half = array.shape[0] // 2
    low = lax.broadcasted_iota(jnp.int32, (half, 128), 1) < 64
    return jnp.where(low, array[:half], array[half:])


def take(table, index):
    return jnp.take_along_axis(table, index, axis=1, mode="promise_in_bounds")


def lanes_of(p):
    return slice(128 * p, 128 * p + 128)


def forward_kernel(
    group, behind_ref, ahead_ref, content_ref, position_ref, ordering_ref, key_ref, value_ref,
    relative_ref, order_ref, away_ref, document_ref, index_ref,
    probs_ref, context_ref, mixed_ref, inverse_ref,
    keys, values, table, bias, scores, peak, total,
):
    step = pl.program_id(1)
    length = key_ref.shape[0]

    @pl.when((step == 0) & (pl.program_id(0) == 0))
    def _():
        for p in range(group):
            for scratch in (keys, values):
                scratch[p, :256, :128] = jnp.zeros((256, 128), bf16)
                scratch[p, 256 + length :, :128] = jnp.zeros((256, 128), bf16)
            keys[p, :, 128:] = away_ref[...]
            values[p, :, 128:] = jnp.ones((length + 512, 128), bf16)

    @pl.when(step == 0)
    def _():
        after = lax.broadcasted_iota(jnp.int32, (32, 128), 0) < 16
        table[...] = jnp.zeros(table.shape, bf16)
        for p in range(group):
            lanes = lanes_of(p)
            keys[p, 256 : 256 + length, :128] = key_ref[:, lanes]
            values[p, 256 : 256 + length, :128] = value_ref[:, lanes]
            orders = jnp.where(after, order_ref[0:1, lanes].astype(f32), order_ref[1:2, lanes].astype(f32)).astype(bf16)
            for half, (relative, order) in enumerate(zip(halves(relative_ref[:, lanes]), halves(orders))):
                both = jnp.concatenate([relative, order], 1)
                table[p, 128 * half : 128 * half + 32, :] = both

    document = document_ref[...]
    near = pl.multiple_of(step * 256, 256)
    queries = []
    for p in range(group):
        even, odd = halves(content_ref[:, lanes_of(p)])
        queries.append(jnp.concatenate(
            [jnp.concatenate([even, document], 1), jnp.concatenate([odd, document], 1)], 0
        ))
    for p in range(group):
        lanes = lanes_of(p)
        places = nt(jnp.concatenate([position_ref[:, lanes], ordering_ref[:, lanes]], 1), table[p]) * (0.125 * LOG2E)
        place = (places[:, :128], places[:, 128:])
        near_scores = nt(queries[p], keys[p, pl.ds(near, NEAR), :])
        for half in range(2):
            rows = slice(BQ * half, BQ * half + BQ)
            for side, bucket in ((0, 31), (1, 15)):
                bias[p, rows, 128 * side : 128 * side + 128] = jnp.broadcast_to(place[half][:, bucket : bucket + 1], (BQ, 128))
            for quarter in range(2):
                own = slice(64 * quarter, 64 * quarter + 64)
                rows = slice(BQ * half + 64 * quarter, BQ * half + 64 * quarter + 64)
                best = None
                for tile in range(NEAR // 128):
                    if tile == 4 - 4 * quarter:
                        extra = bias[p, rows, 128 - 128 * quarter : 256 - 128 * quarter]
                    else:
                        extra = take(place[half][own], index_ref[tile, own])
                    part = near_scores[rows, 128 * tile : 128 * tile + 128] + extra
                    scores[p, rows, pl.ds(near + 128 * tile, 128)] = part
                    best = part if best is None else jnp.maximum(best, part)
                peak[p, rows, :] = best
    behind = behind_ref[step]
    far = behind + ahead_ref[step]

    def start_of(chunk):
        return pl.multiple_of(jnp.where(chunk < behind, near - 256 * (chunk + 1), near + NEAR + 256 * (chunk - behind)), 128)

    @pl.loop(0, far)
    def _(chunk):
        start = start_of(chunk)
        place = pl.multiple_of(jnp.where(chunk < behind, 0, 128), 128)
        for p in range(group):
            part = nt(queries[p], keys[p, pl.ds(start, CHUNK), :])
            extra = bias[p, :, pl.ds(place, 128)]
            left, right = part[:, :128] + extra, part[:, 128:] + extra
            scores[p, :, pl.ds(start, 128)] = left
            scores[p, :, pl.ds(start + 128, 128)] = right
            peak[p] = jnp.maximum(peak[p], jnp.maximum(left, right))

    tops = [jnp.max(peak[p], axis=1, keepdims=True) for p in range(group)]
    for p in range(group):
        peak[p] = jnp.broadcast_to(tops[p], (2 * BQ, 128))
        probs = jnp.exp2(scores[p, :, pl.ds(near, NEAR)] - tops[p]).astype(bf16)
        probs_ref[p, 0, :, pl.ds(near, NEAR)] = probs
        total[p] = nn(probs, values[p, pl.ds(near, NEAR), :])

    @pl.loop(0, far)
    def _(chunk):
        start = start_of(chunk)
        for p in range(group):
            top = peak[p]
            left = jnp.exp2(scores[p, :, pl.ds(start, 128)] - top).astype(bf16)
            right = jnp.exp2(scores[p, :, pl.ds(start + 128, 128)] - top).astype(bf16)
            probs = jnp.concatenate([left, right], 1)
            probs_ref[p, 0, :, pl.ds(start, CHUNK)] = probs
            total[p] += nn(probs, values[p, pl.ds(start, CHUNK), :])

    for p in range(group):
        lanes = lanes_of(p)
        inverse = 1.0 / total[p, :, 128:]
        mixed = pick(total[p, :, :128] * inverse)
        inverse_ref[:, lanes] = pick(inverse)
        mixed_ref[:, lanes] = mixed
        context_ref[:, lanes] = mixed.astype(bf16)


def backward_kernel(
    group, behind_ref, ahead_ref, probs_ref, grad_ref, mixed_ref, inverse_ref, content_ref, position_ref, ordering_ref,
    key_ref, value_ref, relative_ref, order_ref, turn_ref, onehot_ref,
    query_ref, key_low_ref, value_low_ref, relative_out, order_out, sums_out,
    keys, values, table, key_total, value_total, query_total, far_total, bucket, table_total, sums,
):
    step = pl.program_id(1)
    length = key_ref.shape[0]

    @pl.when(step == 0)
    def _():
        slot = lax.broadcasted_iota(jnp.int32, (32, 128), 0)
        table[...] = jnp.zeros(table.shape, bf16)
        for p in range(group):
            lanes = lanes_of(p)
            for scratch, ref in ((keys, key_ref), (values, value_ref)):
                scratch[p, :256, :] = jnp.zeros((256, 128), bf16)
                scratch[p, 256 + length :, :] = jnp.zeros((256, 128), bf16)
                scratch[p, 256 : 256 + length, :] = ref[:, lanes]
            even, odd = halves(relative_ref[:, lanes])
            table[p, 0:32, :128] = even
            table[p, 128:160, :128] = odd
            orders = jnp.where(slot == 0, order_ref[0:1, lanes].astype(f32), order_ref[1:2, lanes].astype(f32))
            even, odd = halves(jnp.where(slot < 2, orders, 0.0))
            table[p, 32:64, 128:] = even.astype(bf16)
            table[p, 160:192, 128:] = odd.astype(bf16)
        key_total[...] = jnp.zeros(key_total.shape, f32)
        value_total[...] = jnp.zeros(value_total.shape, f32)
        table_total[...] = jnp.zeros(table_total.shape, f32)
        sums[...] = jnp.zeros(sums.shape, f32)

    near = pl.multiple_of(step * 256, 256)
    grads, grads_t, content_t, deltas = [], [], [], []
    for p in range(group):
        lanes = lanes_of(p)
        scaled = (grad_ref[:, lanes].astype(f32) * inverse_ref[:, lanes]).astype(bf16)
        both = jnp.concatenate(halves(scaled), 0)
        even, odd = halves(scaled.astype(f32) * mixed_ref[:, lanes])
        deltas.append(jnp.concatenate(
            [jnp.sum(even, axis=1, keepdims=True), jnp.sum(odd, axis=1, keepdims=True)], 0
        ))
        grads.append(both)
        grads_t.append(both.T)
        content_t.append(jnp.concatenate(halves(content_ref[:, lanes]), 0).T)

    def visit(p, start, size):
        probs = probs_ref[p, 0, :, pl.ds(start, size)]
        prob_grad = nt(grads[p], values[p, pl.ds(start, size), :])
        score = probs.astype(f32) * (prob_grad - deltas[p])
        score_low = score.astype(bf16)
        value_total[p, :, pl.ds(start, size)] += nn(grads_t[p], probs)
        key_total[p, :, pl.ds(start, size)] += nn(content_t[p], score_low)
        return score, nn(score_low, keys[p, pl.ds(start, size), :])

    turn = turn_ref[...]
    turns = jnp.concatenate([turn, turn], 0)
    lane = lax.broadcasted_iota(jnp.int32, (64, 128), 1)
    row = lax.broadcasted_iota(jnp.int32, (64, 128), 0)
    first = lane + 2 * row < 128
    zero = jnp.zeros((64, 128), f32)
    for p in range(group):
        score, query_total[p] = visit(p, near, NEAR)
        parts = [score[:, 128 * t : 128 * t + 128] for t in range(5)]
        tiles = [take(part, turns) for part in parts]
        for quarter in range(4):
            rows = slice(64 * quarter, 64 * quarter + 64)
            own = [tile[rows] for tile in tiles]
            if quarter % 2 == 0:
                near_parts = [jnp.where(first, own[t], own[t + 1]) for t in range(3)]
                far_total[p, 0, rows] = jnp.where(first, zero, own[0])
                far_total[p, 1, rows] = jnp.where(first, own[3], zero) + parts[4][rows]
            else:
                near_parts = [jnp.where(first, own[t + 1], own[t + 2]) for t in range(3)]
                far_total[p, 0, rows] = parts[0][rows] + jnp.where(first, zero, own[1])
                far_total[p, 1, rows] = jnp.where(first, own[4], zero)
            for t in range(3):
                bucket[p, rows, 128 * t : 128 * t + 128] = near_parts[t].astype(bf16)
    behind = behind_ref[step]

    @pl.loop(0, behind + ahead_ref[step])
    def _(chunk):
        start = pl.multiple_of(jnp.where(chunk < behind, near - 256 * (chunk + 1), near + NEAR + 256 * (chunk - behind)), 128)
        side = jnp.where(chunk < behind, 0, 1)
        for p in range(group):
            score, part = visit(p, start, CHUNK)
            query_total[p] += part
            far_total[p, side] += score[:, :128] + score[:, 128:]

    for p in range(group):
        lanes = lanes_of(p)
        folded = [far_total[p, side] + pltpu.roll(far_total[p, side], 64, 1) for side in range(2)]
        low_lane = lax.broadcasted_iota(jnp.int32, folded[0].shape, 1) < 64
        bucket[p, :, 384:] = jnp.where(low_lane, *folded).astype(bf16)
        low = (nn(bucket[p], onehot_ref[...]) * 0.125).astype(bf16)
        low = jnp.concatenate([low[:BQ], low[BQ:]], 1)
        placed = nn(low, table[p])
        content_grad = pick(query_total[p]) * 0.125
        query_ref[:, lanes] = (content_grad + placed[:, :128] + placed[:, 128:]).astype(bf16)
        table_total[p] += tn(low, jnp.concatenate([position_ref[:, lanes], ordering_ref[:, lanes]], 1))
        for j, term in enumerate((content_grad, placed[:, :128], placed[:, 128:])):
            sums[j : j + 1, lanes] += jnp.sum(term, axis=0, keepdims=True)

    @pl.when(step == pl.num_programs(1) - 1)
    def _():
        low_lane = lax.broadcasted_iota(jnp.int32, (32, 128), 1) < 64
        for p in range(group):
            lanes = lanes_of(p)
            key_low_ref[:, lanes] = (key_total[p, :, 256 : 256 + length] * LN2).T.astype(bf16)
            value_low_ref[:, lanes] = value_total[p, :, 256 : 256 + length].T.astype(bf16)
            relative_out[:, lanes] = jnp.where(low_lane, table_total[p, 0:32, :128], table_total[p, 128:160, :128])
            order_out[:, lanes] = jnp.where(low_lane[:8], table_total[p, 32:40, 128:], table_total[p, 160:168, 128:])
        sums_out[...] = sums[...]


def fixed(*shape):
    return pl.BlockSpec(shape, lambda *_: (0,) * len(shape), pipeline_mode=pl.Buffered(1))


def ranges(segments):
    length = segments.shape[1]
    own = segments[0]
    blocks = length // (2 * BQ)
    start = 2 * BQ * jnp.arange(blocks, dtype=jnp.int32)
    first = jnp.sum((own[None, :] < own[start][:, None]).astype(jnp.int32), axis=1)
    last = jnp.sum((own[None, :] <= own[start + 2 * BQ - 2][:, None]).astype(jnp.int32), axis=1)
    behind = jnp.maximum(start - 256 - first + CHUNK - 1, 0) // CHUNK
    ahead = jnp.maximum(last - (start - 256 + NEAR) + CHUNK - 1, 0) // CHUNK
    return behind, ahead


def documents(segments):
    length = segments.shape[1]
    lane = jnp.arange(128, dtype=jnp.int32)[None, :]
    same = segments[0][:, None] == lane
    query = same[0::2].astype(bf16)
    away = jnp.where((lane < 8) & ~same, -BIG, 0.0).astype(bf16)
    pad = jnp.broadcast_to(jnp.where(lane < 8, -BIG, 0.0).astype(bf16), (256, 128))
    return query, jnp.concatenate([pad, away, pad], 0)


GROUP = 3


def attend(behind, ahead, content, position, ordering, keys, values, relative, order, away, document):
    rows, width = content.shape
    length = keys.shape[0]
    padded = length + 512
    pairs, blocks, group = width // 128, rows // BQ, GROUP
    wide = 128 * group
    tile = pl.BlockSpec((BQ, wide), lambda p, i, *_: (i, p))
    whole = pl.BlockSpec((length, wide), lambda p, i, *_: (0, p), pipeline_mode=pl.Buffered(1))
    return pl.pallas_call(
        functools.partial(forward_kernel, group),
        name="attend",
        out_shape=(
            jax.ShapeDtypeStruct((pairs, blocks, 2 * BQ, padded), bf16),
            jax.ShapeDtypeStruct((rows, width), bf16),
            jax.ShapeDtypeStruct((rows, width), f32),
            jax.ShapeDtypeStruct((rows, width), f32),
        ),
        grid_spec=pltpu.PrefetchScalarGridSpec(
            num_scalar_prefetch=2,
            grid=(pairs // group, blocks),
            in_specs=[
                tile, tile, tile, whole, whole,
                pl.BlockSpec((32, wide), lambda p, i, *_: (0, p)),
                pl.BlockSpec((2, wide), lambda p, i, *_: (0, p)),
                fixed(padded, 128),
                pl.BlockSpec((BQ, 128), lambda p, i, *_: (i, 0)),
                fixed(5, BQ, 128),
            ],
            out_specs=[pl.BlockSpec((group, 1, 2 * BQ, padded), lambda p, i, *_: (p, i, 0, 0)), tile, tile, tile],
            scratch_shapes=[
                pltpu.VMEM((group, padded, 256), bf16),
                pltpu.VMEM((group, padded, 256), bf16),
                pltpu.VMEM((group, 256, 256), bf16),
                pltpu.VMEM((group, 2 * BQ, 256), f32),
                pltpu.VMEM((group, 2 * BQ, padded), f32),
                pltpu.VMEM((group, 2 * BQ, 128), f32),
                pltpu.VMEM((group, 2 * BQ, 256), f32),
            ],
        ),
        compiler_params=pltpu.CompilerParams(dimension_semantics=("arbitrary", "arbitrary"), vmem_limit_bytes=48 << 20),
        cost_estimate=pl.CostEstimate(flops=40 * 10**9, bytes_accessed=70 * 10**6, transcendentals=10**7),
    )(behind, ahead, content, position, ordering, keys, values, relative, order, away, document,
      jnp.asarray(near_index()))


def attend_back(behind, ahead, probs, grad, mixed, inverse, content, position, ordering, keys, values, relative, order):
    rows, width = content.shape
    length = keys.shape[0]
    padded = length + 512
    pairs, blocks, group = width // 128, rows // BQ, GROUP
    wide = 128 * group
    tile = pl.BlockSpec((BQ, wide), lambda p, i, *_: (i, p))
    whole = pl.BlockSpec((length, wide), lambda p, i, *_: (0, p), pipeline_mode=pl.Buffered(1))
    small = lambda n: pl.BlockSpec((n, wide), lambda p, i, *_: (0, p))
    turn = (np.arange(128)[None, :] + 2 * np.arange(BQ)[:, None]) % 128
    return pl.pallas_call(
        functools.partial(backward_kernel, group),
        name="attend_back",
        out_shape=(
            jax.ShapeDtypeStruct((rows, width), bf16),
            jax.ShapeDtypeStruct((length, width), bf16),
            jax.ShapeDtypeStruct((length, width), bf16),
            jax.ShapeDtypeStruct((32, width), f32),
            jax.ShapeDtypeStruct((8, width), f32),
            jax.ShapeDtypeStruct((8, width), f32),
        ),
        grid_spec=pltpu.PrefetchScalarGridSpec(
            num_scalar_prefetch=2,
            grid=(pairs // group, blocks),
            in_specs=[
                pl.BlockSpec((group, 1, 2 * BQ, padded), lambda p, i, *_: (p, i, 0, 0)),
                tile, tile, tile, tile, tile, tile, whole, whole, small(32), small(2), fixed(BQ, 128), fixed(512, 128),
            ],
            out_specs=[tile, whole, whole, small(32), small(8), small(8)],
            scratch_shapes=[
                pltpu.VMEM((group, padded, 128), bf16),
                pltpu.VMEM((group, padded, 128), bf16),
                pltpu.VMEM((group, 256, 256), bf16),
                pltpu.VMEM((group, 128, padded), f32),
                pltpu.VMEM((group, 128, padded), f32),
                pltpu.VMEM((group, 2 * BQ, 128), f32),
                pltpu.VMEM((group, 2, 2 * BQ, 128), f32),
                pltpu.VMEM((group, 2 * BQ, 512), bf16),
                pltpu.VMEM((group, 256, 256), f32),
                pltpu.VMEM((8, wide), f32),
            ],
        ),
        compiler_params=pltpu.CompilerParams(dimension_semantics=("arbitrary", "arbitrary"), vmem_limit_bytes=48 << 20),
        cost_estimate=pl.CostEstimate(flops=80 * 10**9, bytes_accessed=70 * 10**6, transcendentals=0),
    )(behind, ahead, probs, grad, mixed, inverse, content, position, ordering, keys, values, relative, order,
      jnp.asarray(turn, jnp.int32), jnp.asarray(bucket_onehot(), bf16))


MESH = pl.DeviceIdType.MESH


class Place:
    def __init__(self, replicas, shards):
        self.replicas, self.shards = replicas, shards
        self.cores = 2 if shards % 2 == 0 else 1
        chips = shards // self.cores
        self.across = 2 if chips % 2 == 0 else 1
        self.line = chips // self.across
        self.replica = lax.axis_index("rep")
        own = lax.axis_index("shard")
        self.own = own
        self.core = lax.rem(own, self.cores)
        self.column = lax.rem(own // self.cores, self.across)
        self.spot = own // (self.cores * self.across)

    def shard(self, spot, column, core):
        return (spot * self.across + column) * self.cores + core

    def other_column(self, step):
        return lax.rem(self.column + step, self.across)

    def other_replica(self, step):
        return lax.rem(self.replica + step, self.replicas)

    def device(self, spot=None, column=None, core=None, replica=None):
        spot = self.spot if spot is None else spot
        column = self.column if column is None else column
        core = self.core if core is None else core
        replica = self.replica if replica is None else replica
        return (replica, self.shard(spot, column, core))

    def meet(self):
        barrier = pltpu.get_barrier_semaphore()

        def greet(device):
            pl.semaphore_signal(barrier, inc=1, device_id=device, device_id_type=MESH)

        fixed = 0
        if self.cores > 1:
            greet(self.device(core=1 - self.core))
            fixed += 1
        for step in range(1, self.across):
            greet(self.device(column=self.other_column(step)))
            fixed += 1
        for step in range(1, self.replicas):
            greet(self.device(replica=self.other_replica(step)))
            fixed += 1
        for step, there in ((1, self.spot < self.line - 1), (-1, self.spot > 0)):

            @pl.when(there)
            def _():
                greet(self.device(spot=self.spot + step))

        lined = (self.spot < self.line - 1).astype(jnp.int32) + (self.spot > 0).astype(jnp.int32)
        pl.semaphore_wait(barrier, fixed + lined)


def parts_of(columns, replicas):
    return replicas if columns % (128 * replicas) == 0 else 1


def columns_of(part, parts, columns):
    size = columns // parts
    return pl.ds(pl.multiple_of(part * size, 128), size)


def when(condition, action):
    if condition is True:
        action()
    else:
        pl.when(condition)(action)


def gather_kernel(replicas, shards, count, *refs):
    here = Place(replicas, shards)
    sources, wholes = refs[:count], refs[count : 2 * count]
    line_send, line_recv, cross_send, cross_recv, rep_send, rep_recv, core_send, core_recv = refs[2 * count :]
    here.meet()
    pending = []

    def send(source, whole_view, send_sem, recv_sem, device, condition=True):
        copy = pltpu.make_async_remote_copy(
            src_ref=source, dst_ref=whole_view, send_sem=send_sem, recv_sem=recv_sem, device_id=device, device_id_type=MESH
        )
        when(condition, copy.start)
        pending.append((condition, copy.wait_send))

    def arrived(view, recv_sem, condition=True):
        copy = pltpu.make_async_remote_copy(
            src_ref=view, dst_ref=view, send_sem=recv_sem, recv_sem=recv_sem, device_id=here.device(), device_id_type=MESH
        )
        when(condition, copy.wait_recv)

    def view(k, spot, column, core, part=None):
        whole = wholes[k].at[here.shard(spot, column, core)]
        if part is None:
            return whole
        columns = whole.shape[1]
        return whole.at[:, columns_of(part, parts_of(columns, replicas), columns)]

    def spread(k, spot, condition, own=False):
        columns = wholes[k].shape[2]
        parts = parts_of(columns, replicas)
        part = here.replica if parts > 1 else 0
        target = view(k, spot, here.column, here.core)
        source = sources[k] if own else target
        for step in range(1, here.across):
            cut = columns_of(part, parts, columns)
            send(source.at[:, cut], target.at[:, cut], cross_send.at[k, step, spot], cross_recv.at[k, here.column, spot],
                 here.device(column=here.other_column(step)), condition)
        if here.cores > 1:
            send(source, target, core_send.at[k, 0, here.column, spot], core_recv.at[k, 0, here.column, spot],
                 here.device(core=1 - here.core), condition)

    def crossed(k, spot, condition):
        columns = wholes[k].shape[2]
        parts = parts_of(columns, replicas)
        part = here.replica if parts > 1 else 0
        for step in range(1, here.across):
            column = here.other_column(step)
            piece = view(k, spot, column, here.core, part)
            arrived(piece, cross_recv.at[k, column, spot], condition)
            if parts > 1:
                for hop in range(1, replicas):
                    send(piece, piece, rep_send.at[k, hop, column, spot], rep_recv.at[k, here.replica, column, spot],
                         here.device(replica=here.other_replica(hop)), condition)
            if here.cores > 1:
                send(piece, piece, core_send.at[k, 1, column, spot], core_recv.at[k, 1, column, spot],
                     here.device(core=1 - here.core), condition)

    def replicated(k, spot, condition):
        parts = parts_of(wholes[k].shape[2], replicas)
        if parts == 1:
            return
        for step in range(1, here.across):
            column = here.other_column(step)
            for hop in range(1, replicas):
                replica = here.other_replica(hop)
                piece = view(k, spot, column, here.core, replica)
                arrived(piece, rep_recv.at[k, replica, column, spot], condition)
                if here.cores > 1:
                    send(piece, piece, core_send.at[k, 1 + hop, column, spot], core_recv.at[k, 1 + hop, column, spot],
                         here.device(core=1 - here.core), condition)

    def at(distance, action):
        for k in range(count):
            if distance == 0:
                action(k, here.spot, True)
            else:
                action(k, here.spot - distance, here.spot >= distance)
                action(k, here.spot + distance, here.spot + distance < here.line)

    for k in range(count):
        own = view(k, here.spot, here.column, here.core)
        send(sources[k], own, line_send.at[k, 0, here.spot], line_recv.at[k, here.spot],
             here.device(spot=here.spot + 1), here.spot < here.line - 1)
        send(sources[k], own, line_send.at[k, 1, here.spot], line_recv.at[k, here.spot],
             here.device(spot=here.spot - 1), here.spot > 0)
        spread(k, here.spot, True, own=True)
    for k in range(count):
        wholes[k][here.own] = sources[k][...]

    def along(distance):
        for k in range(count):
            for sign in (-1, 1):
                spot = here.spot + sign * distance
                condition = (spot >= 0) & (spot < here.line)
                piece = view(k, spot, here.column, here.core)
                arrived(piece, line_recv.at[k, spot], condition)
                onward = here.spot - sign
                send(piece, piece, line_send.at[k, 0 if sign < 0 else 1, spot], line_recv.at[k, spot],
                     here.device(spot=onward), condition & (onward >= 0) & (onward < here.line))
                spread(k, spot, condition)

    for distance in range(here.line + 2):
        if 1 <= distance < here.line:
            along(distance)
        if 1 <= distance <= here.line:
            at(distance - 1, crossed)
        if 2 <= distance:
            at(distance - 2, replicated)
    if here.cores > 1:
        for k in range(count):
            columns = wholes[k].shape[2]
            parts = parts_of(columns, replicas)
            for spot in range(here.line):
                other = 1 - here.core
                arrived(view(k, spot, here.column, other), core_recv.at[k, 0, here.column, spot])
                for step in range(1, here.across):
                    column = here.other_column(step)
                    part = here.replica if parts > 1 else 0
                    arrived(view(k, spot, column, other, part), core_recv.at[k, 1, column, spot])
                    for hop in range(1, replicas if parts > 1 else 1):
                        arrived(view(k, spot, column, other, here.other_replica(hop)), core_recv.at[k, 1 + hop, column, spot])
    for condition, wait in pending:
        when(condition, wait)


def gather(mesh, arrays, collective_id):
    replicas, shards = mesh.shape["rep"], mesh.shape["shard"]
    count = len(arrays)
    line = shards // 4
    dma = pltpu.SemaphoreType.DMA
    vmem = pl.BlockSpec(memory_space=pltpu.VMEM)
    moved = sum(a.size * 2 * shards for a in arrays)
    return pl.pallas_call(
        functools.partial(gather_kernel, replicas, shards, count),
        name="gather",
        out_shape=[jax.ShapeDtypeStruct((shards,) + a.shape, a.dtype) for a in arrays],
        in_specs=[vmem] * count,
        out_specs=[vmem] * count,
        scratch_shapes=[
            dma((count, 2, line)), dma((count, line)),
            dma((count, 2, line)), dma((count, 2, line)),
            dma((count, replicas, 2, line)), dma((count, replicas, 2, line)),
            dma((count, replicas + 1, 2, line)), dma((count, replicas + 1, 2, line)),
        ],
        compiler_params=pltpu.CompilerParams(collective_id=collective_id, has_side_effects=True, vmem_limit_bytes=56 << 20),
        cost_estimate=pl.CostEstimate(flops=0, bytes_accessed=moved * 4, transcendentals=0),
    )(*arrays)


def scatter_kernel(replicas, shards, count, chunks, extra, *refs):
    here = Place(replicas, shards)
    take = lambda number: [refs_left.pop(0) for _ in range(number)]
    refs_left = list(refs)
    sources, extras, outs, extra_outs = take(count), take(extra), take(count), take(extra)
    core_bufs, rep_bufs, cross_bufs, line_bufs, last_bufs = (take(count) for _ in range(5))
    extra_bufs = take(extra)
    (core_send, core_recv, rep_send, rep_recv, cross_send, cross_recv, line_send, line_recv, last_send, last_recv) = refs_left
    here.meet()
    pending = []

    def send(source, target, send_sem, recv_sem, device, condition=True):
        copy = pltpu.make_async_remote_copy(
            src_ref=source, dst_ref=target, send_sem=send_sem, recv_sem=recv_sem, device_id=device, device_id_type=MESH
        )
        when(condition, copy.start)
        pending.append((condition, copy.wait_send))

    def arrived(view, recv_sem, condition=True):
        copy = pltpu.make_async_remote_copy(
            src_ref=view, dst_ref=view, send_sem=recv_sem, recv_sem=recv_sem, device_id=here.device(), device_id_type=MESH
        )
        when(condition, copy.wait_recv)

    def add(target, source):
        target[...] = target[...] + source[...]

    steps = range(1, here.across)
    hops = range(1, replicas)

    def split(j):
        return parts_of(chunks[j][2], replicas)

    def columns(j, part=None):
        _, low, size = chunks[j]
        if part is None or split(j) == 1:
            return pl.ds(low, size)
        size = size // replicas
        return pl.ds(pl.multiple_of(low + part * size, 128), size)

    def compact(j):
        _, low, size = chunks[j]
        return pl.ds(low // split(j), size // split(j))

    def mixed(j, column):
        k = chunks[j][0]
        mine = core_bufs[k].at[column, :, :, columns(j)]
        own = sources[k].at[:, column, here.core, :, columns(j)]
        if here.cores > 1:
            arrived(mine, core_recv.at[j, column])
            add(mine, own)
        else:
            mine[...] = own[...]

    def stage_rep(j):
        k = chunks[j][0]
        for step in steps:
            column = here.other_column(step)
            mixed(j, column)
            if split(j) > 1:
                for hop in hops:
                    replica = here.other_replica(hop)
                    send(core_bufs[k].at[column, :, :, columns(j, replica)], rep_bufs[k].at[hop - 1, step - 1, :, :, compact(j)],
                         rep_send.at[j, hop, step], rep_recv.at[j, hop, step], here.device(replica=replica))

    def stage_cross(j):
        k = chunks[j][0]
        for step in steps:
            column = here.other_column(step)
            mine = core_bufs[k].at[column, :, :, columns(j, here.replica)]
            if split(j) > 1:
                for hop in hops:
                    piece = rep_bufs[k].at[hop - 1, step - 1, :, :, compact(j)]
                    arrived(piece, rep_recv.at[j, hop, step])
                    add(mine, piece)
            send(mine, cross_bufs[k].at[step - 1, :, :, compact(j)], cross_send.at[j, step], cross_recv.at[j, step],
                 here.device(column=column))
        mixed(j, here.column)

    def stage_line(distance, j):
        k = chunks[j][0]
        if distance == here.line - 1:
            for step in steps:
                piece = cross_bufs[k].at[step - 1, :, :, compact(j)]
                arrived(piece, cross_recv.at[j, step])
                add(core_bufs[k].at[here.column, :, :, columns(j, here.replica)], piece)
        for sign, way in ((1, 0), (-1, 1)):
            target = here.spot + sign * distance
            inside = (target >= 0) & (target < here.line)
            before = here.spot - sign
            fed = inside & (before >= 0) & (before < here.line)
            mine = core_bufs[k].at[here.column, target, :, columns(j)]
            piece = line_bufs[k].at[way, target, :, columns(j)]
            arrived(piece, line_recv.at[j, way, target], fed)
            when(fed, functools.partial(add, mine, piece))
            send(mine, piece, line_send.at[j, way, target], line_recv.at[j, way, target],
                 here.device(spot=here.spot + sign), inside)

    def stage_last(j):
        k = chunks[j][0]
        mine = core_bufs[k].at[here.column, here.spot, :, columns(j)]
        for sign, way in ((1, 0), (-1, 1)):
            before = here.spot - sign
            fed = (before >= 0) & (before < here.line)
            piece = line_bufs[k].at[way, here.spot, :, columns(j)]
            arrived(piece, line_recv.at[j, way, here.spot], fed)
            when(fed, functools.partial(add, mine, piece))
        for hop in hops:
            send(mine, last_bufs[k].at[here.replica, :, columns(j)], last_send.at[j, hop], last_recv.at[j, here.replica],
                 here.device(replica=here.other_replica(hop)))

    def finish(own, buffer, out, semaphore, cut):
        for hop in hops:
            replica = here.other_replica(hop)
            arrived(buffer.at[replica, :, cut], semaphore.at[replica])
        result = None
        for replica in range(replicas):
            term = jnp.where(here.replica == replica, own[...].astype(f32), buffer[replica, :, cut].astype(f32))
            result = term if result is None else result + term
        out[:, cut] = result

    def stage_finish(j):
        k = chunks[j][0]
        finish(core_bufs[k].at[here.column, here.spot, :, columns(j)], last_bufs[k], outs[k], last_recv.at[j], columns(j))

    if here.cores > 1:
        for j, (k, _, _) in enumerate(chunks):
            for step in (*steps, 0):
                column = here.other_column(step)
                send(sources[k].at[:, column, 1 - here.core, :, columns(j)], core_bufs[k].at[column, :, :, columns(j)],
                     core_send.at[j, column], core_recv.at[j, column], here.device(core=1 - here.core))
    stages = [stage_rep, stage_cross]
    stages += [functools.partial(stage_line, distance) for distance in range(here.line - 1, 0, -1)]
    stages += [stage_last, stage_finish]
    total = len(chunks)
    for time in range(total + len(stages) - 1):
        for place in reversed(range(len(stages))):
            if 0 <= time - place < total:
                stages[place](time - place)
        if time == 0:
            for e in range(extra):
                for hop in hops:
                    send(extras[e], extra_bufs[e].at[here.replica], last_send.at[total + e, hop],
                         last_recv.at[total + e, here.replica], here.device(replica=here.other_replica(hop)))
    for e in range(extra):
        finish(extras[e], extra_bufs[e], extra_outs[e], last_recv.at[total + e], pl.ds(0, extras[e].shape[1]))
    for condition, wait in pending:
        when(condition, wait)


def scatter(mesh, arrays, widths, extras, collective_id):
    replicas, shards = mesh.shape["rep"], mesh.shape["shard"]
    count, extra = len(arrays), len(extras)
    dma = pltpu.SemaphoreType.DMA
    vmem = pl.BlockSpec(memory_space=pltpu.VMEM)
    cores = across = 2
    line = shards // (cores * across)
    shapes = [a.shape[1:] for a in arrays]
    chunks = [
        (k, low, min(width, shapes[k][1])) for k, width in enumerate(widths) for low in range(0, shapes[k][1], min(width, shapes[k][1]))
    ]
    cuts = [(shapes[k][0], shapes[k][1] // parts_of(min(width, shapes[k][1]), replicas)) for k, width in enumerate(widths)]
    moved = sum(a.size * 2 for a in arrays)
    number = len(chunks)
    buffers = (
        [pltpu.VMEM((across, line) + s, bf16) for s in shapes]
        + [pltpu.VMEM((replicas - 1, across - 1, line) + s, bf16) for s in cuts]
        + [pltpu.VMEM((across - 1, line) + s, bf16) for s in cuts]
        + [pltpu.VMEM((2, line) + s, bf16) for s in shapes]
        + [pltpu.VMEM((replicas,) + s, bf16) for s in shapes]
        + [pltpu.VMEM((replicas,) + e.shape, bf16) for e in extras]
    )
    return pl.pallas_call(
        functools.partial(scatter_kernel, replicas, shards, count, chunks, extra),
        name="scatter",
        out_shape=[jax.ShapeDtypeStruct(s, f32) for s in shapes] + [jax.ShapeDtypeStruct(e.shape, f32) for e in extras],
        in_specs=[vmem] * (count + extra),
        out_specs=[vmem] * (count + extra),
        scratch_shapes=buffers + [
            dma((number, across)), dma((number, across)),
            dma((number, replicas, across)), dma((number, replicas, across)),
            dma((number, across)), dma((number, across)),
            dma((number, 2, line)), dma((number, 2, line)),
            dma((number + extra, replicas)), dma((number + extra, replicas)),
        ],
        compiler_params=pltpu.CompilerParams(collective_id=collective_id, has_side_effects=True, vmem_limit_bytes=62 << 20),
        cost_estimate=pl.CostEstimate(flops=0, bytes_accessed=moved * 4, transcendentals=0),
    )(*[a.reshape((line, across, cores) + a.shape[1:]) for a in arrays], *extras)


FIRST_VECTOR = 34


def mixing(mix):
    rows = mix.shape[0]
    place = lax.broadcasted_iota(jnp.int32, (rows, 2 * rows), 1) - 2 * lax.broadcasted_iota(jnp.int32, (rows, 2 * rows), 0)
    own = jnp.broadcast_to(mix[:, :1], place.shape)
    next_one = jnp.broadcast_to(mix[:, 64:65], place.shape)
    return jnp.where(place == 0, own, jnp.where(place == 1, next_one, 0.0)).astype(bf16)


def project_kernel(
    tokens_ref, mix_ref, weight_ref, small_ref,
    pooled_ref, content_ref, position_ref, ordering_ref, key_ref, value_ref,
):
    width = tokens_ref.shape[1]
    tokens = tokens_ref[...]
    pooled = nn(mixing(mix_ref[...]), tokens)
    pooled_ref[...] = pooled
    key_ref[...] = nn(tokens, weight_ref[:, width : 2 * width]).astype(bf16)
    value_ref[...] = nn(tokens, weight_ref[:, 2 * width :]).astype(bf16)
    queries = nn(pooled.astype(bf16), weight_ref[:, :width])
    bias = small_ref[FIRST_VECTOR : FIRST_VECTOR + 3, :].astype(f32)
    content_ref[...] = ((queries + bias[0:1]) * (0.125 * LOG2E)).astype(bf16)
    position_ref[...] = (queries + bias[1:2]).astype(bf16)
    ordering_ref[...] = (queries + bias[2:3]).astype(bf16)


def project(tokens, mix, weight, small):
    length, width = tokens.shape
    block = 256
    steps = length // block
    whole = pl.BlockSpec((block, width), lambda i: (i, 0))
    half = pl.BlockSpec((block // 2, width), lambda i: (i, 0))
    rows = jax.ShapeDtypeStruct((length // 2, width), bf16)
    full = jax.ShapeDtypeStruct((length, width), bf16)
    return pl.pallas_call(
        project_kernel,
        name="project",
        grid=(steps,),
        out_shape=(jax.ShapeDtypeStruct((length // 2, width), f32), rows, rows, rows, full, full),
        in_specs=[whole, pl.BlockSpec((block // 2, 128), lambda i: (i, 0)), fixed(*weight.shape), fixed(*small.shape)],
        out_specs=[half, half, half, half, whole, whole],
        compiler_params=pltpu.CompilerParams(vmem_limit_bytes=40 << 20),
        cost_estimate=pl.CostEstimate(flops=5 * length * width * width, bytes_accessed=10 * length * width, transcendentals=0),
    )(tokens, mix, weight, small)


def mean(values):
    return jnp.mean(values, axis=1, keepdims=True)


def normalize(values):
    centered = values - mean(values)
    inverse = lax.rsqrt(mean(centered * centered) + 1e-05)
    return centered * inverse, inverse


def norm_back(grad, normed, inverse):
    return inverse * (grad - mean(grad) - normed * mean(grad * normed))


def column_sum(values):
    return jnp.sum(values, axis=0, keepdims=True)


def middle_kernel(
    blocks, context_ref, pooled_ref, cotangent_ref, wide_ref, outer_ref, small_ref, bias_ref,
    layer_ref, sum_ref, context_grad_ref, sums_ref, inner_sums_ref, output_out, inner_out, outer_out,
    act, back, slope, first_all, outer_all, attended_all, context_all,
):
    step = pl.program_id(0)
    size, width = pooled_ref.shape
    hidden = bias_ref.shape[1]
    chunks = [slice(c * width, (c + 1) * width) for c in range(hidden // width)]

    @pl.when(step == 0)
    def _():
        sums_ref[...] = jnp.zeros(sums_ref.shape, f32)
        inner_sums_ref[...] = jnp.zeros(inner_sums_ref.shape, f32)

    @pl.when(step < blocks)
    def _():
        rows = pl.ds(pl.multiple_of(step * size, size), size)

        def vector(j):
            return small_ref[FIRST_VECTOR + j : FIRST_VECTOR + j + 1, :].astype(f32)

        context = context_ref[...]
        context_all[rows, :] = context
        first_norm, first_inverse = normalize(pooled_ref[...] + nn(context, wide_ref[:, :width]))
        first = first_norm * vector(3) + vector(4)
        first_low = first.astype(bf16)
        first_all[rows, :] = first_low
        outer = None
        for cut in chunks:
            inner = nn(first_low, wide_ref[:, width + cut.start : width + cut.stop]) + bias_ref[:, cut].astype(f32)
            cumulative = 0.5 * (1.0 + lax.erf(inner * math.sqrt(0.5)))
            act_low = (inner * cumulative).astype(bf16)
            act[rows, cut] = act_low
            slope[:, cut] = cumulative + inner * (jnp.exp(-0.5 * inner * inner) * (1.0 / math.sqrt(2.0 * math.pi)))
            part = nn(act_low, outer_ref[cut, :])
            outer = part if outer is None else outer + part
        second_norm, second_inverse = normalize(first + outer + vector(5))
        layer_ref[...] = (second_norm * vector(6) + vector(7)).astype(bf16)
        cotangent = cotangent_ref[...].astype(f32)
        mid_grad = norm_back(cotangent * vector(6), second_norm, second_inverse)
        outer_low = mid_grad.astype(bf16)
        outer_all[rows, :] = outer_low
        first_grad = mid_grad
        for cut in chunks:
            inner_grad = nt(outer_low, outer_ref[cut, :]) * slope[:, cut]
            inner_low = inner_grad.astype(bf16)
            back[rows, cut] = inner_low
            inner_sums_ref[0:1, cut] += column_sum(inner_low.astype(f32))
            first_grad = first_grad + nt(inner_low, wide_ref[:, width + cut.start : width + cut.stop])
        sum_grad = norm_back(first_grad * vector(3), first_norm, first_inverse)
        sum_ref[...] = sum_grad
        attended_low = sum_grad.astype(bf16)
        attended_all[rows, :] = attended_low
        context_grad_ref[...] = nt(attended_low, wide_ref[:, :width]).astype(bf16)
        for j, term in enumerate(
            (first_grad * first_norm, first_grad, outer_low.astype(f32), cotangent * second_norm, cotangent)
        ):
            sums_ref[j : j + 1, :] += column_sum(term)

    for c, cut in enumerate(chunks):

        @pl.when(step == blocks + c)
        def _():
            outer_out[...] = tn(act[:, cut], outer_all[...]).astype(bf16)
            inner_out[...] = tn(first_all[...], back[:, cut]).astype(bf16)

    @pl.when(step == blocks + len(chunks))
    def _():
        output_out[...] = tn(context_all[...], attended_all[...]).astype(bf16)


def middle(context, pooled, cotangent, wide, outer, small, bias):
    rows, width = context.shape
    hidden = bias.shape[1]
    size = 256
    blocks, chunks = rows // size, hidden // width
    block = pl.BlockSpec((size, width), lambda i: (jnp.minimum(i, blocks - 1), 0))
    chunk = lambda i: jnp.clip(i - blocks, 0, chunks - 1)
    low = jax.ShapeDtypeStruct((rows, width), bf16)
    flops = 18 * rows * width * hidden
    return pl.pallas_call(
        functools.partial(middle_kernel, blocks),
        name="middle",
        grid=(blocks + chunks + 1,),
        out_shape=(
            low,
            jax.ShapeDtypeStruct((rows, width), f32),
            low,
            jax.ShapeDtypeStruct((8, width), f32),
            jax.ShapeDtypeStruct((8, hidden), f32),
            jax.ShapeDtypeStruct((width, width), bf16),
            jax.ShapeDtypeStruct((width, hidden), bf16),
            jax.ShapeDtypeStruct((hidden, width), bf16),
        ),
        in_specs=[block, block, block, fixed(*wide.shape), fixed(*outer.shape), fixed(*small.shape), fixed(*bias.shape)],
        out_specs=[
            block, block, block, fixed(8, width), fixed(8, hidden), fixed(width, width),
            pl.BlockSpec((width, width), lambda i: (0, chunk(i))),
            pl.BlockSpec((width, width), lambda i: (chunk(i), 0)),
        ],
        scratch_shapes=[
            pltpu.VMEM((rows, hidden), bf16),
            pltpu.VMEM((rows, hidden), bf16),
            pltpu.VMEM((size, hidden), f32),
            pltpu.VMEM((rows, width), bf16),
            pltpu.VMEM((rows, width), bf16),
            pltpu.VMEM((rows, width), bf16),
            pltpu.VMEM((rows, width), bf16),
        ],
        compiler_params=pltpu.CompilerParams(vmem_limit_bytes=60 << 20),
        cost_estimate=pl.CostEstimate(flops=flops, bytes_accessed=40 * rows * width, transcendentals=2 * rows * hidden),
    )(context, pooled, cotangent, wide, outer, small, bias)


def tail_kernel(
    tokens_ref, key_ref, value_ref, query_ref, sum_ref, pooled_ref, mix_ref, weight_ref,
    tokens_grad_ref, weight_grad_ref, total,
):
    step = pl.program_id(0)
    width = tokens_ref.shape[1]

    @pl.when(step == 0)
    def _():
        total[...] = jnp.zeros(total.shape, f32)

    tokens, query_low, key_low, value_low = tokens_ref[...], query_ref[...], key_ref[...], value_ref[...]
    pooled_grad = sum_ref[...] + nt(query_low, weight_ref[:, :width])
    coarse = pooled_grad.astype(bf16)
    fine = (pooled_grad - coarse.astype(f32)).astype(bf16)
    mix = mixing(mix_ref[...])
    tokens_grad_ref[...] = (
        tn(mix, coarse) + tn(mix, fine)
        + nt(key_low, weight_ref[:, width : 2 * width])
        + nt(value_low, weight_ref[:, 2 * width :])
    )
    total[:, :width] += tn(pooled_ref[...].astype(bf16), query_low)
    total[:, width : 2 * width] += tn(tokens, key_low)
    total[:, 2 * width :] += tn(tokens, value_low)

    @pl.when(step == pl.num_programs(0) - 1)
    def _():
        weight_grad_ref[...] = total[...].astype(bf16)


def tail(tokens, key_low, value_low, query_low, sum_grad, pooled, mix, weight):
    length, width = tokens.shape
    block = 256
    whole = pl.BlockSpec((block, width), lambda i: (i, 0))
    half = pl.BlockSpec((block // 2, width), lambda i: (i, 0))
    return pl.pallas_call(
        tail_kernel,
        name="tail",
        grid=(length // block,),
        out_shape=(jax.ShapeDtypeStruct((length, width), f32), jax.ShapeDtypeStruct((width, 3 * width), bf16)),
        in_specs=[whole, whole, whole, half, half, half, pl.BlockSpec((block // 2, 128), lambda i: (i, 0)), fixed(*weight.shape)],
        out_specs=[whole, fixed(width, 3 * width)],
        scratch_shapes=[pltpu.VMEM((width, 3 * width), f32)],
        compiler_params=pltpu.CompilerParams(vmem_limit_bytes=48 << 20),
        cost_estimate=pl.CostEstimate(flops=10 * length * width * width, bytes_accessed=16 * length * width, transcendentals=0),
    )(tokens, key_low, value_low, query_low, sum_grad, pooled, mix, weight)


def body(
    mesh,
    tokens,
    segment_ids,
    query_weight,
    key_weight,
    value_weight,
    output_weight,
    relative_table,
    order_table,
    content_bias,
    position_bias,
    order_bias,
    first_gain,
    first_shift,
    inner_weight,
    inner_bias,
    outer_weight,
    outer_bias,
    second_gain,
    second_shift,
    cotangent,
):
    shards = mesh.shape["shard"]
    width = tokens.shape[1]
    hidden = inner_weight.shape[1]
    each = width // shards
    folds = hidden // width
    vectors = (content_bias, position_bias, order_bias, first_gain, first_shift, outer_bias, second_gain, second_shift)
    small = jnp.concatenate(
        [relative_table, order_table] + [v[None, :] for v in vectors] + [inner_bias.reshape(folds, each)], 0
    )
    small_rows = small.shape[0]
    spare = -small_rows % 16
    small = jnp.pad(small, ((0, spare), (0, 128 - each)))
    projections, small_all = gather(mesh, [jnp.concatenate([query_weight, key_weight, value_weight], 1), small], 0)
    projections = projections.reshape(width, 3 * width)
    small_all = small_all[:, :, :each].transpose(1, 0, 2).reshape(-1, width)
    weight_relative, weight_order = small_all[:32], small_all[32:34]
    bias_inner = small_all[42 : 42 + folds].reshape(folds, shards, each).transpose(1, 0, 2).reshape(1, hidden)
    wide = lax.all_gather(jnp.concatenate([output_weight, inner_weight], 1), "shard", axis=0, tiled=True)
    weight_outer = lax.all_gather(outer_weight, "shard", axis=0, tiled=True)

    joined = (segment_ids[0, 0::2] == segment_ids[0, 1::2])[:, None]
    own = jnp.where(joined, 0.5, 1.0)
    mix = jnp.where(jnp.arange(128)[None, :] < 64, own, 1.0 - own)
    pooled, content, position, ordering, keys, values = project(tokens, mix, projections, small_all)
    behind, ahead = ranges(segment_ids)
    document, away = documents(segment_ids)
    probs, context, mixed, inverse = attend(
        behind, ahead, content, position, ordering, keys, values, weight_relative, weight_order, away, document
    )
    layer_out, sum_grad, context_grad, sums, inner_sums, output_grad, inner_grad, outer_grad = middle(
        context, pooled, cotangent, wide, weight_outer, small_all, bias_inner
    )
    query_low, key_low, value_low, relative_grad, order_grad, bias_sums = attend_back(
        behind, ahead, probs, context_grad, mixed, inverse, content, position, ordering,
        keys, values, weight_relative, weight_order,
    )
    tokens_grad, projection_grad = tail(tokens, key_low, value_low, query_low, sum_grad, pooled, mix, projections)
    small_grad = jnp.concatenate(
        [relative_grad, order_grad[:2], bias_sums[:3], sums[:5],
         inner_sums[0].reshape(shards, folds, each).transpose(1, 0, 2).reshape(folds, width)],
        0,
    )
    small_grad = small_grad.reshape(small_rows, shards, each).transpose(1, 0, 2)
    small_grad = jnp.pad(small_grad, ((0, 0), (0, spare), (0, 128 - each))).astype(bf16)
    outer_part = lax.psum_scatter(outer_grad, "shard", scatter_dimension=0, tiled=True)
    inner_sum, output_sum, projection_sum, small_sum, outer_sum = scatter(
        mesh,
        [
            inner_grad.reshape(shards, each, hidden),
            output_grad.reshape(shards, each, width),
            projection_grad.reshape(shards, each, 3 * width),
            small_grad,
        ],
        [width, width, width, 128],
        [outer_part],
        1,
    )
    small_sum = small_sum[:, :each]
    own = [small_sum[34 + j] for j in range(8)]
    return (
        layer_out,
        tokens_grad,
        *[projection_sum[:, j * width : (j + 1) * width] for j in range(3)],
        output_sum,
        small_sum[:32],
        small_sum[32:34],
        *own[:5],
        inner_sum,
        small_sum[42 : 42 + folds].reshape(folds * each),
        outer_sum,
        *own[5:],
    )


def solution(mesh):
    placed = (
        P(("rep", "shard"), None),
        P(("rep", "shard"), None),
        P("shard", None),
        P("shard", None),
        P("shard", None),
        P("shard", None),
        P(None, "shard"),
        P(None, "shard"),
        P("shard"),
        P("shard"),
        P("shard"),
        P("shard"),
        P("shard"),
        P("shard", None),
        P("shard"),
        P("shard", None),
        P("shard"),
        P("shard"),
        P("shard"),
        P(("rep", "shard"), None),
    )
    return jax.shard_map(
        functools.partial(body, mesh),
        mesh=mesh,
        in_specs=placed,
        out_specs=(
            P(("rep", "shard"), None),
            P(("rep", "shard"), None),
            P("shard", None),
            P("shard", None),
            P("shard", None),
            P("shard", None),
            P(None, "shard"),
            P(None, "shard"),
            P("shard"),
            P("shard"),
            P("shard"),
            P("shard"),
            P("shard"),
            P("shard", None),
            P("shard"),
            P("shard", None),
            P("shard"),
            P("shard"),
            P("shard"),
        ),
        check_vma=False,
    )
```

```python
import functools
import math

import jax
import jax.numpy as jnp
import numpy as np
from jax import lax
from jax.experimental import pallas as pl
from jax.experimental.pallas import tpu as pltpu
from jax.sharding import PartitionSpec as P

LIMITS = (1, 2, 3, 4, 5, 6, 7, 8, 12, 16, 24, 32, 48, 64, 128)
BQ = 128
NEAR = 640
CHUNK = 256
LOG2E = math.log2(math.e)
LN2 = math.log(2.0)
BIG = 1e30
f32 = jnp.float32
bf16 = jnp.bfloat16


def bucket_of(offset):
    distance = np.abs(offset)
    passed = sum((distance >= limit).astype(np.int32) for limit in LIMITS)
    return np.where(offset < 0, 15 + passed + (distance >= 256), passed).astype(np.int32)


def near_index():
    row = np.arange(BQ)[None, :, None]
    tile = np.arange(-2, 3)[:, None, None]
    lane = np.arange(128)[None, None, :]
    return bucket_of(128 * tile + lane - 2 * row)


def bucket_onehot():
    out = np.zeros((4 * 128, 128), np.float32)
    offsets = np.concatenate([np.arange(-256, 128), np.full(64, -300), np.full(64, 300)])
    out[np.arange(512), bucket_of(offsets)] = 1
    out[:, 32] = offsets >= 0
    out[:, 33] = offsets < 0
    return out


def nt(left, right):
    return lax.dot_general(left, right, (((1,), (1,)), ((), ())), preferred_element_type=f32)


def nn(left, right):
    return lax.dot_general(left, right, (((1,), (0,)), ((), ())), preferred_element_type=f32)


def tn(left, right):
    return lax.dot_general(left, right, (((0,), (0,)), ((), ())), preferred_element_type=f32)


def halves(array):
    low = lax.broadcasted_iota(jnp.int32, array.shape, 1) < 64
    zero = jnp.zeros_like(array)
    return jnp.where(low, array, zero), jnp.where(low, zero, array)


def pick(array):
    half = array.shape[0] // 2
    low = lax.broadcasted_iota(jnp.int32, (half, 128), 1) < 64
    return jnp.where(low, array[:half], array[half:])


def take(table, index):
    numbers = lax.GatherDimensionNumbers(
        offset_dims=(), collapsed_slice_dims=(1,), start_index_map=(1,),
        operand_batching_dims=(0,), start_indices_batching_dims=(0,),
    )
    return lax.gather(table, index[:, :, None], numbers, (1, 1), mode=lax.GatherScatterMode.PROMISE_IN_BOUNDS)


def lanes_of(p):
    return slice(128 * p, 128 * p + 128)


def far_start(chunk, behind, far, near):
    start = jnp.where(chunk < behind, near - CHUNK * (chunk + 1), near + NEAR + CHUNK * (chunk - behind))
    return pl.multiple_of(jnp.where(chunk < far, start, 0), 128)


def forward_kernel(
    group, behind_ref, ahead_ref, content_ref, position_ref, ordering_ref, key_ref, value_ref,
    relative_ref, order_ref, away_ref, document_ref, index_ref,
    probs_ref, context_ref, mixed_ref, inverse_ref,
    keys, values, table, bias, scores, peak, total,
):
    step = pl.program_id(1)
    length = key_ref.shape[0]

    @pl.when((step == 0) & (pl.program_id(0) == 0))
    def _():
        for p in range(group):
            for scratch in (keys, values):
                scratch[p, :256, :128] = jnp.zeros((256, 128), bf16)
                scratch[p, 256 + length :, :128] = jnp.zeros((256, 128), bf16)
            keys[p, :, 128:] = away_ref[...]
            values[p, :, 128:] = jnp.ones((length + 512, 128), bf16)

    @pl.when(step == 0)
    def _():
        after = lax.broadcasted_iota(jnp.int32, (32, 128), 0) < 16
        table[...] = jnp.zeros(table.shape, bf16)
        for p in range(group):
            lanes = lanes_of(p)
            keys[p, 256 : 256 + length, :128] = key_ref[:, lanes]
            values[p, 256 : 256 + length, :128] = value_ref[:, lanes]
            orders = jnp.where(after, order_ref[0:1, lanes].astype(f32), order_ref[1:2, lanes].astype(f32)).astype(bf16)
            for half, (relative, order) in enumerate(zip(halves(relative_ref[:, lanes]), halves(orders))):
                both = jnp.concatenate([relative, order], 1)
                table[p, 128 * half : 128 * half + 32, :] = both
                for side, bucket in ((0, 31), (1, 15)):
                    start = 256 + 256 * side + 128 * half
                    table[p, start : start + 128, :] = jnp.broadcast_to(both[bucket : bucket + 1].astype(f32), (128, 256)).astype(bf16)

    document = document_ref[...]
    near = pl.multiple_of(step * 256, 256)
    queries = []
    for p in range(group):
        even, odd = halves(content_ref[:, lanes_of(p)])
        queries.append(jnp.concatenate(
            [jnp.concatenate([even, document], 1), jnp.concatenate([odd, document], 1)], 0
        ))
    for p in range(group):
        lanes = lanes_of(p)
        places = nt(jnp.concatenate([position_ref[:, lanes], ordering_ref[:, lanes]], 1), table[p]) * (0.125 * LOG2E)
        place = (places[:, :128], places[:, 128:256])
        near_scores = nt(queries[p], keys[p, pl.ds(near, NEAR), :])
        for half in range(2):
            rows = slice(BQ * half, BQ * half + BQ)
            for side in range(2):
                start = 256 + 256 * side + 128 * half
                bias[p, rows, 128 * side : 128 * side + 128] = places[:, start : start + 128]
            for quarter in range(2):
                own = slice(64 * quarter, 64 * quarter + 64)
                rows = slice(BQ * half + 64 * quarter, BQ * half + 64 * quarter + 64)
                best = None
                for tile in range(NEAR // 128):
                    if tile == 4 - 4 * quarter:
                        extra = bias[p, rows, 128 - 128 * quarter : 256 - 128 * quarter]
                    else:
                        extra = take(place[half][own], index_ref[tile, own])
                    part = near_scores[rows, 128 * tile : 128 * tile + 128] + extra
                    scores[p, rows, pl.ds(near + 128 * tile, 128)] = part
                    best = part if best is None else jnp.maximum(best, part)
                peak[p, rows, :] = best
    behind = behind_ref[step]
    far = behind + ahead_ref[step]

    def start_of(chunk):
        return far_start(chunk, behind, far, near)

    @pl.loop(0, (far + 1) // 2)
    def _(two):
        for chunk in (2 * two, 2 * two + 1):
            start = start_of(chunk)
            place = pl.multiple_of(jnp.where(chunk < behind, 0, 128), 128)
            for p in range(group):
                part = nt(queries[p], keys[p, pl.ds(start, CHUNK), :])
                extra = bias[p, :, pl.ds(place, 128)]
                left, right = part[:, :128] + extra, part[:, 128:] + extra
                scores[p, :, pl.ds(start, 128)] = left
                scores[p, :, pl.ds(start + 128, 128)] = right
                peak[p] = jnp.maximum(peak[p], jnp.maximum(left, right))

    tops = [jnp.max(peak[p], axis=1, keepdims=True) for p in range(group)]
    for p in range(group):
        peak[p] = jnp.broadcast_to(tops[p], (2 * BQ, 128))
        probs = jnp.exp2(scores[p, :, pl.ds(near, NEAR)] - tops[p]).astype(bf16)
        probs_ref[p, 0, :, pl.ds(near, NEAR)] = probs
        total[p] = nn(probs, values[p, pl.ds(near, NEAR), :])

    @pl.loop(0, (far + 1) // 2)
    def _(two):
        starts = [start_of(2 * two), start_of(2 * two + 1)]
        for p in range(group):
            top = peak[p]
            parts = []
            for start in starts:
                left = jnp.exp2(scores[p, :, pl.ds(start, 128)] - top).astype(bf16)
                right = jnp.exp2(scores[p, :, pl.ds(start + 128, 128)] - top).astype(bf16)
                probs = jnp.concatenate([left, right], 1)
                probs_ref[p, 0, :, pl.ds(start, CHUNK)] = probs
                parts.append(nn(probs, values[p, pl.ds(start, CHUNK), :]))
            total[p] += parts[0] + parts[1]

    for p in range(group):
        lanes = lanes_of(p)
        inverse = 1.0 / total[p, :, 128:]
        mixed = pick(total[p, :, :128] * inverse)
        inverse_ref[:, lanes] = pick(inverse)
        mixed_ref[:, lanes] = mixed
        context_ref[:, lanes] = mixed.astype(bf16)


def backward_kernel(
    group, behind_ref, ahead_ref, probs_ref, grad_ref, mixed_ref, inverse_ref, content_ref, position_ref, ordering_ref,
    key_ref, value_ref, relative_ref, order_ref, turn_ref, onehot_ref,
    query_ref, key_low_ref, value_low_ref, relative_out, order_out, sums_out,
    keys, values, table, key_total, value_total, query_total, far_total, bucket, table_total, sums,
):
    step = pl.program_id(1)
    length = key_ref.shape[0]

    @pl.when(step == 0)
    def _():
        slot = lax.broadcasted_iota(jnp.int32, (32, 128), 0)
        table[...] = jnp.zeros(table.shape, bf16)
        for p in range(group):
            lanes = lanes_of(p)
            for scratch, ref in ((keys, key_ref), (values, value_ref)):
                scratch[p, :256, :] = jnp.zeros((256, 128), bf16)
                scratch[p, 256 + length :, :] = jnp.zeros((256, 128), bf16)
                scratch[p, 256 : 256 + length, :] = ref[:, lanes]
            even, odd = halves(relative_ref[:, lanes])
            table[p, 0:32, :128] = even
            table[p, 128:160, :128] = odd
            orders = jnp.where(slot == 0, order_ref[0:1, lanes].astype(f32), order_ref[1:2, lanes].astype(f32))
            even, odd = halves(jnp.where(slot < 2, orders, 0.0))
            table[p, 32:64, 128:] = even.astype(bf16)
            table[p, 160:192, 128:] = odd.astype(bf16)
        key_total[...] = jnp.zeros(key_total.shape, f32)
        value_total[...] = jnp.zeros(value_total.shape, f32)
        table_total[...] = jnp.zeros(table_total.shape, f32)
        sums[...] = jnp.zeros(sums.shape, f32)

    near = pl.multiple_of(step * 256, 256)
    grads, grads_t, content_t, deltas = [], [], [], []
    for p in range(group):
        lanes = lanes_of(p)
        scaled = (grad_ref[:, lanes].astype(f32) * inverse_ref[:, lanes]).astype(bf16)
        both = jnp.concatenate(halves(scaled), 0)
        even, odd = halves(scaled.astype(f32) * mixed_ref[:, lanes])
        deltas.append(jnp.concatenate(
            [jnp.sum(even, axis=1, keepdims=True), jnp.sum(odd, axis=1, keepdims=True)], 0
        ))
        grads.append(both)
        grads_t.append(both.T)
        content_t.append(jnp.concatenate(halves(content_ref[:, lanes]), 0).T)

    def visit(p, start, size):
        probs = probs_ref[p, 0, :, pl.ds(start, size)]
        prob_grad = nt(grads[p], values[p, pl.ds(start, size), :])
        score = probs.astype(f32) * (prob_grad - deltas[p])
        score_low = score.astype(bf16)
        value_total[p, :, pl.ds(start, size)] += nn(grads_t[p], probs)
        key_total[p, :, pl.ds(start, size)] += nn(content_t[p], score_low)
        return score, nn(score_low, keys[p, pl.ds(start, size), :])

    turn = turn_ref[...]
    turns = jnp.concatenate([turn, turn], 0)
    lane = lax.broadcasted_iota(jnp.int32, (64, 128), 1)
    row = lax.broadcasted_iota(jnp.int32, (64, 128), 0)
    first = lane + 2 * row < 128
    zero = jnp.zeros((64, 128), f32)
    for p in range(group):
        score, query_total[p] = visit(p, near, NEAR)
        parts = [score[:, 128 * t : 128 * t + 128] for t in range(5)]
        tiles = [take(part, turns) for part in parts]
        for quarter in range(4):
            rows = slice(64 * quarter, 64 * quarter + 64)
            own = [tile[rows] for tile in tiles]
            if quarter % 2 == 0:
                near_parts = [jnp.where(first, own[t], own[t + 1]) for t in range(3)]
                far_total[p, 0, rows] = jnp.where(first, zero, own[0])
                far_total[p, 1, rows] = jnp.where(first, own[3], zero) + parts[4][rows]
            else:
                near_parts = [jnp.where(first, own[t + 1], own[t + 2]) for t in range(3)]
                far_total[p, 0, rows] = parts[0][rows] + jnp.where(first, zero, own[1])
                far_total[p, 1, rows] = jnp.where(first, own[4], zero)
            for t in range(3):
                bucket[p, rows, 128 * t : 128 * t + 128] = near_parts[t].astype(bf16)
    behind = behind_ref[step]

    far = behind + ahead_ref[step]

    @pl.loop(0, (far + 1) // 2)
    def _(two):
        for chunk in (2 * two, 2 * two + 1):
            start = far_start(chunk, behind, far, near)
            side = jnp.where(chunk < behind, 0, 1)
            for p in range(group):
                score, part = visit(p, start, CHUNK)
                query_total[p] += part
                far_total[p, side] += score[:, :128] + score[:, 128:]

    for p in range(group):
        lanes = lanes_of(p)
        folded = [far_total[p, side] + pltpu.roll(far_total[p, side], 64, 1) for side in range(2)]
        low_lane = lax.broadcasted_iota(jnp.int32, folded[0].shape, 1) < 64
        bucket[p, :, 384:] = jnp.where(low_lane, *folded).astype(bf16)
        low = (nn(bucket[p], onehot_ref[...]) * 0.125).astype(bf16)
        low = jnp.concatenate([low[:BQ], low[BQ:]], 1)
        placed = nn(low, table[p])
        content_grad = pick(query_total[p]) * 0.125
        query_ref[:, lanes] = (content_grad + placed[:, :128] + placed[:, 128:]).astype(bf16)
        table_total[p] += tn(low, jnp.concatenate([position_ref[:, lanes], ordering_ref[:, lanes]], 1))
        for j, term in enumerate((content_grad, placed[:, :128], placed[:, 128:])):
            sums[j : j + 1, lanes] += jnp.sum(term, axis=0, keepdims=True)

    @pl.when(step == pl.num_programs(1) - 1)
    def _():
        low_lane = lax.broadcasted_iota(jnp.int32, (32, 128), 1) < 64
        for p in range(group):
            lanes = lanes_of(p)
            key_low_ref[:, lanes] = (key_total[p, :, 256 : 256 + length] * LN2).T.astype(bf16)
            value_low_ref[:, lanes] = value_total[p, :, 256 : 256 + length].T.astype(bf16)
            relative_out[:, lanes] = jnp.where(low_lane, table_total[p, 0:32, :128], table_total[p, 128:160, :128])
            order_out[:, lanes] = jnp.where(low_lane[:8], table_total[p, 32:40, 128:], table_total[p, 160:168, 128:])
        sums_out[...] = sums[...]


def fixed(*shape):
    return pl.BlockSpec(shape, lambda *_: (0,) * len(shape), pipeline_mode=pl.Buffered(1))


def ranges(segments):
    length = segments.shape[1]
    own = segments[0][None, :]
    place = jnp.arange(length, dtype=jnp.int32)[None, :]
    start = 2 * BQ * jnp.arange(length // (2 * BQ), dtype=jnp.int32)
    count = lambda marks: jnp.sum(marks.astype(jnp.int32), axis=1)
    at = lambda where: jnp.sum(jnp.where(place == where[:, None], own, 0), axis=1)
    first = count(own < at(start)[:, None])
    last = count(own <= at(start + 2 * BQ - 2)[:, None])
    behind = jnp.maximum(start - 256 - first + CHUNK - 1, 0) // CHUNK
    ahead = jnp.maximum(last - (start - 256 + NEAR) + CHUNK - 1, 0) // CHUNK
    return behind, ahead


GROUP = 3


def attend(behind, ahead, content, position, ordering, keys, values, relative, order, away, document):
    rows, width = content.shape
    length = keys.shape[0]
    padded = length + 512
    pairs, blocks, group = width // 128, rows // BQ, GROUP
    wide = 128 * group
    tile = pl.BlockSpec((BQ, wide), lambda p, i, *_: (i, p))
    whole = pl.BlockSpec((length, wide), lambda p, i, *_: (0, p), pipeline_mode=pl.Buffered(1))
    return pl.pallas_call(
        functools.partial(forward_kernel, group),
        name="attend",
        out_shape=(
            jax.ShapeDtypeStruct((pairs, blocks, 2 * BQ, padded), bf16),
            jax.ShapeDtypeStruct((rows, width), bf16),
            jax.ShapeDtypeStruct((rows, width), f32),
            jax.ShapeDtypeStruct((rows, width), f32),
        ),
        grid_spec=pltpu.PrefetchScalarGridSpec(
            num_scalar_prefetch=2,
            grid=(pairs // group, blocks),
            in_specs=[
                tile, tile, tile, whole, whole,
                pl.BlockSpec((32, wide), lambda p, i, *_: (0, p)),
                pl.BlockSpec((2, wide), lambda p, i, *_: (0, p)),
                fixed(padded, 128),
                pl.BlockSpec((BQ, 128), lambda p, i, *_: (i, 0)),
                fixed(5, BQ, 128),
            ],
            out_specs=[pl.BlockSpec((group, 1, 2 * BQ, padded), lambda p, i, *_: (p, i, 0, 0)), tile, tile, tile],
            scratch_shapes=[
                pltpu.VMEM((group, padded, 256), bf16),
                pltpu.VMEM((group, padded, 256), bf16),
                pltpu.VMEM((group, 768, 256), bf16),
                pltpu.VMEM((group, 2 * BQ, 256), f32),
                pltpu.VMEM((group, 2 * BQ, padded), f32),
                pltpu.VMEM((group, 2 * BQ, 128), f32),
                pltpu.VMEM((group, 2 * BQ, 256), f32),
            ],
        ),
        compiler_params=pltpu.CompilerParams(dimension_semantics=("arbitrary", "arbitrary"), vmem_limit_bytes=62 << 20),
        cost_estimate=pl.CostEstimate(flops=40 * 10**9, bytes_accessed=70 * 10**6, transcendentals=10**7),
    )(behind, ahead, content, position, ordering, keys, values, relative, order, away, document,
      jnp.asarray(near_index()))


def attend_back(behind, ahead, probs, grad, mixed, inverse, content, position, ordering, keys, values, relative, order):
    rows, width = content.shape
    length = keys.shape[0]
    padded = length + 512
    pairs, blocks, group = width // 128, rows // BQ, GROUP
    wide = 128 * group
    tile = pl.BlockSpec((BQ, wide), lambda p, i, *_: (i, p))
    whole = pl.BlockSpec((length, wide), lambda p, i, *_: (0, p), pipeline_mode=pl.Buffered(1))
    small = lambda n: pl.BlockSpec((n, wide), lambda p, i, *_: (0, p))
    turn = (np.arange(128)[None, :] + 2 * np.arange(BQ)[:, None]) % 128
    return pl.pallas_call(
        functools.partial(backward_kernel, group),
        name="attend_back",
        out_shape=(
            jax.ShapeDtypeStruct((rows, width), bf16),
            jax.ShapeDtypeStruct((length, width), bf16),
            jax.ShapeDtypeStruct((length, width), bf16),
            jax.ShapeDtypeStruct((32, width), f32),
            jax.ShapeDtypeStruct((8, width), f32),
            jax.ShapeDtypeStruct((8, width), f32),
        ),
        grid_spec=pltpu.PrefetchScalarGridSpec(
            num_scalar_prefetch=2,
            grid=(pairs // group, blocks),
            in_specs=[
                pl.BlockSpec((group, 1, 2 * BQ, padded), lambda p, i, *_: (p, i, 0, 0)),
                tile, tile, tile, tile, tile, tile, whole, whole, small(32), small(2), fixed(BQ, 128), fixed(512, 128),
            ],
            out_specs=[tile, whole, whole, small(32), small(8), small(8)],
            scratch_shapes=[
                pltpu.VMEM((group, padded, 128), bf16),
                pltpu.VMEM((group, padded, 128), bf16),
                pltpu.VMEM((group, 256, 256), bf16),
                pltpu.VMEM((group, 128, padded), f32),
                pltpu.VMEM((group, 128, padded), f32),
                pltpu.VMEM((group, 2 * BQ, 128), f32),
                pltpu.VMEM((group, 2, 2 * BQ, 128), f32),
                pltpu.VMEM((group, 2 * BQ, 512), bf16),
                pltpu.VMEM((group, 256, 256), f32),
                pltpu.VMEM((8, wide), f32),
            ],
        ),
        compiler_params=pltpu.CompilerParams(dimension_semantics=("arbitrary", "arbitrary"), vmem_limit_bytes=62 << 20),
        cost_estimate=pl.CostEstimate(flops=80 * 10**9, bytes_accessed=70 * 10**6, transcendentals=0),
    )(behind, ahead, probs, grad, mixed, inverse, content, position, ordering, keys, values, relative, order,
      jnp.asarray(turn, jnp.int32), jnp.asarray(bucket_onehot(), bf16))


MESH = pl.DeviceIdType.MESH


class Place:
    def __init__(self, replicas, shards):
        self.replicas, self.shards = replicas, shards
        self.cores = 2 if shards % 2 == 0 else 1
        chips = shards // self.cores
        self.across = 2 if chips % 2 == 0 else 1
        self.line = chips // self.across
        self.replica = lax.axis_index("rep")
        own = lax.axis_index("shard")
        self.own = own
        self.core = lax.rem(own, self.cores)
        self.column = lax.rem(own // self.cores, self.across)
        self.spot = own // (self.cores * self.across)

    def shard(self, spot, column, core):
        return (spot * self.across + column) * self.cores + core

    def other_column(self, step):
        return lax.rem(self.column + step, self.across)

    def other_replica(self, step):
        return lax.rem(self.replica + step, self.replicas)

    def device(self, spot=None, column=None, core=None, replica=None):
        spot = self.spot if spot is None else spot
        column = self.column if column is None else column
        core = self.core if core is None else core
        replica = self.replica if replica is None else replica
        return (replica, self.shard(spot, column, core))

    def meet(self):
        barrier = pltpu.get_barrier_semaphore()

        def greet(device):
            pl.semaphore_signal(barrier, inc=1, device_id=device, device_id_type=MESH)

        fixed = 0
        if self.cores > 1:
            greet(self.device(core=1 - self.core))
            fixed += 1
        for step in range(1, self.across):
            greet(self.device(column=self.other_column(step)))
            fixed += 1
        for step in range(1, self.replicas):
            greet(self.device(replica=self.other_replica(step)))
            fixed += 1
        for step, there in ((1, self.spot < self.line - 1), (-1, self.spot > 0)):

            @pl.when(there)
            def _():
                greet(self.device(spot=self.spot + step))

        lined = (self.spot < self.line - 1).astype(jnp.int32) + (self.spot > 0).astype(jnp.int32)
        pl.semaphore_wait(barrier, fixed + lined)


def parts_of(columns, replicas):
    return replicas if columns % (128 * replicas) == 0 else 1


def columns_of(part, parts, columns):
    size = columns // parts
    return pl.ds(pl.multiple_of(part * size, 128), size)


def when(condition, action):
    if condition is True:
        action()
    else:
        pl.when(condition)(action)


def gather_kernel(replicas, shards, count, *refs):
    here = Place(replicas, shards)
    sources, wholes = refs[:count], refs[count : 2 * count]
    line_send, line_recv, cross_send, cross_recv, rep_send, rep_recv, core_send, core_recv = refs[2 * count :]
    here.meet()
    pending = []

    def send(source, whole_view, send_sem, recv_sem, device, condition=True):
        copy = pltpu.make_async_remote_copy(
            src_ref=source, dst_ref=whole_view, send_sem=send_sem, recv_sem=recv_sem, device_id=device, device_id_type=MESH
        )
        when(condition, copy.start)
        pending.append((condition, copy.wait_send))

    def arrived(view, recv_sem, condition=True):
        copy = pltpu.make_async_remote_copy(
            src_ref=view, dst_ref=view, send_sem=recv_sem, recv_sem=recv_sem, device_id=here.device(), device_id_type=MESH
        )
        when(condition, copy.wait_recv)

    def view(k, spot, column, core, part=None):
        whole = wholes[k].at[here.shard(spot, column, core)]
        if part is None:
            return whole
        columns = whole.shape[1]
        return whole.at[:, columns_of(part, parts_of(columns, replicas), columns)]

    def spread(k, spot, condition, own=False):
        columns = wholes[k].shape[2]
        parts = parts_of(columns, replicas)
        part = here.replica if parts > 1 else 0
        target = view(k, spot, here.column, here.core)
        source = sources[k] if own else target
        for step in range(1, here.across):
            cut = columns_of(part, parts, columns)
            send(source.at[:, cut], target.at[:, cut], cross_send.at[k, step, spot], cross_recv.at[k, here.column, spot],
                 here.device(column=here.other_column(step)), condition)
        if here.cores > 1:
            send(source, target, core_send.at[k, 0, here.column, spot], core_recv.at[k, 0, here.column, spot],
                 here.device(core=1 - here.core), condition)

    def crossed(k, spot, condition):
        columns = wholes[k].shape[2]
        parts = parts_of(columns, replicas)
        part = here.replica if parts > 1 else 0
        for step in range(1, here.across):
            column = here.other_column(step)
            piece = view(k, spot, column, here.core, part)
            arrived(piece, cross_recv.at[k, column, spot], condition)
            if parts > 1:
                for hop in range(1, replicas):
                    send(piece, piece, rep_send.at[k, hop, column, spot], rep_recv.at[k, here.replica, column, spot],
                         here.device(replica=here.other_replica(hop)), condition)
            if here.cores > 1:
                send(piece, piece, core_send.at[k, 1, column, spot], core_recv.at[k, 1, column, spot],
                     here.device(core=1 - here.core), condition)

    def replicated(k, spot, condition):
        parts = parts_of(wholes[k].shape[2], replicas)
        if parts == 1:
            return
        for step in range(1, here.across):
            column = here.other_column(step)
            for hop in range(1, replicas):
                replica = here.other_replica(hop)
                piece = view(k, spot, column, here.core, replica)
                arrived(piece, rep_recv.at[k, replica, column, spot], condition)
                if here.cores > 1:
                    send(piece, piece, core_send.at[k, 1 + hop, column, spot], core_recv.at[k, 1 + hop, column, spot],
                         here.device(core=1 - here.core), condition)

    def at(distance, action):
        for k in range(count):
            if distance == 0:
                action(k, here.spot, True)
            else:
                action(k, here.spot - distance, here.spot >= distance)
                action(k, here.spot + distance, here.spot + distance < here.line)

    for k in range(count):
        own = view(k, here.spot, here.column, here.core)
        send(sources[k], own, line_send.at[k, 0, here.spot], line_recv.at[k, here.spot],
             here.device(spot=here.spot + 1), here.spot < here.line - 1)
        send(sources[k], own, line_send.at[k, 1, here.spot], line_recv.at[k, here.spot],
             here.device(spot=here.spot - 1), here.spot > 0)
        spread(k, here.spot, True, own=True)
    for k in range(count):
        wholes[k][here.own] = sources[k][...]

    def along(distance):
        for k in range(count):
            for sign in (-1, 1):
                spot = here.spot + sign * distance
                condition = (spot >= 0) & (spot < here.line)
                piece = view(k, spot, here.column, here.core)
                arrived(piece, line_recv.at[k, spot], condition)
                onward = here.spot - sign
                send(piece, piece, line_send.at[k, 0 if sign < 0 else 1, spot], line_recv.at[k, spot],
                     here.device(spot=onward), condition & (onward >= 0) & (onward < here.line))
                spread(k, spot, condition)

    for distance in range(here.line + 2):
        if 1 <= distance < here.line:
            along(distance)
        if 1 <= distance <= here.line:
            at(distance - 1, crossed)
        if 2 <= distance:
            at(distance - 2, replicated)
    if here.cores > 1:
        for k in range(count):
            columns = wholes[k].shape[2]
            parts = parts_of(columns, replicas)
            for spot in range(here.line):
                other = 1 - here.core
                arrived(view(k, spot, here.column, other), core_recv.at[k, 0, here.column, spot])
                for step in range(1, here.across):
                    column = here.other_column(step)
                    part = here.replica if parts > 1 else 0
                    arrived(view(k, spot, column, other, part), core_recv.at[k, 1, column, spot])
                    for hop in range(1, replicas if parts > 1 else 1):
                        arrived(view(k, spot, column, other, here.other_replica(hop)), core_recv.at[k, 1 + hop, column, spot])
    for condition, wait in pending:
        when(condition, wait)


def gather(mesh, arrays, collective_id):
    replicas, shards = mesh.shape["rep"], mesh.shape["shard"]
    count = len(arrays)
    line = shards // 4
    dma = pltpu.SemaphoreType.DMA
    vmem = pl.BlockSpec(memory_space=pltpu.VMEM)
    moved = sum(a.size * 2 * shards for a in arrays)
    return pl.pallas_call(
        functools.partial(gather_kernel, replicas, shards, count),
        name="gather",
        out_shape=[jax.ShapeDtypeStruct((shards,) + a.shape, a.dtype) for a in arrays],
        in_specs=[vmem] * count,
        out_specs=[vmem] * count,
        scratch_shapes=[
            dma((count, 2, line)), dma((count, line)),
            dma((count, 2, line)), dma((count, 2, line)),
            dma((count, replicas, 2, line)), dma((count, replicas, 2, line)),
            dma((count, replicas + 1, 2, line)), dma((count, replicas + 1, 2, line)),
        ],
        compiler_params=pltpu.CompilerParams(collective_id=collective_id, has_side_effects=True, vmem_limit_bytes=56 << 20),
        cost_estimate=pl.CostEstimate(flops=0, bytes_accessed=moved * 4, transcendentals=0),
    )(*arrays)


def scatter_kernel(replicas, shards, count, chunks, extra, *refs):
    here = Place(replicas, shards)
    take = lambda number: [refs_left.pop(0) for _ in range(number)]
    refs_left = list(refs)
    sources, extras, outs, extra_outs = take(count), take(extra), take(count), take(extra)
    core_bufs, rep_bufs, cross_bufs, line_bufs, last_bufs = (take(count) for _ in range(5))
    extra_bufs = take(extra)
    (core_send, core_recv, rep_send, rep_recv, cross_send, cross_recv, line_send, line_recv, last_send, last_recv) = refs_left
    here.meet()
    pending = []

    def send(source, target, send_sem, recv_sem, device, condition=True):
        copy = pltpu.make_async_remote_copy(
            src_ref=source, dst_ref=target, send_sem=send_sem, recv_sem=recv_sem, device_id=device, device_id_type=MESH
        )
        when(condition, copy.start)
        pending.append((condition, copy.wait_send))

    def arrived(view, recv_sem, condition=True):
        copy = pltpu.make_async_remote_copy(
            src_ref=view, dst_ref=view, send_sem=recv_sem, recv_sem=recv_sem, device_id=here.device(), device_id_type=MESH
        )
        when(condition, copy.wait_recv)

    def add(target, source):
        target[...] = target[...] + source[...]

    steps = range(1, here.across)
    hops = range(1, replicas)

    def split(j):
        return parts_of(chunks[j][2], replicas)

    def columns(j, part=None):
        _, low, size = chunks[j]
        if part is None or split(j) == 1:
            return pl.ds(low, size)
        size = size // replicas
        return pl.ds(pl.multiple_of(low + part * size, 128), size)

    def compact(j):
        _, low, size = chunks[j]
        return pl.ds(low // split(j), size // split(j))

    def mixed(j, column):
        k = chunks[j][0]
        mine = core_bufs[k].at[column, :, :, columns(j)]
        own = sources[k].at[:, column, here.core, :, columns(j)]
        if here.cores > 1:
            arrived(mine, core_recv.at[j, column])
            add(mine, own)
        else:
            mine[...] = own[...]

    def stage_rep(j):
        k = chunks[j][0]
        for step in steps:
            column = here.other_column(step)
            mixed(j, column)
            if split(j) > 1:
                for hop in hops:
                    replica = here.other_replica(hop)
                    send(core_bufs[k].at[column, :, :, columns(j, replica)], rep_bufs[k].at[hop - 1, step - 1, :, :, compact(j)],
                         rep_send.at[j, hop, step], rep_recv.at[j, hop, step], here.device(replica=replica))

    def stage_cross(j):
        k = chunks[j][0]
        for step in steps:
            column = here.other_column(step)
            mine = core_bufs[k].at[column, :, :, columns(j, here.replica)]
            if split(j) > 1:
                for hop in hops:
                    piece = rep_bufs[k].at[hop - 1, step - 1, :, :, compact(j)]
                    arrived(piece, rep_recv.at[j, hop, step])
                    add(mine, piece)
            send(mine, cross_bufs[k].at[step - 1, :, :, compact(j)], cross_send.at[j, step], cross_recv.at[j, step],
                 here.device(column=column))
        mixed(j, here.column)

    def stage_line(distance, j):
        k = chunks[j][0]
        if distance == here.line - 1:
            for step in steps:
                piece = cross_bufs[k].at[step - 1, :, :, compact(j)]
                arrived(piece, cross_recv.at[j, step])
                add(core_bufs[k].at[here.column, :, :, columns(j, here.replica)], piece)
        for sign, way in ((1, 0), (-1, 1)):
            target = here.spot + sign * distance
            inside = (target >= 0) & (target < here.line)
            before = here.spot - sign
            fed = inside & (before >= 0) & (before < here.line)
            mine = core_bufs[k].at[here.column, target, :, columns(j)]
            piece = line_bufs[k].at[way, target, :, columns(j)]
            arrived(piece, line_recv.at[j, way, target], fed)
            when(fed, functools.partial(add, mine, piece))
            send(mine, piece, line_send.at[j, way, target], line_recv.at[j, way, target],
                 here.device(spot=here.spot + sign), inside)

    def stage_last(j):
        k = chunks[j][0]
        mine = core_bufs[k].at[here.column, here.spot, :, columns(j)]
        for sign, way in ((1, 0), (-1, 1)):
            before = here.spot - sign
            fed = (before >= 0) & (before < here.line)
            piece = line_bufs[k].at[way, here.spot, :, columns(j)]
            arrived(piece, line_recv.at[j, way, here.spot], fed)
            when(fed, functools.partial(add, mine, piece))
        for hop in hops:
            send(mine, last_bufs[k].at[here.replica, :, columns(j)], last_send.at[j, hop], last_recv.at[j, here.replica],
                 here.device(replica=here.other_replica(hop)))

    def finish(own, buffer, out, semaphore, cut):
        for hop in hops:
            replica = here.other_replica(hop)
            arrived(buffer.at[replica, :, cut], semaphore.at[replica])
        result = None
        for replica in range(replicas):
            term = jnp.where(here.replica == replica, own[...].astype(f32), buffer[replica, :, cut].astype(f32))
            result = term if result is None else result + term
        out[:, cut] = result

    def stage_finish(j):
        k = chunks[j][0]
        finish(core_bufs[k].at[here.column, here.spot, :, columns(j)], last_bufs[k], outs[k], last_recv.at[j], columns(j))

    if here.cores > 1:
        for j, (k, _, _) in enumerate(chunks):
            for step in (*steps, 0):
                column = here.other_column(step)
                send(sources[k].at[:, column, 1 - here.core, :, columns(j)], core_bufs[k].at[column, :, :, columns(j)],
                     core_send.at[j, column], core_recv.at[j, column], here.device(core=1 - here.core))
    stages = [stage_rep, stage_cross]
    stages += [functools.partial(stage_line, distance) for distance in range(here.line - 1, 0, -1)]
    stages += [stage_last, stage_finish]
    total = len(chunks)
    for time in range(total + len(stages) - 1):
        for place in reversed(range(len(stages))):
            if 0 <= time - place < total:
                stages[place](time - place)
        if time == 0:
            for e in range(extra):
                for hop in hops:
                    send(extras[e], extra_bufs[e].at[here.replica], last_send.at[total + e, hop],
                         last_recv.at[total + e, here.replica], here.device(replica=here.other_replica(hop)))
    for e in range(extra):
        finish(extras[e], extra_bufs[e], extra_outs[e], last_recv.at[total + e], pl.ds(0, extras[e].shape[1]))
    for condition, wait in pending:
        when(condition, wait)


def scatter(mesh, arrays, widths, extras, collective_id):
    replicas, shards = mesh.shape["rep"], mesh.shape["shard"]
    count, extra = len(arrays), len(extras)
    dma = pltpu.SemaphoreType.DMA
    vmem = pl.BlockSpec(memory_space=pltpu.VMEM)
    cores = across = 2
    line = shards // (cores * across)
    shapes = [a.shape[1:] for a in arrays]
    chunks = [
        (k, low, min(width, shapes[k][1])) for k, width in enumerate(widths) for low in range(0, shapes[k][1], min(width, shapes[k][1]))
    ]
    cuts = [(shapes[k][0], shapes[k][1] // parts_of(min(width, shapes[k][1]), replicas)) for k, width in enumerate(widths)]
    moved = sum(a.size * 2 for a in arrays)
    number = len(chunks)
    buffers = (
        [pltpu.VMEM((across, line) + s, bf16) for s in shapes]
        + [pltpu.VMEM((replicas - 1, across - 1, line) + s, bf16) for s in cuts]
        + [pltpu.VMEM((across - 1, line) + s, bf16) for s in cuts]
        + [pltpu.VMEM((2, line) + s, bf16) for s in shapes]
        + [pltpu.VMEM((replicas,) + s, bf16) for s in shapes]
        + [pltpu.VMEM((replicas,) + e.shape, bf16) for e in extras]
    )
    return pl.pallas_call(
        functools.partial(scatter_kernel, replicas, shards, count, chunks, extra),
        name="scatter",
        out_shape=[jax.ShapeDtypeStruct(s, f32) for s in shapes] + [jax.ShapeDtypeStruct(e.shape, f32) for e in extras],
        in_specs=[vmem] * (count + extra),
        out_specs=[vmem] * (count + extra),
        scratch_shapes=buffers + [
            dma((number, across)), dma((number, across)),
            dma((number, replicas, across)), dma((number, replicas, across)),
            dma((number, across)), dma((number, across)),
            dma((number, 2, line)), dma((number, 2, line)),
            dma((number + extra, replicas)), dma((number + extra, replicas)),
        ],
        compiler_params=pltpu.CompilerParams(collective_id=collective_id, has_side_effects=True, vmem_limit_bytes=62 << 20),
        cost_estimate=pl.CostEstimate(flops=0, bytes_accessed=moved * 4, transcendentals=0),
    )(*[a.reshape((line, across, cores) + a.shape[1:]) for a in arrays], *extras)


FIRST_VECTOR = 34
VMEM_ALL = 62 << 20


def place_of(rows):
    return lax.broadcasted_iota(jnp.int32, (rows, 2 * rows), 1) - 2 * lax.broadcasted_iota(jnp.int32, (rows, 2 * rows), 0)


def mixing(own, rest):
    place = place_of(own.shape[0])
    return jnp.where(place == 0, own, jnp.where(place == 1, rest, 0.0)).astype(bf16)


def project_kernel(
    tokens_ref, hot_ref, weight_ref, small_ref,
    pooled_ref, content_ref, position_ref, ordering_ref, key_ref, value_ref, document_ref, mix_ref,
):
    width = tokens_ref.shape[1]
    rows = pooled_ref.shape[0]
    tokens = tokens_ref[...]
    place = place_of(rows)
    first, second = (nn(jnp.where(place == j, 1.0, 0.0).astype(bf16), hot_ref[...]) for j in range(2))
    document_ref[...] = first.astype(bf16)
    own = 1.0 / (1.0 + jnp.sum(first * second, axis=1, keepdims=True))
    mix_ref[...] = jnp.broadcast_to(own, mix_ref.shape)
    pooled = nn(mixing(own, 1.0 - own), tokens)
    pooled_ref[...] = pooled
    key_ref[...] = nn(tokens, weight_ref[:, width : 2 * width]).astype(bf16)
    value_ref[...] = nn(tokens, weight_ref[:, 2 * width :]).astype(bf16)
    queries = nn(pooled.astype(bf16), weight_ref[:, :width])
    bias = small_ref[2:5, :].astype(f32)
    content_ref[...] = ((queries + bias[0:1]) * (0.125 * LOG2E)).astype(bf16)
    position_ref[...] = (queries + bias[1:2]).astype(bf16)
    ordering_ref[...] = (queries + bias[2:3]).astype(bf16)


def project(tokens, hot, weight, small):
    length, width = tokens.shape
    block = 256
    steps = length // block
    whole = lambda n: pl.BlockSpec((block, n), lambda i: (i, 0))
    half = lambda n: pl.BlockSpec((block // 2, n), lambda i: (i, 0))
    rows = jax.ShapeDtypeStruct((length // 2, width), bf16)
    full = jax.ShapeDtypeStruct((length, width), bf16)
    narrow = lambda kind: jax.ShapeDtypeStruct((length // 2, 128), kind)
    return pl.pallas_call(
        project_kernel,
        name="project",
        grid=(steps,),
        out_shape=(jax.ShapeDtypeStruct((length // 2, width), f32), rows, rows, rows, full, full, narrow(bf16), narrow(f32)),
        in_specs=[whole(width), whole(128), fixed(*weight.shape), fixed(*small.shape)],
        out_specs=[half(width)] * 4 + [whole(width)] * 2 + [half(128)] * 2,
        compiler_params=pltpu.CompilerParams(vmem_limit_bytes=VMEM_ALL),
        cost_estimate=pl.CostEstimate(flops=5 * length * width * width, bytes_accessed=10 * length * width, transcendentals=0),
    )(tokens, hot, weight, small)


def mean(values):
    return jnp.mean(values, axis=1, keepdims=True)


def normalize(values):
    centered = values - mean(values)
    inverse = lax.rsqrt(mean(centered * centered) + 1e-05)
    return centered * inverse, inverse


def norm_back(grad, normed, inverse):
    return inverse * (grad - mean(grad) - normed * mean(grad * normed))


def column_sum(values):
    return jnp.sum(values, axis=0, keepdims=True)


def middle_kernel(
    blocks, context_ref, pooled_ref, cotangent_ref, wide_ref, outer_ref, small_ref, bias_ref,
    layer_ref, sum_ref, context_grad_ref, sums_ref, inner_sums_ref, output_out, inner_out, outer_out,
    act, back, slope, first_all, outer_all, attended_all, context_all,
):
    step = pl.program_id(0)
    size, width = pooled_ref.shape
    hidden = bias_ref.shape[1]
    chunks = [slice(c * width, (c + 1) * width) for c in range(hidden // width)]

    @pl.when(step == 0)
    def _():
        sums_ref[...] = jnp.zeros(sums_ref.shape, f32)
        inner_sums_ref[...] = jnp.zeros(inner_sums_ref.shape, f32)

    @pl.when(step < blocks)
    def _():
        rows = pl.ds(pl.multiple_of(step * size, size), size)

        def vector(j):
            return small_ref[2 + j : 3 + j, :].astype(f32)

        context = context_ref[...]
        context_all[rows, :] = context
        first_norm, first_inverse = normalize(pooled_ref[...] + nn(context, wide_ref[:, :width]))
        first = first_norm * vector(3) + vector(4)
        first_low = first.astype(bf16)
        first_all[rows, :] = first_low
        outer = None
        for cut in chunks:
            inner = nn(first_low, wide_ref[:, width + cut.start : width + cut.stop]) + bias_ref[:, cut].astype(f32)
            cumulative = 0.5 * (1.0 + lax.erf(inner * math.sqrt(0.5)))
            act_low = (inner * cumulative).astype(bf16)
            act[rows, cut] = act_low
            slope[:, cut] = cumulative + inner * (jnp.exp(-0.5 * inner * inner) * (1.0 / math.sqrt(2.0 * math.pi)))
            part = nn(act_low, outer_ref[cut, :])
            outer = part if outer is None else outer + part
        second_norm, second_inverse = normalize(first + outer + vector(5))
        layer_ref[...] = (second_norm * vector(6) + vector(7)).astype(bf16)
        cotangent = cotangent_ref[...].astype(f32)
        mid_grad = norm_back(cotangent * vector(6), second_norm, second_inverse)
        outer_low = mid_grad.astype(bf16)
        outer_all[rows, :] = outer_low
        first_grad = mid_grad
        for cut in chunks:
            inner_grad = nt(outer_low, outer_ref[cut, :]) * slope[:, cut]
            inner_low = inner_grad.astype(bf16)
            back[rows, cut] = inner_low
            inner_sums_ref[0:1, cut] += column_sum(inner_low.astype(f32))
            first_grad = first_grad + nt(inner_low, wide_ref[:, width + cut.start : width + cut.stop])
        sum_grad = norm_back(first_grad * vector(3), first_norm, first_inverse)
        sum_ref[...] = sum_grad
        attended_low = sum_grad.astype(bf16)
        attended_all[rows, :] = attended_low
        context_grad_ref[...] = nt(attended_low, wide_ref[:, :width]).astype(bf16)
        for j, term in enumerate(
            (first_grad * first_norm, first_grad, outer_low.astype(f32), cotangent * second_norm, cotangent)
        ):
            sums_ref[j : j + 1, :] += column_sum(term)

    @pl.when((step >= blocks) & (step < blocks + len(chunks)))
    def _():
        cut = pl.ds(pl.multiple_of((step - blocks) * width, width), width)
        outer_out[...] = tn(act[:, cut], outer_all[...]).astype(bf16)
        inner_out[...] = tn(first_all[...], back[:, cut]).astype(bf16)

    @pl.when(step == blocks + len(chunks))
    def _():
        output_out[...] = tn(context_all[...], attended_all[...]).astype(bf16)


def middle(context, pooled, cotangent, wide, outer, small, bias):
    rows, width = context.shape
    hidden = bias.shape[1]
    size = 256
    blocks, chunks = rows // size, hidden // width
    block = pl.BlockSpec((size, width), lambda i: (jnp.minimum(i, blocks - 1), 0))
    chunk = lambda i: jnp.clip(i - blocks, 0, chunks - 1)
    low = jax.ShapeDtypeStruct((rows, width), bf16)
    flops = 18 * rows * width * hidden
    return pl.pallas_call(
        functools.partial(middle_kernel, blocks),
        name="middle",
        grid=(blocks + chunks + 1,),
        out_shape=(
            low,
            jax.ShapeDtypeStruct((rows, width), f32),
            low,
            jax.ShapeDtypeStruct((8, width), f32),
            jax.ShapeDtypeStruct((8, hidden), f32),
            jax.ShapeDtypeStruct((width, width), bf16),
            jax.ShapeDtypeStruct((width, hidden), bf16),
            jax.ShapeDtypeStruct((hidden, width), bf16),
        ),
        in_specs=[block, block, block, fixed(*wide.shape), fixed(*outer.shape), fixed(*small.shape), fixed(*bias.shape)],
        out_specs=[
            block, block, block, fixed(8, width), fixed(8, hidden), fixed(width, width),
            pl.BlockSpec((width, width), lambda i: (0, chunk(i))),
            pl.BlockSpec((width, width), lambda i: (chunk(i), 0)),
        ],
        scratch_shapes=[
            pltpu.VMEM((rows, hidden), bf16),
            pltpu.VMEM((rows, hidden), bf16),
            pltpu.VMEM((size, hidden), f32),
            pltpu.VMEM((rows, width), bf16),
            pltpu.VMEM((rows, width), bf16),
            pltpu.VMEM((rows, width), bf16),
            pltpu.VMEM((rows, width), bf16),
        ],
        compiler_params=pltpu.CompilerParams(vmem_limit_bytes=60 << 20),
        cost_estimate=pl.CostEstimate(flops=flops, bytes_accessed=40 * rows * width, transcendentals=2 * rows * hidden),
    )(context, pooled, cotangent, wide, outer, small, bias)


def tail_kernel(
    tokens_ref, key_ref, value_ref, query_ref, sum_ref, pooled_ref, mix_ref, weight_ref,
    tokens_grad_ref, weight_grad_ref, total,
):
    step = pl.program_id(0)
    width = tokens_ref.shape[1]

    @pl.when(step == 0)
    def _():
        total[...] = jnp.zeros(total.shape, f32)

    tokens, query_low, key_low, value_low = tokens_ref[...], query_ref[...], key_ref[...], value_ref[...]
    pooled_grad = sum_ref[...] + nt(query_low, weight_ref[:, :width])
    coarse = pooled_grad.astype(bf16)
    fine = (pooled_grad - coarse.astype(f32)).astype(bf16)
    own = mix_ref[:, :1]
    mix = mixing(own, 1.0 - own)
    tokens_grad_ref[...] = (
        tn(mix, coarse) + tn(mix, fine)
        + nt(key_low, weight_ref[:, width : 2 * width])
        + nt(value_low, weight_ref[:, 2 * width :])
    )
    total[:, :width] += tn(pooled_ref[...].astype(bf16), query_low)
    total[:, width : 2 * width] += tn(tokens, key_low)
    total[:, 2 * width :] += tn(tokens, value_low)

    @pl.when(step == pl.num_programs(0) - 1)
    def _():
        weight_grad_ref[...] = total[...].astype(bf16)


def tail(tokens, key_low, value_low, query_low, sum_grad, pooled, mix, weight):
    length, width = tokens.shape
    block = 256
    whole = pl.BlockSpec((block, width), lambda i: (i, 0))
    half = pl.BlockSpec((block // 2, width), lambda i: (i, 0))
    return pl.pallas_call(
        tail_kernel,
        name="tail",
        grid=(length // block,),
        out_shape=(jax.ShapeDtypeStruct((length, width), f32), jax.ShapeDtypeStruct((width, 3 * width), bf16)),
        in_specs=[whole, whole, whole, half, half, half, pl.BlockSpec((block // 2, 128), lambda i: (i, 0)), fixed(*weight.shape)],
        out_specs=[whole, fixed(width, 3 * width)],
        scratch_shapes=[pltpu.VMEM((width, 3 * width), f32)],
        compiler_params=pltpu.CompilerParams(vmem_limit_bytes=VMEM_ALL),
        cost_estimate=pl.CostEstimate(flops=10 * length * width * width, bytes_accessed=16 * length * width, transcendentals=0),
    )(tokens, key_low, value_low, query_low, sum_grad, pooled, mix, weight)


def pack_kernel(count, folds, *refs):
    output_ref, inner_ref, relative_ref, order_ref = refs[:4]
    vectors, bias_ref = refs[4 : 4 + count], refs[4 + count]
    wide_ref, small_ref = refs[5 + count :]
    width = output_ref.shape[1]
    each = relative_ref.shape[1]
    wide_ref[:, :width] = output_ref[...]
    wide_ref[:, width:] = inner_ref[...]
    small_ref[...] = jnp.zeros(small_ref.shape, bf16)
    rows = [relative_ref[...].astype(f32), order_ref[...].astype(f32)]
    rows += [ref[...].astype(f32).reshape(1, each) for ref in vectors]
    bias = bias_ref[...].astype(f32).reshape(1, folds * each)
    rows += [bias[:, j * each : (j + 1) * each] for j in range(folds)]
    small_ref[: FIRST_VECTOR + count + folds, :each] = jnp.concatenate(rows, 0).astype(bf16)


def pack(output, inner, relative, order, vectors, bias, folds):
    rows = -(-(FIRST_VECTOR + len(vectors) + folds) // 16) * 16
    return pl.pallas_call(
        functools.partial(pack_kernel, len(vectors), folds),
        name="pack",
        out_shape=(
            jax.ShapeDtypeStruct((output.shape[0], output.shape[1] + inner.shape[1]), bf16),
            jax.ShapeDtypeStruct((rows, 128), bf16),
        ),
        cost_estimate=pl.CostEstimate(flops=0, bytes_accessed=4 * inner.size, transcendentals=0),
    )(output, inner, relative, order, *vectors, bias)


def finish_kernel(count, folds, projection_ref, output_ref, inner_ref, outer_ref, small_ref, *outs):
    width = output_ref.shape[1]
    squares, (output_out, inner_out, outer_out, relative_out, order_out) = outs[:3], outs[3:8]
    vectors, bias_out = outs[8 : 8 + count], outs[8 + count]
    each = relative_out.shape[1]
    for j, ref in enumerate(squares):
        ref[...] = projection_ref[:, j * width : (j + 1) * width]
    output_out[...] = output_ref[...]
    inner_out[...] = inner_ref[...]
    outer_out[...] = outer_ref[...]
    small = small_ref[...]
    relative_out[...] = small[:32, :each]
    order_out[...] = small[32:34, :each]
    for j, ref in enumerate(vectors):
        ref[...] = small[FIRST_VECTOR + j, :each]
    start = FIRST_VECTOR + count
    bias_out[...] = jnp.concatenate([small[start + j : start + j + 1, :each] for j in range(folds)], 1).reshape(folds * each)


def finish(projection, output, inner, outer, small, count, folds):
    each, width = small.shape[0], output.shape[1]
    rows = output.shape[0]
    shape = lambda *s: jax.ShapeDtypeStruct(s, f32)
    return pl.pallas_call(
        functools.partial(finish_kernel, count, folds),
        name="finish",
        out_shape=(
            [shape(rows, width)] * 4 + [shape(*inner.shape), shape(*outer.shape), shape(32, rows), shape(2, rows)]
            + [shape(rows)] * count + [shape(folds * rows)]
        ),
        cost_estimate=pl.CostEstimate(flops=0, bytes_accessed=8 * inner.size, transcendentals=0),
    )(projection, output, inner, outer, small)


def unpack_kernel(shards, folds, start, small_ref, segment_ref, relative_out, order_out, vectors_out, bias_out, hot_out, away_out):
    each = relative_out.shape[1] // shards
    length = segment_ref.shape[1]
    own = [small_ref[s].astype(f32) for s in range(shards)]
    whole = jnp.concatenate([piece[:start, :each] for piece in own], 1).astype(bf16)
    relative_out[...] = whole[:32]
    order_out[...] = whole[32:34]
    vectors_out[: start - 32, :] = whole[32:]
    bias_out[...] = jnp.concatenate(
        [piece[start + j : start + j + 1, :each] for piece in own for j in range(folds)], 1
    ).astype(bf16)
    document = lax.broadcasted_iota(jnp.int32, (128, length), 0)
    same = jnp.where(segment_ref[...] == document, 1.0, 0.0).T
    counted = lax.broadcasted_iota(jnp.int32, same.shape, 1) < 8
    hot_out[...] = same.astype(bf16)
    away_out[256 : 256 + length, :] = jnp.where(counted, -BIG * (1.0 - same), 0.0).astype(bf16)
    pad = jnp.where(counted[:256], -BIG, 0.0).astype(bf16)
    away_out[:256, :] = pad
    away_out[256 + length :, :] = pad


def unpack(small, segments, width, count, folds):
    shards = small.shape[0]
    length = segments.shape[1]
    start = FIRST_VECTOR + count
    shape = lambda *s: jax.ShapeDtypeStruct(s, bf16)
    return pl.pallas_call(
        functools.partial(unpack_kernel, shards, folds, start),
        name="unpack",
        out_shape=(shape(32, width), shape(2, width), shape(16, width), shape(1, folds * width), shape(length, 128), shape(length + 512, 128)),
        compiler_params=pltpu.CompilerParams(vmem_limit_bytes=VMEM_ALL),
        cost_estimate=pl.CostEstimate(flops=0, bytes_accessed=1 << 20, transcendentals=0),
    )(small, segments)


def collect_kernel(folds, relative_ref, order_ref, bias_ref, sums_ref, inner_ref, out_ref):
    shards, rows, _ = out_ref.shape
    width = relative_ref.shape[1]
    each = width // shards
    whole = jnp.concatenate([relative_ref[...], order_ref[:2], bias_ref[:3], sums_ref[:5]], 0)
    inner = inner_ref[0:1, :]
    out_ref[...] = jnp.zeros(out_ref.shape, bf16)
    for s in range(shards):
        cut = slice(s * each, s * each + each)
        own = [inner[:, (s * folds + j) * each : (s * folds + j + 1) * each] for j in range(folds)]
        piece = jnp.concatenate([whole[:, cut], *own], 0)
        out_ref[s, : piece.shape[0], :each] = piece.astype(bf16)


def collect(relative, order, bias, sums, inner, shards, count, folds):
    rows = -(-(FIRST_VECTOR + count + folds) // 16) * 16
    return pl.pallas_call(
        functools.partial(collect_kernel, folds),
        name="collect",
        out_shape=jax.ShapeDtypeStruct((shards, rows, 128), bf16),
        compiler_params=pltpu.CompilerParams(vmem_limit_bytes=VMEM_ALL),
        cost_estimate=pl.CostEstimate(flops=0, bytes_accessed=1 << 19, transcendentals=0),
    )(relative, order, bias, sums, inner)


def body(
    mesh,
    tokens,
    segment_ids,
    query_weight,
    key_weight,
    value_weight,
    output_weight,
    relative_table,
    order_table,
    content_bias,
    position_bias,
    order_bias,
    first_gain,
    first_shift,
    inner_weight,
    inner_bias,
    outer_weight,
    outer_bias,
    second_gain,
    second_shift,
    cotangent,
):
    shards = mesh.shape["shard"]
    width = tokens.shape[1]
    hidden = inner_weight.shape[1]
    each = width // shards
    folds = hidden // width
    vectors = (content_bias, position_bias, order_bias, first_gain, first_shift, outer_bias, second_gain, second_shift)
    wide_own, small = pack(output_weight, inner_weight, relative_table, order_table, vectors, inner_bias, folds)
    projections, small_all = gather(mesh, [jnp.concatenate([query_weight, key_weight, value_weight], 1), small], 0)
    projections = projections.reshape(width, 3 * width)
    weight_relative, weight_order, small_all, bias_inner, hot, away = unpack(small_all, segment_ids, width, len(vectors), folds)
    wide = lax.all_gather(wide_own, "shard", axis=0, tiled=True)
    weight_outer = lax.all_gather(outer_weight, "shard", axis=0, tiled=True)

    behind, ahead = ranges(segment_ids)
    pooled, content, position, ordering, keys, values, document, mix = project(tokens, hot, projections, small_all)
    probs, context, mixed, inverse = attend(
        behind, ahead, content, position, ordering, keys, values, weight_relative, weight_order, away, document
    )
    layer_out, sum_grad, context_grad, sums, inner_sums, output_grad, inner_grad, outer_grad = middle(
        context, pooled, cotangent, wide, weight_outer, small_all, bias_inner
    )
    query_low, key_low, value_low, relative_grad, order_grad, bias_sums = attend_back(
        behind, ahead, probs, context_grad, mixed, inverse, content, position, ordering,
        keys, values, weight_relative, weight_order,
    )
    tokens_grad, projection_grad = tail(tokens, key_low, value_low, query_low, sum_grad, pooled, mix, projections)
    small_grad = collect(relative_grad, order_grad, bias_sums, sums, inner_sums, shards, len(vectors), folds)
    outer_part = lax.psum_scatter(outer_grad, "shard", scatter_dimension=0, tiled=True)
    inner_sum, output_sum, projection_sum, small_sum, outer_sum = scatter(
        mesh,
        [
            inner_grad.reshape(shards, each, hidden),
            output_grad.reshape(shards, each, width),
            projection_grad.reshape(shards, each, 3 * width),
            small_grad,
        ],
        [width, width, width, 128],
        [outer_part],
        1,
    )
    parts = finish(projection_sum, output_sum, inner_sum, outer_sum, small_sum, len(vectors), folds)
    squares, (inner_sum, outer_sum, relative_sum, order_sum) = parts[:4], parts[4:8]
    own, bias_sum = parts[8:-1], parts[-1]
    return (
        layer_out, tokens_grad, *squares, relative_sum, order_sum, *own[:5],
        inner_sum, bias_sum, outer_sum, *own[5:],
    )


def solution(mesh):
    placed = (
        P(("rep", "shard"), None),
        P(("rep", "shard"), None),
        P("shard", None),
        P("shard", None),
        P("shard", None),
        P("shard", None),
        P(None, "shard"),
        P(None, "shard"),
        P("shard"),
        P("shard"),
        P("shard"),
        P("shard"),
        P("shard"),
        P("shard", None),
        P("shard"),
        P("shard", None),
        P("shard"),
        P("shard"),
        P("shard"),
        P(("rep", "shard"), None),
    )
    return jax.shard_map(
        functools.partial(body, mesh),
        mesh=mesh,
        in_specs=placed,
        out_specs=(
            P(("rep", "shard"), None),
            P(("rep", "shard"), None),
            P("shard", None),
            P("shard", None),
            P("shard", None),
            P("shard", None),
            P(None, "shard"),
            P(None, "shard"),
            P("shard"),
            P("shard"),
            P("shard"),
            P("shard"),
            P("shard"),
            P("shard", None),
            P("shard"),
            P("shard", None),
            P("shard"),
            P("shard"),
            P("shard"),
        ),
        check_vma=False,
    )
```

```python
import functools
import math

import jax
import jax.numpy as jnp
import numpy as np
from jax import lax
from jax.experimental import pallas as pl
from jax.experimental.pallas import tpu as pltpu
from jax.sharding import PartitionSpec as P

LIMITS = (1, 2, 3, 4, 5, 6, 7, 8, 12, 16, 24, 32, 48, 64, 128)
BQ = 128
NEAR = 640
CHUNK = 256
LOG2E = math.log2(math.e)
LN2 = math.log(2.0)
BIG = 1e30
f32 = jnp.float32
bf16 = jnp.bfloat16


def bucket_of(offset):
    distance = np.abs(offset)
    passed = sum((distance >= limit).astype(np.int32) for limit in LIMITS)
    return np.where(offset < 0, 15 + passed + (distance >= 256), passed).astype(np.int32)


def near_index():
    row = np.arange(BQ)[None, :, None]
    tile = np.arange(-2, 3)[:, None, None]
    lane = np.arange(128)[None, None, :]
    return bucket_of(128 * tile + lane - 2 * row)


def bucket_onehot():
    out = np.zeros((4 * 128, 128), np.float32)
    offsets = np.concatenate([np.arange(-256, 128), np.full(64, -300), np.full(64, 300)])
    out[np.arange(512), bucket_of(offsets)] = 1
    out[:, 32] = offsets >= 0
    out[:, 33] = offsets < 0
    return out


def nt(left, right):
    return lax.dot_general(left, right, (((1,), (1,)), ((), ())), preferred_element_type=f32)


def nn(left, right):
    return lax.dot_general(left, right, (((1,), (0,)), ((), ())), preferred_element_type=f32)


def tn(left, right):
    return lax.dot_general(left, right, (((0,), (0,)), ((), ())), preferred_element_type=f32)


def halves(array):
    low = lax.broadcasted_iota(jnp.int32, array.shape, 1) < 64
    zero = jnp.zeros_like(array)
    return jnp.where(low, array, zero), jnp.where(low, zero, array)


def pick(array):
    half = array.shape[0] // 2
    low = lax.broadcasted_iota(jnp.int32, (half, 128), 1) < 64
    return jnp.where(low, array[:half], array[half:])


def take(table, index):
    numbers = lax.GatherDimensionNumbers(
        offset_dims=(), collapsed_slice_dims=(1,), start_index_map=(1,),
        operand_batching_dims=(0,), start_indices_batching_dims=(0,),
    )
    return lax.gather(table, index[:, :, None], numbers, (1, 1), mode=lax.GatherScatterMode.PROMISE_IN_BOUNDS)


def lanes_of(p):
    return slice(128 * p, 128 * p + 128)


def far_start(chunk, behind, far, near):
    start = jnp.where(chunk < behind, near - CHUNK * (chunk + 1), near + NEAR + CHUNK * (chunk - behind))
    return pl.multiple_of(jnp.where(chunk < far, start, 0), 128)


def forward_kernel(
    group, behind_ref, ahead_ref, content_ref, position_ref, ordering_ref, key_ref, value_ref,
    relative_ref, order_ref, away_ref, document_ref, index_ref,
    probs_ref, context_ref, mixed_ref, inverse_ref,
    keys, values, table, bias, scores, peak, total,
):
    step = pl.program_id(1)
    length = key_ref.shape[0]

    @pl.when((step == 0) & (pl.program_id(0) == 0))
    def _():
        for p in range(group):
            for scratch in (keys, values):
                scratch[p, :256, :128] = jnp.zeros((256, 128), bf16)
                scratch[p, 256 + length :, :128] = jnp.zeros((256, 128), bf16)
            keys[p, :, 128:] = away_ref[...]
            values[p, :, 128:] = jnp.ones((length + 512, 128), bf16)

    @pl.when(step == 0)
    def _():
        after = lax.broadcasted_iota(jnp.int32, (32, 128), 0) < 16
        table[...] = jnp.zeros(table.shape, bf16)
        for p in range(group):
            lanes = lanes_of(p)
            keys[p, 256 : 256 + length, :128] = key_ref[:, lanes]
            values[p, 256 : 256 + length, :128] = value_ref[:, lanes]
            orders = jnp.where(after, order_ref[0:1, lanes].astype(f32), order_ref[1:2, lanes].astype(f32)).astype(bf16)
            for half, (relative, order) in enumerate(zip(halves(relative_ref[:, lanes]), halves(orders))):
                both = jnp.concatenate([relative, order], 1)
                table[p, 128 * half : 128 * half + 32, :] = both
                for side, bucket in ((0, 31), (1, 15)):
                    start = 256 + 256 * side + 128 * half
                    table[p, start : start + 128, :] = jnp.broadcast_to(both[bucket : bucket + 1].astype(f32), (128, 256)).astype(bf16)

    document = document_ref[...]
    near = pl.multiple_of(step * 256, 256)
    queries = []
    for p in range(group):
        even, odd = halves(content_ref[:, lanes_of(p)])
        queries.append(jnp.concatenate(
            [jnp.concatenate([even, document], 1), jnp.concatenate([odd, document], 1)], 0
        ))
    for p in range(group):
        lanes = lanes_of(p)
        places = nt(jnp.concatenate([position_ref[:, lanes], ordering_ref[:, lanes]], 1), table[p]) * (0.125 * LOG2E)
        place = (places[:, :128], places[:, 128:256])
        near_scores = nt(queries[p], keys[p, pl.ds(near, NEAR), :])
        for half in range(2):
            rows = slice(BQ * half, BQ * half + BQ)
            for side in range(2):
                start = 256 + 256 * side + 128 * half
                bias[p, rows, 128 * side : 128 * side + 128] = places[:, start : start + 128]
            for quarter in range(2):
                own = slice(64 * quarter, 64 * quarter + 64)
                rows = slice(BQ * half + 64 * quarter, BQ * half + 64 * quarter + 64)
                best = None
                for tile in range(NEAR // 128):
                    if tile == 4 - 4 * quarter:
                        extra = bias[p, rows, 128 - 128 * quarter : 256 - 128 * quarter]
                    else:
                        extra = take(place[half][own], index_ref[tile, own])
                    part = near_scores[rows, 128 * tile : 128 * tile + 128] + extra
                    scores[p, rows, pl.ds(near + 128 * tile, 128)] = part
                    best = part if best is None else jnp.maximum(best, part)
                peak[p, rows, :] = best
    behind = behind_ref[step, 0]
    far = behind + ahead_ref[step, 0]

    def start_of(chunk):
        return far_start(chunk, behind, far, near)

    @pl.loop(0, (far + 1) // 2)
    def _(two):
        for chunk in (2 * two, 2 * two + 1):
            start = start_of(chunk)
            place = pl.multiple_of(jnp.where(chunk < behind, 0, 128), 128)
            for p in range(group):
                part = nt(queries[p], keys[p, pl.ds(start, CHUNK), :])
                extra = bias[p, :, pl.ds(place, 128)]
                left, right = part[:, :128] + extra, part[:, 128:] + extra
                scores[p, :, pl.ds(start, 128)] = left
                scores[p, :, pl.ds(start + 128, 128)] = right
                peak[p] = jnp.maximum(peak[p], jnp.maximum(left, right))

    tops = [jnp.max(peak[p], axis=1, keepdims=True) for p in range(group)]
    for p in range(group):
        peak[p] = jnp.broadcast_to(tops[p], (2 * BQ, 128))
        probs = jnp.exp2(scores[p, :, pl.ds(near, NEAR)] - tops[p]).astype(bf16)
        probs_ref[p, 0, :, pl.ds(near, NEAR)] = probs
        total[p] = nn(probs, values[p, pl.ds(near, NEAR), :])

    @pl.loop(0, (far + 1) // 2)
    def _(two):
        starts = [start_of(2 * two), start_of(2 * two + 1)]
        for p in range(group):
            top = peak[p]
            parts = []
            for start in starts:
                left = jnp.exp2(scores[p, :, pl.ds(start, 128)] - top).astype(bf16)
                right = jnp.exp2(scores[p, :, pl.ds(start + 128, 128)] - top).astype(bf16)
                probs = jnp.concatenate([left, right], 1)
                probs_ref[p, 0, :, pl.ds(start, CHUNK)] = probs
                parts.append(nn(probs, values[p, pl.ds(start, CHUNK), :]))
            total[p] += parts[0] + parts[1]

    for p in range(group):
        lanes = lanes_of(p)
        inverse = 1.0 / total[p, :, 128:]
        mixed = pick(total[p, :, :128] * inverse)
        inverse_ref[:, lanes] = pick(inverse)
        mixed_ref[:, lanes] = mixed
        context_ref[:, lanes] = mixed.astype(bf16)


def backward_kernel(
    group, behind_ref, ahead_ref, probs_ref, grad_ref, mixed_ref, inverse_ref, content_ref, position_ref, ordering_ref,
    key_ref, value_ref, relative_ref, order_ref, turn_ref, onehot_ref,
    query_ref, key_low_ref, value_low_ref, relative_out, order_out, sums_out,
    keys, values, table, key_total, value_total, query_total, far_total, bucket, table_total, sums,
):
    step = pl.program_id(1)
    length = key_ref.shape[0]

    @pl.when(step == 0)
    def _():
        slot = lax.broadcasted_iota(jnp.int32, (32, 128), 0)
        table[...] = jnp.zeros(table.shape, bf16)
        for p in range(group):
            lanes = lanes_of(p)
            for scratch, ref in ((keys, key_ref), (values, value_ref)):
                scratch[p, :256, :] = jnp.zeros((256, 128), bf16)
                scratch[p, 256 + length :, :] = jnp.zeros((256, 128), bf16)
                scratch[p, 256 : 256 + length, :] = ref[:, lanes]
            even, odd = halves(relative_ref[:, lanes])
            table[p, 0:32, :128] = even
            table[p, 128:160, :128] = odd
            orders = jnp.where(slot == 0, order_ref[0:1, lanes].astype(f32), order_ref[1:2, lanes].astype(f32))
            even, odd = halves(jnp.where(slot < 2, orders, 0.0))
            table[p, 32:64, 128:] = even.astype(bf16)
            table[p, 160:192, 128:] = odd.astype(bf16)
        key_total[...] = jnp.zeros(key_total.shape, f32)
        value_total[...] = jnp.zeros(value_total.shape, f32)
        table_total[...] = jnp.zeros(table_total.shape, f32)
        sums[...] = jnp.zeros(sums.shape, f32)

    near = pl.multiple_of(step * 256, 256)
    grads, grads_t, content_t, deltas = [], [], [], []
    for p in range(group):
        lanes = lanes_of(p)
        scaled = (grad_ref[:, lanes].astype(f32) * inverse_ref[:, lanes]).astype(bf16)
        both = jnp.concatenate(halves(scaled), 0)
        even, odd = halves(scaled.astype(f32) * mixed_ref[:, lanes])
        deltas.append(jnp.concatenate(
            [jnp.sum(even, axis=1, keepdims=True), jnp.sum(odd, axis=1, keepdims=True)], 0
        ))
        grads.append(both)
        grads_t.append(both.T)
        content_t.append(jnp.concatenate(halves(content_ref[:, lanes]), 0).T)

    def visit(p, start, size):
        probs = probs_ref[p, 0, :, pl.ds(start, size)]
        prob_grad = nt(grads[p], values[p, pl.ds(start, size), :])
        score = probs.astype(f32) * (prob_grad - deltas[p])
        score_low = score.astype(bf16)
        value_total[p, :, pl.ds(start, size)] += nn(grads_t[p], probs)
        key_total[p, :, pl.ds(start, size)] += nn(content_t[p], score_low)
        return score, nn(score_low, keys[p, pl.ds(start, size), :])

    turn = turn_ref[...]
    turns = jnp.concatenate([turn, turn], 0)
    lane = lax.broadcasted_iota(jnp.int32, (64, 128), 1)
    row = lax.broadcasted_iota(jnp.int32, (64, 128), 0)
    first = lane + 2 * row < 128
    zero = jnp.zeros((64, 128), f32)
    for p in range(group):
        score, query_total[p] = visit(p, near, NEAR)
        parts = [score[:, 128 * t : 128 * t + 128] for t in range(5)]
        tiles = [take(part, turns) for part in parts]
        for quarter in range(4):
            rows = slice(64 * quarter, 64 * quarter + 64)
            own = [tile[rows] for tile in tiles]
            if quarter % 2 == 0:
                near_parts = [jnp.where(first, own[t], own[t + 1]) for t in range(3)]
                far_total[p, 0, rows] = jnp.where(first, zero, own[0])
                far_total[p, 1, rows] = jnp.where(first, own[3], zero) + parts[4][rows]
            else:
                near_parts = [jnp.where(first, own[t + 1], own[t + 2]) for t in range(3)]
                far_total[p, 0, rows] = parts[0][rows] + jnp.where(first, zero, own[1])
                far_total[p, 1, rows] = jnp.where(first, own[4], zero)
            for t in range(3):
                bucket[p, rows, 128 * t : 128 * t + 128] = near_parts[t].astype(bf16)
    behind = behind_ref[step, 0]

    far = behind + ahead_ref[step, 0]

    @pl.loop(0, (far + 1) // 2)
    def _(two):
        for chunk in (2 * two, 2 * two + 1):
            start = far_start(chunk, behind, far, near)
            side = jnp.where(chunk < behind, 0, 1)
            for p in range(group):
                score, part = visit(p, start, CHUNK)
                query_total[p] += part
                far_total[p, side] += score[:, :128] + score[:, 128:]

    for p in range(group):
        lanes = lanes_of(p)
        folded = [far_total[p, side] + pltpu.roll(far_total[p, side], 64, 1) for side in range(2)]
        low_lane = lax.broadcasted_iota(jnp.int32, folded[0].shape, 1) < 64
        bucket[p, :, 384:] = jnp.where(low_lane, *folded).astype(bf16)
        low = (nn(bucket[p], onehot_ref[...]) * 0.125).astype(bf16)
        low = jnp.concatenate([low[:BQ], low[BQ:]], 1)
        placed = nn(low, table[p])
        content_grad = pick(query_total[p]) * 0.125
        query_ref[:, lanes] = (content_grad + placed[:, :128] + placed[:, 128:]).astype(bf16)
        table_total[p] += tn(low, jnp.concatenate([position_ref[:, lanes], ordering_ref[:, lanes]], 1))
        for j, term in enumerate((content_grad, placed[:, :128], placed[:, 128:])):
            sums[j : j + 1, lanes] += jnp.sum(term, axis=0, keepdims=True)

    @pl.when(step == pl.num_programs(1) - 1)
    def _():
        low_lane = lax.broadcasted_iota(jnp.int32, (32, 128), 1) < 64
        for p in range(group):
            lanes = lanes_of(p)
            key_low_ref[:, lanes] = (key_total[p, :, 256 : 256 + length] * LN2).T.astype(bf16)
            value_low_ref[:, lanes] = value_total[p, :, 256 : 256 + length].T.astype(bf16)
            relative_out[:, lanes] = jnp.where(low_lane, table_total[p, 0:32, :128], table_total[p, 128:160, :128])
            order_out[:, lanes] = jnp.where(low_lane[:8], table_total[p, 32:40, 128:], table_total[p, 160:168, 128:])
        sums_out[...] = sums[...]


def fixed(*shape):
    return pl.BlockSpec(shape, lambda *_: (0,) * len(shape), pipeline_mode=pl.Buffered(1))


GROUP = 3


def attend(behind, ahead, content, position, ordering, keys, values, relative, order, away, document):
    rows, width = content.shape
    length = keys.shape[0]
    padded = length + 512
    pairs, blocks, group = width // 128, rows // BQ, GROUP
    wide = 128 * group
    tile = pl.BlockSpec((BQ, wide), lambda p, i, *_: (i, p))
    whole = pl.BlockSpec((length, wide), lambda p, i, *_: (0, p), pipeline_mode=pl.Buffered(1))
    return pl.pallas_call(
        functools.partial(forward_kernel, group),
        name="attend",
        out_shape=(
            jax.ShapeDtypeStruct((pairs, blocks, 2 * BQ, padded), bf16),
            jax.ShapeDtypeStruct((rows, width), bf16),
            jax.ShapeDtypeStruct((rows, width), f32),
            jax.ShapeDtypeStruct((rows, width), f32),
        ),
        grid_spec=pltpu.PrefetchScalarGridSpec(
            num_scalar_prefetch=2,
            grid=(pairs // group, blocks),
            in_specs=[
                tile, tile, tile, whole, whole,
                pl.BlockSpec((32, wide), lambda p, i, *_: (0, p)),
                pl.BlockSpec((2, wide), lambda p, i, *_: (0, p)),
                fixed(padded, 128),
                pl.BlockSpec((BQ, 128), lambda p, i, *_: (i, 0)),
                fixed(5, BQ, 128),
            ],
            out_specs=[pl.BlockSpec((group, 1, 2 * BQ, padded), lambda p, i, *_: (p, i, 0, 0)), tile, tile, tile],
            scratch_shapes=[
                pltpu.VMEM((group, padded, 256), bf16),
                pltpu.VMEM((group, padded, 256), bf16),
                pltpu.VMEM((group, 768, 256), bf16),
                pltpu.VMEM((group, 2 * BQ, 256), f32),
                pltpu.VMEM((group, 2 * BQ, padded), f32),
                pltpu.VMEM((group, 2 * BQ, 128), f32),
                pltpu.VMEM((group, 2 * BQ, 256), f32),
            ],
        ),
        compiler_params=pltpu.CompilerParams(dimension_semantics=("arbitrary", "arbitrary"), vmem_limit_bytes=62 << 20),
        cost_estimate=pl.CostEstimate(flops=40 * 10**9, bytes_accessed=70 * 10**6, transcendentals=10**7),
    )(behind, ahead, content, position, ordering, keys, values, relative, order, away, document,
      jnp.asarray(near_index()))


def attend_back(behind, ahead, probs, grad, mixed, inverse, content, position, ordering, keys, values, relative, order):
    rows, width = content.shape
    length = keys.shape[0]
    padded = length + 512
    pairs, blocks, group = width // 128, rows // BQ, GROUP
    wide = 128 * group
    tile = pl.BlockSpec((BQ, wide), lambda p, i, *_: (i, p))
    whole = pl.BlockSpec((length, wide), lambda p, i, *_: (0, p), pipeline_mode=pl.Buffered(1))
    small = lambda n: pl.BlockSpec((n, wide), lambda p, i, *_: (0, p))
    turn = (np.arange(128)[None, :] + 2 * np.arange(BQ)[:, None]) % 128
    return pl.pallas_call(
        functools.partial(backward_kernel, group),
        name="attend_back",
        out_shape=(
            jax.ShapeDtypeStruct((rows, width), bf16),
            jax.ShapeDtypeStruct((length, width), bf16),
            jax.ShapeDtypeStruct((length, width), bf16),
            jax.ShapeDtypeStruct((32, width), f32),
            jax.ShapeDtypeStruct((8, width), f32),
            jax.ShapeDtypeStruct((8, width), f32),
        ),
        grid_spec=pltpu.PrefetchScalarGridSpec(
            num_scalar_prefetch=2,
            grid=(pairs // group, blocks),
            in_specs=[
                pl.BlockSpec((group, 1, 2 * BQ, padded), lambda p, i, *_: (p, i, 0, 0)),
                tile, tile, tile, tile, tile, tile, whole, whole, small(32), small(2), fixed(BQ, 128), fixed(512, 128),
            ],
            out_specs=[tile, whole, whole, small(32), small(8), small(8)],
            scratch_shapes=[
                pltpu.VMEM((group, padded, 128), bf16),
                pltpu.VMEM((group, padded, 128), bf16),
                pltpu.VMEM((group, 256, 256), bf16),
                pltpu.VMEM((group, 128, padded), f32),
                pltpu.VMEM((group, 128, padded), f32),
                pltpu.VMEM((group, 2 * BQ, 128), f32),
                pltpu.VMEM((group, 2, 2 * BQ, 128), f32),
                pltpu.VMEM((group, 2 * BQ, 512), bf16),
                pltpu.VMEM((group, 256, 256), f32),
                pltpu.VMEM((8, wide), f32),
            ],
        ),
        compiler_params=pltpu.CompilerParams(dimension_semantics=("arbitrary", "arbitrary"), vmem_limit_bytes=62 << 20),
        cost_estimate=pl.CostEstimate(flops=80 * 10**9, bytes_accessed=70 * 10**6, transcendentals=0),
    )(behind, ahead, probs, grad, mixed, inverse, content, position, ordering, keys, values, relative, order,
      jnp.asarray(turn, jnp.int32), jnp.asarray(bucket_onehot(), bf16))


MESH = pl.DeviceIdType.MESH


class Place:
    def __init__(self, replicas, shards):
        self.replicas, self.shards = replicas, shards
        self.cores = 2 if shards % 2 == 0 else 1
        chips = shards // self.cores
        self.across = 2 if chips % 2 == 0 else 1
        self.line = chips // self.across
        self.replica = lax.axis_index("rep")
        own = lax.axis_index("shard")
        self.own = own
        self.core = lax.rem(own, self.cores)
        self.column = lax.rem(own // self.cores, self.across)
        self.spot = own // (self.cores * self.across)

    def shard(self, spot, column, core):
        return (spot * self.across + column) * self.cores + core

    def other_column(self, step):
        return lax.rem(self.column + step, self.across)

    def other_replica(self, step):
        return lax.rem(self.replica + step, self.replicas)

    def device(self, spot=None, column=None, core=None, replica=None):
        spot = self.spot if spot is None else spot
        column = self.column if column is None else column
        core = self.core if core is None else core
        replica = self.replica if replica is None else replica
        return (replica, self.shard(spot, column, core))

    def meet(self):
        barrier = pltpu.get_barrier_semaphore()

        def greet(device):
            pl.semaphore_signal(barrier, inc=1, device_id=device, device_id_type=MESH)

        fixed = 0
        if self.cores > 1:
            greet(self.device(core=1 - self.core))
            fixed += 1
        for step in range(1, self.across):
            greet(self.device(column=self.other_column(step)))
            fixed += 1
        for step in range(1, self.replicas):
            greet(self.device(replica=self.other_replica(step)))
            fixed += 1
        for step, there in ((1, self.spot < self.line - 1), (-1, self.spot > 0)):

            @pl.when(there)
            def _():
                greet(self.device(spot=self.spot + step))

        lined = (self.spot < self.line - 1).astype(jnp.int32) + (self.spot > 0).astype(jnp.int32)
        pl.semaphore_wait(barrier, fixed + lined)


def parts_of(columns, replicas):
    return replicas if columns % (128 * replicas) == 0 else 1


def columns_of(part, parts, columns):
    size = columns // parts
    return pl.ds(pl.multiple_of(part * size, 128), size)


def when(condition, action):
    if condition is True:
        action()
    else:
        pl.when(condition)(action)


def gather_kernel(replicas, shards, count, *refs):
    here = Place(replicas, shards)
    sources, wholes = refs[:count], refs[count : 2 * count]
    line_send, line_recv, cross_send, cross_recv, rep_send, rep_recv, core_send, core_recv = refs[2 * count :]
    here.meet()
    pending = []

    def send(source, whole_view, send_sem, recv_sem, device, condition=True):
        copy = pltpu.make_async_remote_copy(
            src_ref=source, dst_ref=whole_view, send_sem=send_sem, recv_sem=recv_sem, device_id=device, device_id_type=MESH
        )
        when(condition, copy.start)
        pending.append((condition, copy.wait_send))

    def arrived(view, recv_sem, condition=True):
        copy = pltpu.make_async_remote_copy(
            src_ref=view, dst_ref=view, send_sem=recv_sem, recv_sem=recv_sem, device_id=here.device(), device_id_type=MESH
        )
        when(condition, copy.wait_recv)

    def view(k, spot, column, core, part=None):
        whole = wholes[k].at[here.shard(spot, column, core)]
        if part is None:
            return whole
        columns = whole.shape[1]
        return whole.at[:, columns_of(part, parts_of(columns, replicas), columns)]

    def spread(k, spot, condition, own=False):
        columns = wholes[k].shape[2]
        parts = parts_of(columns, replicas)
        part = here.replica if parts > 1 else 0
        target = view(k, spot, here.column, here.core)
        source = sources[k] if own else target
        for step in range(1, here.across):
            cut = columns_of(part, parts, columns)
            send(source.at[:, cut], target.at[:, cut], cross_send.at[k, step, spot], cross_recv.at[k, here.column, spot],
                 here.device(column=here.other_column(step)), condition)
        if here.cores > 1:
            send(source, target, core_send.at[k, 0, here.column, spot], core_recv.at[k, 0, here.column, spot],
                 here.device(core=1 - here.core), condition)

    def crossed(k, spot, condition):
        columns = wholes[k].shape[2]
        parts = parts_of(columns, replicas)
        part = here.replica if parts > 1 else 0
        for step in range(1, here.across):
            column = here.other_column(step)
            piece = view(k, spot, column, here.core, part)
            arrived(piece, cross_recv.at[k, column, spot], condition)
            if parts > 1:
                for hop in range(1, replicas):
                    send(piece, piece, rep_send.at[k, hop, column, spot], rep_recv.at[k, here.replica, column, spot],
                         here.device(replica=here.other_replica(hop)), condition)
            if here.cores > 1:
                send(piece, piece, core_send.at[k, 1, column, spot], core_recv.at[k, 1, column, spot],
                     here.device(core=1 - here.core), condition)

    def replicated(k, spot, condition):
        parts = parts_of(wholes[k].shape[2], replicas)
        if parts == 1:
            return
        for step in range(1, here.across):
            column = here.other_column(step)
            for hop in range(1, replicas):
                replica = here.other_replica(hop)
                piece = view(k, spot, column, here.core, replica)
                arrived(piece, rep_recv.at[k, replica, column, spot], condition)
                if here.cores > 1:
                    send(piece, piece, core_send.at[k, 1 + hop, column, spot], core_recv.at[k, 1 + hop, column, spot],
                         here.device(core=1 - here.core), condition)

    def at(distance, action):
        for k in range(count):
            if distance == 0:
                action(k, here.spot, True)
            else:
                action(k, here.spot - distance, here.spot >= distance)
                action(k, here.spot + distance, here.spot + distance < here.line)

    for k in range(count):
        own = view(k, here.spot, here.column, here.core)
        send(sources[k], own, line_send.at[k, 0, here.spot], line_recv.at[k, here.spot],
             here.device(spot=here.spot + 1), here.spot < here.line - 1)
        send(sources[k], own, line_send.at[k, 1, here.spot], line_recv.at[k, here.spot],
             here.device(spot=here.spot - 1), here.spot > 0)
        spread(k, here.spot, True, own=True)
    for k in range(count):
        wholes[k][here.own] = sources[k][...]

    def along(distance):
        for k in range(count):
            for sign in (-1, 1):
                spot = here.spot + sign * distance
                condition = (spot >= 0) & (spot < here.line)
                piece = view(k, spot, here.column, here.core)
                arrived(piece, line_recv.at[k, spot], condition)
                onward = here.spot - sign
                send(piece, piece, line_send.at[k, 0 if sign < 0 else 1, spot], line_recv.at[k, spot],
                     here.device(spot=onward), condition & (onward >= 0) & (onward < here.line))
                spread(k, spot, condition)

    for distance in range(here.line + 2):
        if 1 <= distance < here.line:
            along(distance)
        if 1 <= distance <= here.line:
            at(distance - 1, crossed)
        if 2 <= distance:
            at(distance - 2, replicated)
    if here.cores > 1:
        for k in range(count):
            columns = wholes[k].shape[2]
            parts = parts_of(columns, replicas)
            for spot in range(here.line):
                other = 1 - here.core
                arrived(view(k, spot, here.column, other), core_recv.at[k, 0, here.column, spot])
                for step in range(1, here.across):
                    column = here.other_column(step)
                    part = here.replica if parts > 1 else 0
                    arrived(view(k, spot, column, other, part), core_recv.at[k, 1, column, spot])
                    for hop in range(1, replicas if parts > 1 else 1):
                        arrived(view(k, spot, column, other, here.other_replica(hop)), core_recv.at[k, 1 + hop, column, spot])
    for condition, wait in pending:
        when(condition, wait)


def gather(mesh, arrays, collective_id):
    replicas, shards = mesh.shape["rep"], mesh.shape["shard"]
    count = len(arrays)
    line = shards // 4
    dma = pltpu.SemaphoreType.DMA
    vmem = pl.BlockSpec(memory_space=pltpu.VMEM)
    moved = sum(a.size * 2 * shards for a in arrays)
    return pl.pallas_call(
        functools.partial(gather_kernel, replicas, shards, count),
        name="gather",
        out_shape=[jax.ShapeDtypeStruct((shards,) + a.shape, a.dtype) for a in arrays],
        in_specs=[vmem] * count,
        out_specs=[vmem] * count,
        scratch_shapes=[
            dma((count, 2, line)), dma((count, line)),
            dma((count, 2, line)), dma((count, 2, line)),
            dma((count, replicas, 2, line)), dma((count, replicas, 2, line)),
            dma((count, replicas + 1, 2, line)), dma((count, replicas + 1, 2, line)),
        ],
        compiler_params=pltpu.CompilerParams(collective_id=collective_id, has_side_effects=True, vmem_limit_bytes=56 << 20),
        cost_estimate=pl.CostEstimate(flops=0, bytes_accessed=moved * 4, transcendentals=0),
    )(*arrays)


WORK_INPUTS = ("key_low", "value_low", "query_low", "sum_grad", "mix", "weight")


def scatter_kernel(replicas, shards, count, chunks, extra, work, *refs):
    here = Place(replicas, shards)
    take = lambda number: [refs_left.pop(0) for _ in range(number)]
    refs_left = list(refs)
    sources, extras, work_in = take(count), take(extra), take(len(WORK_INPUTS))
    outs, extra_outs, (tokens_grad,) = take(count), take(extra), take(1)
    own_bufs, core_bufs, rep_bufs, cross_bufs, line_bufs, last_bufs = (take(count) for _ in range(6))
    extra_bufs = take(extra)
    work_bufs, (block_buf, own_sems, work_sems, block_sems) = take(len(WORK_INPUTS)), take(4)
    (core_send, core_recv, rep_send, rep_recv, cross_send, cross_recv, line_send, line_recv, last_send, last_recv) = refs_left
    local = []
    for j, (k, low, size) in enumerate(chunks):
        for column in range(here.across):
            cut = pl.ds(low, size)
            local.append(pltpu.make_async_copy(
                sources[k].at[:, column, here.core, :, cut], own_bufs[k].at[column, :, :, cut], own_sems.at[j, column]
            ))
    here.meet()
    pending = []

    def send(source, target, send_sem, recv_sem, device, condition=True):
        copy = pltpu.make_async_remote_copy(
            src_ref=source, dst_ref=target, send_sem=send_sem, recv_sem=recv_sem, device_id=device, device_id_type=MESH
        )
        when(condition, copy.start)
        pending.append((condition, copy.wait_send))

    def arrived(view, recv_sem, condition=True):
        copy = pltpu.make_async_remote_copy(
            src_ref=view, dst_ref=view, send_sem=recv_sem, recv_sem=recv_sem, device_id=here.device(), device_id_type=MESH
        )
        when(condition, copy.wait_recv)

    def add(target, source):
        target[...] = target[...] + source[...]

    steps = range(1, here.across)
    hops = range(1, replicas)

    def split(j):
        return parts_of(chunks[j][2], replicas)

    def columns(j, part=None):
        _, low, size = chunks[j]
        if part is None or split(j) == 1:
            return pl.ds(low, size)
        size = size // replicas
        return pl.ds(pl.multiple_of(low + part * size, 128), size)

    def compact(j):
        _, low, size = chunks[j]
        return pl.ds(low // split(j), size // split(j))

    def mixed(j, column):
        k = chunks[j][0]
        mine = core_bufs[k].at[column, :, :, columns(j)]
        own = own_bufs[k].at[column, :, :, columns(j)]
        _, low, size = chunks[j]
        cut = pl.ds(low, size)
        pltpu.make_async_copy(
            sources[k].at[:, column, here.core, :, cut], own_bufs[k].at[column, :, :, cut], own_sems.at[j, column]
        ).wait()
        if here.cores > 1:
            arrived(mine, core_recv.at[j, column])
            add(mine, own)
        else:
            mine[...] = own[...]

    def stage_rep(j):
        k = chunks[j][0]
        for step in steps:
            column = here.other_column(step)
            mixed(j, column)
            if split(j) > 1:
                for hop in hops:
                    replica = here.other_replica(hop)
                    send(core_bufs[k].at[column, :, :, columns(j, replica)], rep_bufs[k].at[hop - 1, step - 1, :, :, compact(j)],
                         rep_send.at[j, hop, step], rep_recv.at[j, hop, step], here.device(replica=replica))

    def stage_cross(j):
        k = chunks[j][0]
        for step in steps:
            column = here.other_column(step)
            mine = core_bufs[k].at[column, :, :, columns(j, here.replica)]
            if split(j) > 1:
                for hop in hops:
                    piece = rep_bufs[k].at[hop - 1, step - 1, :, :, compact(j)]
                    arrived(piece, rep_recv.at[j, hop, step])
                    add(mine, piece)
            send(mine, cross_bufs[k].at[step - 1, :, :, compact(j)], cross_send.at[j, step], cross_recv.at[j, step],
                 here.device(column=column))
        mixed(j, here.column)

    def stage_line(distance, j):
        k = chunks[j][0]
        if distance == here.line - 1:
            for step in steps:
                piece = cross_bufs[k].at[step - 1, :, :, compact(j)]
                arrived(piece, cross_recv.at[j, step])
                add(core_bufs[k].at[here.column, :, :, columns(j, here.replica)], piece)
        for sign, way in ((1, 0), (-1, 1)):
            target = here.spot + sign * distance
            inside = (target >= 0) & (target < here.line)
            before = here.spot - sign
            fed = inside & (before >= 0) & (before < here.line)
            mine = core_bufs[k].at[here.column, target, :, columns(j)]
            piece = line_bufs[k].at[way, target, :, columns(j)]
            arrived(piece, line_recv.at[j, way, target], fed)
            when(fed, functools.partial(add, mine, piece))
            send(mine, piece, line_send.at[j, way, target], line_recv.at[j, way, target],
                 here.device(spot=here.spot + sign), inside)

    def stage_last(j):
        k = chunks[j][0]
        mine = core_bufs[k].at[here.column, here.spot, :, columns(j)]
        for sign, way in ((1, 0), (-1, 1)):
            before = here.spot - sign
            fed = (before >= 0) & (before < here.line)
            piece = line_bufs[k].at[way, here.spot, :, columns(j)]
            arrived(piece, line_recv.at[j, way, here.spot], fed)
            when(fed, functools.partial(add, mine, piece))
        for hop in hops:
            send(mine, last_bufs[k].at[here.replica, :, columns(j)], last_send.at[j, hop], last_recv.at[j, here.replica],
                 here.device(replica=here.other_replica(hop)))

    def finish(own, buffer, out, semaphore, cut):
        for hop in hops:
            replica = here.other_replica(hop)
            arrived(buffer.at[replica, :, cut], semaphore.at[replica])
        result = None
        for replica in range(replicas):
            term = jnp.where(here.replica == replica, own[...].astype(f32), buffer[replica, :, cut].astype(f32))
            result = term if result is None else result + term
        out[:, cut] = result

    def stage_finish(j):
        k = chunks[j][0]
        finish(core_bufs[k].at[here.column, here.spot, :, columns(j)], last_bufs[k], outs[k], last_recv.at[j], columns(j))

    if here.cores > 1:
        for j, (k, _, _) in enumerate(chunks):
            for step in (*steps, 0):
                column = here.other_column(step)
                send(sources[k].at[:, column, 1 - here.core, :, columns(j)], core_bufs[k].at[column, :, :, columns(j)],
                     core_send.at[j, column], core_recv.at[j, column], here.device(core=1 - here.core))
    for copy in local:
        copy.start()
    loads = [pltpu.make_async_copy(ref, buf, work_sems.at[i]) for i, (ref, buf) in enumerate(zip(work_in, work_bufs))]
    for copy in loads:
        copy.start()
    stores = []

    def block(b):
        if b == 0:
            for copy in loads:
                copy.wait()
        if b >= 2:
            stores[b - 2].wait()
        block_buf[b % 2] = work(b, *work_bufs)
        size = block_buf.shape[1]
        stores.append(pltpu.make_async_copy(block_buf.at[b % 2], tokens_grad.at[pl.ds(b * size, size)], block_sems.at[b % 2]))
        stores[b].start()

    blocks = tokens_grad.shape[0] // block_buf.shape[1]
    stages = [stage_rep, stage_cross]
    stages += [functools.partial(stage_line, distance) for distance in range(here.line - 1, 0, -1)]
    stages += [stage_last, stage_finish]
    total = len(chunks)
    for time in range(total + len(stages) - 1):
        for place in reversed(range(len(stages))):
            if 0 <= time - place < total:
                stages[place](time - place)
        if time == 0:
            for e in range(extra):
                for hop in hops:
                    send(extras[e], extra_bufs[e].at[here.replica], last_send.at[total + e, hop],
                         last_recv.at[total + e, here.replica], here.device(replica=here.other_replica(hop)))
        elif time <= blocks:
            block(time - 1)
    for b in range(min(blocks, total + len(stages) - 2), blocks):
        block(b)
    for b in range(max(blocks - 2, 0), blocks):
        stores[b].wait()
    for e in range(extra):
        finish(extras[e], extra_bufs[e], extra_outs[e], last_recv.at[total + e], pl.ds(0, extras[e].shape[1]))
    for condition, wait in pending:
        when(condition, wait)


def scatter(mesh, arrays, widths, extras, inputs, work, collective_id):
    replicas, shards = mesh.shape["rep"], mesh.shape["shard"]
    count, extra = len(arrays), len(extras)
    dma = pltpu.SemaphoreType.DMA
    vmem = pl.BlockSpec(memory_space=pltpu.VMEM)
    cores = across = 2
    line = shards // (cores * across)
    shapes = [a.shape[1:] for a in arrays]
    chunks = [
        (k, low, min(width, shapes[k][1])) for k, width in enumerate(widths) for low in range(0, shapes[k][1], min(width, shapes[k][1]))
    ]
    cuts = [(shapes[k][0], shapes[k][1] // parts_of(min(width, shapes[k][1]), replicas)) for k, width in enumerate(widths)]
    moved = sum(a.size * 2 for a in arrays)
    number = len(chunks)
    rows = inputs[0].shape[0]
    size = min(rows, 256)
    anywhere = pl.BlockSpec(memory_space=pl.ANY)
    buffers = (
        [pltpu.VMEM((across, line) + s, bf16) for s in shapes]
        + [pltpu.VMEM((across, line) + s, bf16) for s in shapes]
        + [pltpu.VMEM((replicas - 1, across - 1, line) + s, bf16) for s in cuts]
        + [pltpu.VMEM((across - 1, line) + s, bf16) for s in cuts]
        + [pltpu.VMEM((2, line) + s, bf16) for s in shapes]
        + [pltpu.VMEM((replicas,) + s, bf16) for s in shapes]
        + [pltpu.VMEM((replicas,) + e.shape, bf16) for e in extras]
        + [pltpu.VMEM(i.shape, i.dtype) for i in inputs]
        + [pltpu.VMEM((2, size, inputs[0].shape[1]), f32), dma((number, across)), dma((len(inputs),)), dma((2,))]
    )
    return pl.pallas_call(
        functools.partial(scatter_kernel, replicas, shards, count, chunks, extra, work),
        name="scatter",
        out_shape=(
            [jax.ShapeDtypeStruct(s, f32) for s in shapes]
            + [jax.ShapeDtypeStruct(e.shape, f32) for e in extras]
            + [jax.ShapeDtypeStruct(inputs[0].shape, f32)]
        ),
        in_specs=[anywhere] * count + [vmem] * extra + [anywhere] * len(inputs),
        out_specs=[vmem] * (count + extra) + [anywhere],
        scratch_shapes=buffers + [
            dma((number, across)), dma((number, across)),
            dma((number, replicas, across)), dma((number, replicas, across)),
            dma((number, across)), dma((number, across)),
            dma((number, 2, line)), dma((number, 2, line)),
            dma((number + extra, replicas)), dma((number + extra, replicas)),
        ],
        compiler_params=pltpu.CompilerParams(collective_id=collective_id, has_side_effects=True, vmem_limit_bytes=62 << 20),
        cost_estimate=pl.CostEstimate(flops=0, bytes_accessed=moved * 4, transcendentals=0),
    )(*[a.reshape((line, across, cores) + a.shape[1:]) for a in arrays], *extras, *inputs)


FIRST_VECTOR = 34
VMEM_ALL = 62 << 20


def place_of(rows):
    return lax.broadcasted_iota(jnp.int32, (rows, 2 * rows), 1) - 2 * lax.broadcasted_iota(jnp.int32, (rows, 2 * rows), 0)


def mixing(own, rest):
    place = place_of(own.shape[0])
    return jnp.where(place == 0, own, jnp.where(place == 1, rest, 0.0)).astype(bf16)


def project_kernel(
    tokens_ref, hot_ref, weight_ref, small_ref,
    pooled_ref, content_ref, position_ref, ordering_ref, key_ref, value_ref, document_ref, mix_ref,
):
    width = tokens_ref.shape[1]
    rows = pooled_ref.shape[0]
    tokens = tokens_ref[...]
    place = place_of(rows)
    first, second = (nn(jnp.where(place == j, 1.0, 0.0).astype(bf16), hot_ref[...]) for j in range(2))
    document_ref[...] = first.astype(bf16)
    own = 1.0 / (1.0 + jnp.sum(first * second, axis=1, keepdims=True))
    mix_ref[...] = jnp.broadcast_to(own, mix_ref.shape)
    pooled = nn(mixing(own, 1.0 - own), tokens)
    pooled_ref[...] = pooled
    key_ref[...] = nn(tokens, weight_ref[:, width : 2 * width]).astype(bf16)
    value_ref[...] = nn(tokens, weight_ref[:, 2 * width :]).astype(bf16)
    queries = nn(pooled.astype(bf16), weight_ref[:, :width])
    bias = small_ref[2:5, :].astype(f32)
    content_ref[...] = ((queries + bias[0:1]) * (0.125 * LOG2E)).astype(bf16)
    position_ref[...] = (queries + bias[1:2]).astype(bf16)
    ordering_ref[...] = (queries + bias[2:3]).astype(bf16)


def project(tokens, hot, weight, small):
    length, width = tokens.shape
    block = 256
    steps = length // block
    whole = lambda n: pl.BlockSpec((block, n), lambda i: (i, 0))
    half = lambda n: pl.BlockSpec((block // 2, n), lambda i: (i, 0))
    rows = jax.ShapeDtypeStruct((length // 2, width), bf16)
    full = jax.ShapeDtypeStruct((length, width), bf16)
    narrow = lambda kind: jax.ShapeDtypeStruct((length // 2, 128), kind)
    return pl.pallas_call(
        project_kernel,
        name="project",
        grid=(steps,),
        out_shape=(jax.ShapeDtypeStruct((length // 2, width), f32), rows, rows, rows, full, full, narrow(bf16), narrow(f32)),
        in_specs=[whole(width), whole(128), fixed(*weight.shape), fixed(*small.shape)],
        out_specs=[half(width)] * 4 + [whole(width)] * 2 + [half(128)] * 2,
        compiler_params=pltpu.CompilerParams(vmem_limit_bytes=VMEM_ALL),
        cost_estimate=pl.CostEstimate(flops=5 * length * width * width, bytes_accessed=10 * length * width, transcendentals=0),
    )(tokens, hot, weight, small)


def mean(values):
    return jnp.mean(values, axis=1, keepdims=True)


def normalize(values):
    centered = values - mean(values)
    inverse = lax.rsqrt(mean(centered * centered) + 1e-05)
    return centered * inverse, inverse


def norm_back(grad, normed, inverse):
    return inverse * (grad - mean(grad) - normed * mean(grad * normed))


def column_sum(values):
    return jnp.sum(values, axis=0, keepdims=True)


def middle_kernel(
    blocks, context_ref, pooled_ref, cotangent_ref, wide_ref, outer_ref, small_ref, bias_ref,
    layer_ref, sum_ref, context_grad_ref, sums_ref, inner_sums_ref, output_out, inner_out, outer_out,
    act, back, slope, first_all, outer_all, attended_all, context_all,
):
    step = pl.program_id(0)
    size, width = pooled_ref.shape
    hidden = bias_ref.shape[1]
    chunks = [slice(c * width, (c + 1) * width) for c in range(hidden // width)]

    @pl.when(step == 0)
    def _():
        sums_ref[...] = jnp.zeros(sums_ref.shape, f32)
        inner_sums_ref[...] = jnp.zeros(inner_sums_ref.shape, f32)

    @pl.when(step < blocks)
    def _():
        rows = pl.ds(pl.multiple_of(step * size, size), size)

        def vector(j):
            return small_ref[2 + j : 3 + j, :].astype(f32)

        context = context_ref[...]
        context_all[rows, :] = context
        first_norm, first_inverse = normalize(pooled_ref[...] + nn(context, wide_ref[:, :width]))
        first = first_norm * vector(3) + vector(4)
        first_low = first.astype(bf16)
        first_all[rows, :] = first_low
        outer = None
        for cut in chunks:
            inner = nn(first_low, wide_ref[:, width + cut.start : width + cut.stop]) + bias_ref[:, cut].astype(f32)
            cumulative = 0.5 * (1.0 + lax.erf(inner * math.sqrt(0.5)))
            act_low = (inner * cumulative).astype(bf16)
            act[rows, cut] = act_low
            slope[:, cut] = cumulative + inner * (jnp.exp(-0.5 * inner * inner) * (1.0 / math.sqrt(2.0 * math.pi)))
            part = nn(act_low, outer_ref[cut, :])
            outer = part if outer is None else outer + part
        second_norm, second_inverse = normalize(first + outer + vector(5))
        layer_ref[...] = (second_norm * vector(6) + vector(7)).astype(bf16)
        cotangent = cotangent_ref[...].astype(f32)
        mid_grad = norm_back(cotangent * vector(6), second_norm, second_inverse)
        outer_low = mid_grad.astype(bf16)
        outer_all[rows, :] = outer_low
        first_grad = mid_grad
        for cut in chunks:
            inner_grad = nt(outer_low, outer_ref[cut, :]) * slope[:, cut]
            inner_low = inner_grad.astype(bf16)
            back[rows, cut] = inner_low
            inner_sums_ref[0:1, cut] += column_sum(inner_low.astype(f32))
            first_grad = first_grad + nt(inner_low, wide_ref[:, width + cut.start : width + cut.stop])
        sum_grad = norm_back(first_grad * vector(3), first_norm, first_inverse)
        sum_ref[...] = sum_grad
        attended_low = sum_grad.astype(bf16)
        attended_all[rows, :] = attended_low
        context_grad_ref[...] = nt(attended_low, wide_ref[:, :width]).astype(bf16)
        for j, term in enumerate(
            (first_grad * first_norm, first_grad, outer_low.astype(f32), cotangent * second_norm, cotangent)
        ):
            sums_ref[j : j + 1, :] += column_sum(term)

    @pl.when((step >= blocks) & (step < blocks + len(chunks)))
    def _():
        cut = pl.ds(pl.multiple_of((step - blocks) * width, width), width)
        outer_out[...] = tn(act[:, cut], outer_all[...]).astype(bf16)
        inner_out[...] = tn(first_all[...], back[:, cut]).astype(bf16)

    @pl.when(step == blocks + len(chunks))
    def _():
        output_out[...] = tn(context_all[...], attended_all[...]).astype(bf16)


def middle(context, pooled, cotangent, wide, outer, small, bias):
    rows, width = context.shape
    hidden = bias.shape[1]
    size = 256
    blocks, chunks = rows // size, hidden // width
    block = pl.BlockSpec((size, width), lambda i: (jnp.minimum(i, blocks - 1), 0))
    chunk = lambda i: jnp.clip(i - blocks, 0, chunks - 1)
    low = jax.ShapeDtypeStruct((rows, width), bf16)
    flops = 18 * rows * width * hidden
    return pl.pallas_call(
        functools.partial(middle_kernel, blocks),
        name="middle",
        grid=(blocks + chunks + 1,),
        out_shape=(
            low,
            jax.ShapeDtypeStruct((rows, width), f32),
            low,
            jax.ShapeDtypeStruct((8, width), f32),
            jax.ShapeDtypeStruct((8, hidden), f32),
            jax.ShapeDtypeStruct((width, width), bf16),
            jax.ShapeDtypeStruct((width, hidden), bf16),
            jax.ShapeDtypeStruct((hidden, width), bf16),
        ),
        in_specs=[block, block, block, fixed(*wide.shape), fixed(*outer.shape), fixed(*small.shape), fixed(*bias.shape)],
        out_specs=[
            block, block, block, fixed(8, width), fixed(8, hidden), fixed(width, width),
            pl.BlockSpec((width, width), lambda i: (0, chunk(i))),
            pl.BlockSpec((width, width), lambda i: (chunk(i), 0)),
        ],
        scratch_shapes=[
            pltpu.VMEM((rows, hidden), bf16),
            pltpu.VMEM((rows, hidden), bf16),
            pltpu.VMEM((size, hidden), f32),
            pltpu.VMEM((rows, width), bf16),
            pltpu.VMEM((rows, width), bf16),
            pltpu.VMEM((rows, width), bf16),
            pltpu.VMEM((rows, width), bf16),
        ],
        compiler_params=pltpu.CompilerParams(vmem_limit_bytes=60 << 20),
        cost_estimate=pl.CostEstimate(flops=flops, bytes_accessed=40 * rows * width, transcendentals=2 * rows * hidden),
    )(context, pooled, cotangent, wide, outer, small, bias)


def tail_kernel(tokens_ref, key_ref, value_ref, query_ref, pooled_ref, weight_grad_ref, total):
    step = pl.program_id(0)
    width = tokens_ref.shape[1]

    @pl.when(step == 0)
    def _():
        total[...] = jnp.zeros(total.shape, f32)

    tokens = tokens_ref[...]
    total[:, :width] += tn(pooled_ref[...].astype(bf16), query_ref[...])
    total[:, width : 2 * width] += tn(tokens, key_ref[...])
    total[:, 2 * width :] += tn(tokens, value_ref[...])

    @pl.when(step == pl.num_programs(0) - 1)
    def _():
        weight_grad_ref[...] = total[...].astype(bf16)


def tail(tokens, key_low, value_low, query_low, pooled):
    length, width = tokens.shape
    block = 512
    whole = pl.BlockSpec((block, width), lambda i: (i, 0))
    half = pl.BlockSpec((block // 2, width), lambda i: (i, 0))
    return pl.pallas_call(
        tail_kernel,
        name="tail",
        grid=(length // block,),
        out_shape=jax.ShapeDtypeStruct((width, 3 * width), bf16),
        in_specs=[whole, whole, whole, half, half],
        out_specs=fixed(width, 3 * width),
        scratch_shapes=[pltpu.VMEM((width, 3 * width), f32)],
        compiler_params=pltpu.CompilerParams(vmem_limit_bytes=VMEM_ALL),
        cost_estimate=pl.CostEstimate(flops=5 * length * width * width, bytes_accessed=8 * length * width, transcendentals=0),
    )(tokens, key_low, value_low, query_low, pooled)


def tokens_block(block, key_ref, value_ref, query_ref, sum_ref, mix_ref, weight_ref):
    width = key_ref.shape[1]
    whole, half = slice(256 * block, 256 * block + 256), slice(128 * block, 128 * block + 128)
    pooled_grad = sum_ref[half, :] + nt(query_ref[half, :], weight_ref[:, :width])
    coarse = pooled_grad.astype(bf16)
    fine = (pooled_grad - coarse.astype(f32)).astype(bf16)
    own = mix_ref[half, :1]
    mix = mixing(own, 1.0 - own)
    return (
        tn(mix, coarse) + tn(mix, fine)
        + nt(key_ref[whole, :], weight_ref[:, width : 2 * width])
        + nt(value_ref[whole, :], weight_ref[:, 2 * width :])
    )


def pack_kernel(count, folds, *refs):
    squares, (output_ref, inner_ref, relative_ref, order_ref) = refs[:3], refs[3:7]
    vectors, bias_ref = refs[7 : 7 + count], refs[7 + count]
    wide_ref, small_ref, projections_ref = refs[8 + count :]
    width = output_ref.shape[1]
    each = relative_ref.shape[1]
    for j, ref in enumerate(squares):
        projections_ref[:, j * width : (j + 1) * width] = ref[...]
    wide_ref[:, :width] = output_ref[...]
    wide_ref[:, width:] = inner_ref[...]
    small_ref[...] = jnp.zeros(small_ref.shape, bf16)
    rows = [relative_ref[...].astype(f32), order_ref[...].astype(f32)]
    rows += [ref[...].astype(f32).reshape(1, each) for ref in vectors]
    bias = bias_ref[...].astype(f32).reshape(1, folds * each)
    rows += [bias[:, j * each : (j + 1) * each] for j in range(folds)]
    small_ref[: FIRST_VECTOR + count + folds, :each] = jnp.concatenate(rows, 0).astype(bf16)


def pack(squares, output, inner, relative, order, vectors, bias, folds):
    rows = -(-(FIRST_VECTOR + len(vectors) + folds) // 16) * 16
    return pl.pallas_call(
        functools.partial(pack_kernel, len(vectors), folds),
        name="pack",
        out_shape=(
            jax.ShapeDtypeStruct((output.shape[0], output.shape[1] + inner.shape[1]), bf16),
            jax.ShapeDtypeStruct((rows, 128), bf16),
            jax.ShapeDtypeStruct((output.shape[0], 3 * output.shape[1]), bf16),
        ),
        cost_estimate=pl.CostEstimate(flops=0, bytes_accessed=4 * inner.size, transcendentals=0),
    )(*squares, output, inner, relative, order, *vectors, bias)


def finish_kernel(count, folds, projection_ref, output_ref, inner_ref, outer_ref, small_ref, *outs):
    width = output_ref.shape[1]
    squares, (output_out, inner_out, outer_out, relative_out, order_out) = outs[:3], outs[3:8]
    vectors, bias_out = outs[8 : 8 + count], outs[8 + count]
    each = relative_out.shape[1]
    for j, ref in enumerate(squares):
        ref[...] = projection_ref[:, j * width : (j + 1) * width]
    output_out[...] = output_ref[...]
    inner_out[...] = inner_ref[...]
    outer_out[...] = outer_ref[...]
    small = small_ref[...]
    relative_out[...] = small[:32, :each]
    order_out[...] = small[32:34, :each]
    for j, ref in enumerate(vectors):
        ref[...] = small[FIRST_VECTOR + j, :each]
    start = FIRST_VECTOR + count
    bias_out[...] = jnp.concatenate([small[start + j : start + j + 1, :each] for j in range(folds)], 1).reshape(folds * each)


def finish(projection, output, inner, outer, small, count, folds):
    each, width = small.shape[0], output.shape[1]
    rows = output.shape[0]
    shape = lambda *s: jax.ShapeDtypeStruct(s, f32)
    return pl.pallas_call(
        functools.partial(finish_kernel, count, folds),
        name="finish",
        out_shape=(
            [shape(rows, width)] * 4 + [shape(*inner.shape), shape(*outer.shape), shape(32, rows), shape(2, rows)]
            + [shape(rows)] * count + [shape(folds * rows)]
        ),
        cost_estimate=pl.CostEstimate(flops=0, bytes_accessed=8 * inner.size, transcendentals=0),
    )(projection, output, inner, outer, small)


def unpack_kernel(shards, folds, start, small_ref, segment_ref, relative_out, order_out, vectors_out, bias_out, hot_out, away_out, behind_out, ahead_out):
    each = relative_out.shape[1] // shards
    length = segment_ref.shape[1]
    own = [small_ref[s].astype(f32) for s in range(shards)]
    whole = jnp.concatenate([piece[:start, :each] for piece in own], 1).astype(bf16)
    relative_out[...] = whole[:32]
    order_out[...] = whole[32:34]
    vectors_out[: start - 32, :] = whole[32:]
    bias_out[...] = jnp.concatenate(
        [piece[start + j : start + j + 1, :each] for piece in own for j in range(folds)], 1
    ).astype(bf16)
    document = lax.broadcasted_iota(jnp.int32, (128, length), 0)
    same = jnp.where(segment_ref[...] == document, 1.0, 0.0).T
    counted = lax.broadcasted_iota(jnp.int32, same.shape, 1) < 8
    hot_out[...] = same.astype(bf16)
    away_out[256 : 256 + length, :] = jnp.where(counted, -BIG * (1.0 - same), 0.0).astype(bf16)
    pad = jnp.where(counted[:256], -BIG, 0.0).astype(bf16)
    away_out[:256, :] = pad
    away_out[256 + length :, :] = pad
    blocks = behind_out.shape[0]
    own_row = jnp.broadcast_to(segment_ref[...], (blocks, length))
    lane = lax.broadcasted_iota(jnp.int32, (blocks, length), 1)
    start = 2 * BQ * lax.broadcasted_iota(jnp.int32, (blocks, length), 0)
    total = lambda values: jnp.sum(values, axis=1, keepdims=True)
    at = lambda place: total(jnp.where(lane == place, own_row, 0))
    first = total(jnp.where(own_row < at(start), 1, 0))
    last = total(jnp.where(own_row <= at(start + 2 * BQ - 2), 1, 0))
    chunks = lambda rest: lax.shift_right_logical(jnp.maximum(rest + CHUNK - 1, 0), CHUNK.bit_length() - 1)
    behind_out[...] = chunks(start[:, :128] - 256 - first)
    ahead_out[...] = chunks(last - (start[:, :128] - 256 + NEAR))


def unpack(small, segments, width, count, folds):
    shards = small.shape[0]
    length = segments.shape[1]
    start = FIRST_VECTOR + count
    shape = lambda *s: jax.ShapeDtypeStruct(s, bf16)
    return pl.pallas_call(
        functools.partial(unpack_kernel, shards, folds, start),
        name="unpack",
        out_shape=(shape(32, width), shape(2, width), shape(16, width), shape(1, folds * width), shape(length, 128), shape(length + 512, 128))
        + (jax.ShapeDtypeStruct((length // (2 * BQ), 128), jnp.int32),) * 2,
        compiler_params=pltpu.CompilerParams(vmem_limit_bytes=VMEM_ALL),
        cost_estimate=pl.CostEstimate(flops=0, bytes_accessed=1 << 20, transcendentals=0),
    )(small, segments)


def collect_kernel(folds, relative_ref, order_ref, bias_ref, sums_ref, inner_ref, out_ref):
    shards, rows, _ = out_ref.shape
    width = relative_ref.shape[1]
    each = width // shards
    whole = jnp.concatenate([relative_ref[...], order_ref[:2], bias_ref[:3], sums_ref[:5]], 0)
    inner = inner_ref[0:1, :]
    out_ref[...] = jnp.zeros(out_ref.shape, bf16)
    for s in range(shards):
        cut = slice(s * each, s * each + each)
        own = [inner[:, (s * folds + j) * each : (s * folds + j + 1) * each] for j in range(folds)]
        piece = jnp.concatenate([whole[:, cut], *own], 0)
        out_ref[s, : piece.shape[0], :each] = piece.astype(bf16)


def collect(relative, order, bias, sums, inner, shards, count, folds):
    rows = -(-(FIRST_VECTOR + count + folds) // 16) * 16
    return pl.pallas_call(
        functools.partial(collect_kernel, folds),
        name="collect",
        out_shape=jax.ShapeDtypeStruct((shards, rows, 128), bf16),
        compiler_params=pltpu.CompilerParams(vmem_limit_bytes=VMEM_ALL),
        cost_estimate=pl.CostEstimate(flops=0, bytes_accessed=1 << 19, transcendentals=0),
    )(relative, order, bias, sums, inner)


def body(
    mesh,
    tokens,
    segment_ids,
    query_weight,
    key_weight,
    value_weight,
    output_weight,
    relative_table,
    order_table,
    content_bias,
    position_bias,
    order_bias,
    first_gain,
    first_shift,
    inner_weight,
    inner_bias,
    outer_weight,
    outer_bias,
    second_gain,
    second_shift,
    cotangent,
):
    shards = mesh.shape["shard"]
    width = tokens.shape[1]
    hidden = inner_weight.shape[1]
    each = width // shards
    folds = hidden // width
    vectors = (content_bias, position_bias, order_bias, first_gain, first_shift, outer_bias, second_gain, second_shift)
    wide_own, small, projections_own = pack(
        (query_weight, key_weight, value_weight), output_weight, inner_weight, relative_table, order_table, vectors, inner_bias, folds
    )
    projections, small_all = gather(mesh, [projections_own, small], 0)
    projections = projections.reshape(width, 3 * width)
    weight_relative, weight_order, small_all, bias_inner, hot, away, behind, ahead = unpack(
        small_all, segment_ids, width, len(vectors), folds
    )
    wide = lax.all_gather(wide_own, "shard", axis=0, tiled=True)
    weight_outer = lax.all_gather(outer_weight, "shard", axis=0, tiled=True)

    pooled, content, position, ordering, keys, values, document, mix = project(tokens, hot, projections, small_all)
    probs, context, mixed, inverse = attend(
        behind, ahead, content, position, ordering, keys, values, weight_relative, weight_order, away, document
    )
    layer_out, sum_grad, context_grad, sums, inner_sums, output_grad, inner_grad, outer_grad = middle(
        context, pooled, cotangent, wide, weight_outer, small_all, bias_inner
    )
    query_low, key_low, value_low, relative_grad, order_grad, bias_sums = attend_back(
        behind, ahead, probs, context_grad, mixed, inverse, content, position, ordering,
        keys, values, weight_relative, weight_order,
    )
    projection_grad = tail(tokens, key_low, value_low, query_low, pooled)
    small_grad = collect(relative_grad, order_grad, bias_sums, sums, inner_sums, shards, len(vectors), folds)
    outer_part = lax.psum_scatter(outer_grad, "shard", scatter_dimension=0, tiled=True)
    inner_sum, output_sum, projection_sum, small_sum, outer_sum, tokens_grad = scatter(
        mesh,
        [
            inner_grad.reshape(shards, each, hidden),
            output_grad.reshape(shards, each, width),
            projection_grad.reshape(shards, each, 3 * width),
            small_grad,
        ],
        [width, width, width, 128],
        [outer_part],
        [key_low, value_low, query_low, sum_grad, mix, projections],
        tokens_block,
        1,
    )
    parts = finish(projection_sum, output_sum, inner_sum, outer_sum, small_sum, len(vectors), folds)
    squares, (inner_sum, outer_sum, relative_sum, order_sum) = parts[:4], parts[4:8]
    own, bias_sum = parts[8:-1], parts[-1]
    return (
        layer_out, tokens_grad, *squares, relative_sum, order_sum, *own[:5],
        inner_sum, bias_sum, outer_sum, *own[5:],
    )


def solution(mesh):
    placed = (
        P(("rep", "shard"), None),
        P(("rep", "shard"), None),
        P("shard", None),
        P("shard", None),
        P("shard", None),
        P("shard", None),
        P(None, "shard"),
        P(None, "shard"),
        P("shard"),
        P("shard"),
        P("shard"),
        P("shard"),
        P("shard"),
        P("shard", None),
        P("shard"),
        P("shard", None),
        P("shard"),
        P("shard"),
        P("shard"),
        P(("rep", "shard"), None),
    )
    return jax.shard_map(
        functools.partial(body, mesh),
        mesh=mesh,
        in_specs=placed,
        out_specs=(
            P(("rep", "shard"), None),
            P(("rep", "shard"), None),
            P("shard", None),
            P("shard", None),
            P("shard", None),
            P("shard", None),
            P(None, "shard"),
            P(None, "shard"),
            P("shard"),
            P("shard"),
            P("shard"),
            P("shard"),
            P("shard"),
            P("shard", None),
            P("shard"),
            P("shard", None),
            P("shard"),
            P("shard"),
            P("shard"),
        ),
        check_vma=False,
    )
```

```python
import functools
import math

import jax
import jax.numpy as jnp
import numpy as np
from jax import lax
from jax.experimental import pallas as pl
from jax.experimental.pallas import tpu as pltpu
from jax.sharding import PartitionSpec as P

LIMITS = (1, 2, 3, 4, 5, 6, 7, 8, 12, 16, 24, 32, 48, 64, 128)
BQ = 128
NEAR = 640
CHUNK = 256
LOG2E = math.log2(math.e)
LN2 = math.log(2.0)
BIG = 1e30
f32 = jnp.float32
bf16 = jnp.bfloat16


def bucket_of(offset):
    distance = np.abs(offset)
    passed = sum((distance >= limit).astype(np.int32) for limit in LIMITS)
    return np.where(offset < 0, 15 + passed + (distance >= 256), passed).astype(np.int32)


def bucket_onehot():
    out = np.zeros((4 * 128, 128), np.float32)
    offsets = np.concatenate([np.arange(-256, 128), np.full(64, -300), np.full(64, 300)])
    out[np.arange(512), bucket_of(offsets)] = 1
    out[:, 32] = offsets >= 0
    out[:, 33] = offsets < 0
    return out


def nt(left, right):
    return lax.dot_general(left, right, (((1,), (1,)), ((), ())), preferred_element_type=f32)


def nn(left, right):
    return lax.dot_general(left, right, (((1,), (0,)), ((), ())), preferred_element_type=f32)


def tn(left, right):
    return lax.dot_general(left, right, (((0,), (0,)), ((), ())), preferred_element_type=f32)


def halves(array):
    low = lax.broadcasted_iota(jnp.int32, array.shape, 1) < 64
    zero = jnp.zeros_like(array)
    return jnp.where(low, array, zero), jnp.where(low, zero, array)


def pick(array):
    half = array.shape[0] // 2
    low = lax.broadcasted_iota(jnp.int32, (half, 128), 1) < 64
    return jnp.where(low, array[:half], array[half:])


def take(table, index):
    numbers = lax.GatherDimensionNumbers(
        offset_dims=(), collapsed_slice_dims=(1,), start_index_map=(1,),
        operand_batching_dims=(0,), start_indices_batching_dims=(0,),
    )
    return lax.gather(table, index[:, :, None], numbers, (1, 1), mode=lax.GatherScatterMode.PROMISE_IN_BOUNDS)


def lanes_of(p):
    return slice(128 * p, 128 * p + 128)


def far_start(chunk, behind, far, near):
    start = jnp.where(chunk < behind, near - CHUNK * (chunk + 1), near + NEAR + CHUNK * (chunk - behind))
    return pl.multiple_of(jnp.where(chunk < far, start, 0), 128)


def forward_kernel(
    group, behind_ref, ahead_ref, content_ref, position_ref, ordering_ref, key_ref, value_ref,
    relative_ref, order_ref, away_ref, document_ref,
    probs_ref, context_ref, mixed_ref, inverse_ref,
    index_ref, keys, values, table, bias, scores, peak, total,
):
    step = pl.program_id(1)
    length = key_ref.shape[0]

    rows_each = 256
    pieces = length // rows_each

    @pl.when((step == 0) & (pl.program_id(0) == 0))
    def _():
        @pl.loop(0, NEAR // 128)
        def _(tile):
            lane = lax.broadcasted_iota(jnp.int32, (BQ, 128), 1)
            row = lax.broadcasted_iota(jnp.int32, (BQ, 128), 0)
            offset = 128 * (tile - 2) + lane - 2 * row
            distance = jnp.abs(offset)
            passed = jnp.zeros_like(offset)
            for limit in LIMITS:
                passed = passed + jnp.where(distance >= limit, 1, 0)
            index_ref[tile] = jnp.where(offset < 0, 15 + passed + jnp.where(distance >= 256, 1, 0), passed)

        @pl.loop(0, group)
        def _(p):
            for scratch in (keys, values):
                scratch[p, :256, :128] = jnp.zeros((256, 128), bf16)
                scratch[p, 256 + length :, :128] = jnp.zeros((256, 128), bf16)

            @pl.loop(0, pieces + 2)
            def _(piece):
                rows = pl.ds(pl.multiple_of(piece * rows_each, rows_each), rows_each)
                keys[p, rows, 128:] = away_ref[rows, :]
                values[p, rows, 128:] = jnp.ones((rows_each, 128), bf16)

    @pl.when(step == 0)
    def _():
        @pl.loop(0, pieces)
        def _(piece):
            source = pl.ds(pl.multiple_of(piece * rows_each, rows_each), rows_each)
            target = pl.ds(pl.multiple_of((piece + 1) * rows_each, rows_each), rows_each)
            for p in range(group):
                keys[p, target, :128] = key_ref[source, lanes_of(p)]
                values[p, target, :128] = value_ref[source, lanes_of(p)]

        after = lax.broadcasted_iota(jnp.int32, (32, 128), 0) < 16
        table[...] = jnp.zeros(table.shape, bf16)
        for p in range(group):
            lanes = lanes_of(p)
            orders = jnp.where(after, order_ref[0:1, lanes].astype(f32), order_ref[1:2, lanes].astype(f32)).astype(bf16)
            for half, (relative, order) in enumerate(zip(halves(relative_ref[:, lanes]), halves(orders))):
                both = jnp.concatenate([relative, order], 1)
                table[p, 128 * half : 128 * half + 32, :] = both
                for side, bucket in ((0, 31), (1, 15)):
                    start = 256 + 256 * side + 128 * half
                    table[p, start : start + 128, :] = jnp.broadcast_to(both[bucket : bucket + 1].astype(f32), (128, 256)).astype(bf16)

    document = document_ref[...]
    near = pl.multiple_of(step * 256, 256)
    queries = []
    for p in range(group):
        even, odd = halves(content_ref[:, lanes_of(p)])
        queries.append(jnp.concatenate(
            [jnp.concatenate([even, document], 1), jnp.concatenate([odd, document], 1)], 0
        ))
    for p in range(group):
        lanes = lanes_of(p)
        places = nt(jnp.concatenate([position_ref[:, lanes], ordering_ref[:, lanes]], 1), table[p]) * (0.125 * LOG2E)
        place = (places[:, :128], places[:, 128:256])
        near_scores = nt(queries[p], keys[p, pl.ds(near, NEAR), :])
        for half in range(2):
            rows = slice(BQ * half, BQ * half + BQ)
            for side in range(2):
                start = 256 + 256 * side + 128 * half
                bias[p, rows, 128 * side : 128 * side + 128] = places[:, start : start + 128]
            for quarter in range(2):
                own = slice(64 * quarter, 64 * quarter + 64)
                rows = slice(BQ * half + 64 * quarter, BQ * half + 64 * quarter + 64)
                best = None
                for tile in range(NEAR // 128):
                    if tile == 4 - 4 * quarter:
                        extra = bias[p, rows, 128 - 128 * quarter : 256 - 128 * quarter]
                    else:
                        extra = take(place[half][own], index_ref[tile, own])
                    part = near_scores[rows, 128 * tile : 128 * tile + 128] + extra
                    scores[p, rows, pl.ds(near + 128 * tile, 128)] = part
                    best = part if best is None else jnp.maximum(best, part)
                peak[p, rows, :] = best
    behind = behind_ref[step, 0]
    far = behind + ahead_ref[step, 0]

    def start_of(chunk):
        return far_start(chunk, behind, far, near)

    @pl.loop(0, (far + 1) // 2)
    def _(two):
        for chunk in (2 * two, 2 * two + 1):
            start = start_of(chunk)
            place = pl.multiple_of(jnp.where(chunk < behind, 0, 128), 128)
            for p in range(group):
                part = nt(queries[p], keys[p, pl.ds(start, CHUNK), :])
                extra = bias[p, :, pl.ds(place, 128)]
                left, right = part[:, :128] + extra, part[:, 128:] + extra
                scores[p, :, pl.ds(start, 128)] = left
                scores[p, :, pl.ds(start + 128, 128)] = right
                peak[p] = jnp.maximum(peak[p], jnp.maximum(left, right))

    tops = [jnp.max(peak[p], axis=1, keepdims=True) for p in range(group)]
    for p in range(group):
        peak[p] = jnp.broadcast_to(tops[p], (2 * BQ, 128))
        probs = jnp.exp2(scores[p, :, pl.ds(near, NEAR)] - tops[p]).astype(bf16)
        probs_ref[p, 0, :, pl.ds(near, NEAR)] = probs
        total[p] = nn(probs, values[p, pl.ds(near, NEAR), :])

    @pl.loop(0, (far + 1) // 2)
    def _(two):
        starts = [start_of(2 * two), start_of(2 * two + 1)]
        for p in range(group):
            top = peak[p]
            parts = []
            for start in starts:
                left = jnp.exp2(scores[p, :, pl.ds(start, 128)] - top).astype(bf16)
                right = jnp.exp2(scores[p, :, pl.ds(start + 128, 128)] - top).astype(bf16)
                probs = jnp.concatenate([left, right], 1)
                probs_ref[p, 0, :, pl.ds(start, CHUNK)] = probs
                parts.append(nn(probs, values[p, pl.ds(start, CHUNK), :]))
            total[p] += parts[0] + parts[1]

    for p in range(group):
        lanes = lanes_of(p)
        inverse = 1.0 / total[p, :, 128:]
        mixed = pick(total[p, :, :128] * inverse)
        inverse_ref[:, lanes] = pick(inverse)
        mixed_ref[:, lanes] = mixed
        context_ref[:, lanes] = mixed.astype(bf16)


def backward_kernel(
    group, behind_ref, ahead_ref, probs_ref, grad_ref, mixed_ref, inverse_ref, content_ref, position_ref, ordering_ref,
    key_ref, value_ref, relative_ref, order_ref, turn_ref, onehot_ref,
    query_ref, key_low_ref, value_low_ref, relative_out, order_out, sums_out,
    keys, values, table, key_total, value_total, query_total, far_total, bucket, table_total, sums,
):
    step = pl.program_id(1)
    length = key_ref.shape[0]

    @pl.when(step == 0)
    def _():
        slot = lax.broadcasted_iota(jnp.int32, (32, 128), 0)
        table[...] = jnp.zeros(table.shape, bf16)
        for p in range(group):
            lanes = lanes_of(p)
            even, odd = halves(relative_ref[:, lanes])
            table[p, 0:32, :128] = even
            table[p, 128:160, :128] = odd
            orders = jnp.where(slot == 0, order_ref[0:1, lanes].astype(f32), order_ref[1:2, lanes].astype(f32))
            even, odd = halves(jnp.where(slot < 2, orders, 0.0))
            table[p, 32:64, 128:] = even.astype(bf16)
            table[p, 160:192, 128:] = odd.astype(bf16)

        @pl.loop(0, length // 256 + 2)
        def _(piece):
            rows = pl.ds(pl.multiple_of(piece * 256, 256), 256)
            for p in range(group):
                for total in (key_total, value_total):
                    total[p, :, rows] = jnp.zeros((128, 256), f32)

        for scratch in (keys, values):
            scratch[:, :256, :] = jnp.zeros((group, 256, 128), bf16)
            scratch[:, 256 + length :, :] = jnp.zeros((group, 256, 128), bf16)

        @pl.loop(0, length // 256)
        def _(piece):
            source = pl.ds(pl.multiple_of(piece * 256, 256), 256)
            target = pl.ds(pl.multiple_of((piece + 1) * 256, 256), 256)
            for p in range(group):
                for scratch, ref in ((keys, key_ref), (values, value_ref)):
                    scratch[p, target, :] = ref[source, lanes_of(p)]

        table_total[...] = jnp.zeros(table_total.shape, f32)
        sums[...] = jnp.zeros(sums.shape, f32)

    near = pl.multiple_of(step * 256, 256)
    grads, grads_t, content_t, deltas = [], [], [], []
    for p in range(group):
        lanes = lanes_of(p)
        scaled = (grad_ref[:, lanes].astype(f32) * inverse_ref[:, lanes]).astype(bf16)
        both = jnp.concatenate(halves(scaled), 0)
        even, odd = halves(scaled.astype(f32) * mixed_ref[:, lanes])
        deltas.append(jnp.concatenate(
            [jnp.sum(even, axis=1, keepdims=True), jnp.sum(odd, axis=1, keepdims=True)], 0
        ))
        grads.append(both)
        grads_t.append(both.T)
        content_t.append(jnp.concatenate(halves(content_ref[:, lanes]), 0).T)

    def visit(p, start, size):
        probs = probs_ref[p, 0, :, pl.ds(start, size)]
        prob_grad = nt(grads[p], values[p, pl.ds(start, size), :])
        score = probs.astype(f32) * (prob_grad - deltas[p])
        score_low = score.astype(bf16)
        value_total[p, :, pl.ds(start, size)] += nn(grads_t[p], probs)
        key_total[p, :, pl.ds(start, size)] += nn(content_t[p], score_low)
        return score, nn(score_low, keys[p, pl.ds(start, size), :])

    turn = turn_ref[...]
    turns = jnp.concatenate([turn, turn], 0)
    lane = lax.broadcasted_iota(jnp.int32, (64, 128), 1)
    row = lax.broadcasted_iota(jnp.int32, (64, 128), 0)
    first = lane + 2 * row < 128
    zero = jnp.zeros((64, 128), f32)
    for p in range(group):
        score, query_total[p] = visit(p, near, NEAR)
        parts = [score[:, 128 * t : 128 * t + 128] for t in range(5)]
        tiles = [take(part, turns) for part in parts]
        for quarter in range(4):
            rows = slice(64 * quarter, 64 * quarter + 64)
            own = [tile[rows] for tile in tiles]
            if quarter % 2 == 0:
                near_parts = [jnp.where(first, own[t], own[t + 1]) for t in range(3)]
                far_total[p, 0, rows] = jnp.where(first, zero, own[0])
                far_total[p, 1, rows] = jnp.where(first, own[3], zero) + parts[4][rows]
            else:
                near_parts = [jnp.where(first, own[t + 1], own[t + 2]) for t in range(3)]
                far_total[p, 0, rows] = parts[0][rows] + jnp.where(first, zero, own[1])
                far_total[p, 1, rows] = jnp.where(first, own[4], zero)
            for t in range(3):
                bucket[p, rows, 128 * t : 128 * t + 128] = near_parts[t].astype(bf16)
    behind = behind_ref[step, 0]

    far = behind + ahead_ref[step, 0]

    @pl.loop(0, (far + 1) // 2)
    def _(two):
        for chunk in (2 * two, 2 * two + 1):
            start = far_start(chunk, behind, far, near)
            side = jnp.where(chunk < behind, 0, 1)
            for p in range(group):
                score, part = visit(p, start, CHUNK)
                query_total[p] += part
                far_total[p, side] += score[:, :128] + score[:, 128:]

    for p in range(group):
        lanes = lanes_of(p)
        folded = [far_total[p, side] + pltpu.roll(far_total[p, side], 64, 1) for side in range(2)]
        low_lane = lax.broadcasted_iota(jnp.int32, folded[0].shape, 1) < 64
        bucket[p, :, 384:] = jnp.where(low_lane, *folded).astype(bf16)
        low = (nn(bucket[p], onehot_ref[...]) * 0.125).astype(bf16)
        low = jnp.concatenate([low[:BQ], low[BQ:]], 1)
        placed = nn(low, table[p])
        content_grad = pick(query_total[p]) * 0.125
        query_ref[:, lanes] = (content_grad + placed[:, :128] + placed[:, 128:]).astype(bf16)
        table_total[p] += tn(low, jnp.concatenate([position_ref[:, lanes], ordering_ref[:, lanes]], 1))
        for j, term in enumerate((content_grad, placed[:, :128], placed[:, 128:])):
            sums[j : j + 1, lanes] += jnp.sum(term, axis=0, keepdims=True)

    @pl.when(step == pl.num_programs(1) - 1)
    def _():
        low_lane = lax.broadcasted_iota(jnp.int32, (32, 128), 1) < 64
        for p in range(group):
            lanes = lanes_of(p)
            relative_out[:, lanes] = jnp.where(low_lane, table_total[p, 0:32, :128], table_total[p, 128:160, :128])
            order_out[:, lanes] = jnp.where(low_lane[:8], table_total[p, 32:40, 128:], table_total[p, 160:168, 128:])
        sums_out[...] = sums[...]

        @pl.loop(0, length // 512)
        def _(piece):
            rows = pl.ds(pl.multiple_of(piece * 512, 512), 512)
            columns = pl.ds(pl.multiple_of(piece * 512 + 256, 256), 512)
            for p in range(group):
                key_low_ref[rows, lanes_of(p)] = (key_total[p, :, columns] * LN2).T.astype(bf16)
                value_low_ref[rows, lanes_of(p)] = value_total[p, :, columns].T.astype(bf16)


def fixed(*shape):
    return pl.BlockSpec(shape, lambda *_: (0,) * len(shape), pipeline_mode=pl.Buffered(1))


GROUP = 3


def attend(behind, ahead, content, position, ordering, keys, values, relative, order, away, document):
    rows, width = content.shape
    length = keys.shape[0]
    padded = length + 512
    pairs, blocks, group = width // 128, rows // BQ, GROUP
    wide = 128 * group
    tile = pl.BlockSpec((BQ, wide), lambda p, i, *_: (i, p))
    whole = pl.BlockSpec((length, wide), lambda p, i, *_: (0, p), pipeline_mode=pl.Buffered(1))
    return pl.pallas_call(
        functools.partial(forward_kernel, group),
        name="attend",
        out_shape=(
            jax.ShapeDtypeStruct((pairs, blocks, 2 * BQ, padded), bf16),
            jax.ShapeDtypeStruct((rows, width), bf16),
            jax.ShapeDtypeStruct((rows, width), f32),
            jax.ShapeDtypeStruct((rows, width), f32),
        ),
        grid_spec=pltpu.PrefetchScalarGridSpec(
            num_scalar_prefetch=2,
            grid=(pairs // group, blocks),
            in_specs=[
                tile, tile, tile, whole, whole,
                pl.BlockSpec((32, wide), lambda p, i, *_: (0, p)),
                pl.BlockSpec((2, wide), lambda p, i, *_: (0, p)),
                fixed(padded, 128),
                pl.BlockSpec((BQ, 128), lambda p, i, *_: (i, 0)),
            ],
            out_specs=[pl.BlockSpec((group, 1, 2 * BQ, padded), lambda p, i, *_: (p, i, 0, 0)), tile, tile, tile],
            scratch_shapes=[
                pltpu.VMEM((NEAR // 128, BQ, 128), jnp.int32),
                pltpu.VMEM((group, padded, 256), bf16),
                pltpu.VMEM((group, padded, 256), bf16),
                pltpu.VMEM((group, 768, 256), bf16),
                pltpu.VMEM((group, 2 * BQ, 256), f32),
                pltpu.VMEM((group, 2 * BQ, padded), f32),
                pltpu.VMEM((group, 2 * BQ, 128), f32),
                pltpu.VMEM((group, 2 * BQ, 256), f32),
            ],
        ),
        compiler_params=pltpu.CompilerParams(dimension_semantics=("arbitrary", "arbitrary"), vmem_limit_bytes=62 << 20),
        cost_estimate=pl.CostEstimate(flops=40 * 10**9, bytes_accessed=70 * 10**6, transcendentals=10**7),
    )(behind, ahead, content, position, ordering, keys, values, relative, order, away, document)


def attend_back(behind, ahead, probs, grad, mixed, inverse, content, position, ordering, keys, values, relative, order):
    rows, width = content.shape
    length = keys.shape[0]
    padded = length + 512
    pairs, blocks, group = width // 128, rows // BQ, GROUP
    wide = 128 * group
    tile = pl.BlockSpec((BQ, wide), lambda p, i, *_: (i, p))
    whole = pl.BlockSpec((length, wide), lambda p, i, *_: (0, p), pipeline_mode=pl.Buffered(1))
    small = lambda n: pl.BlockSpec((n, wide), lambda p, i, *_: (0, p))
    turn = (np.arange(128)[None, :] + 2 * np.arange(BQ)[:, None]) % 128
    return pl.pallas_call(
        functools.partial(backward_kernel, group),
        name="attend_back",
        out_shape=(
            jax.ShapeDtypeStruct((rows, width), bf16),
            jax.ShapeDtypeStruct((length, width), bf16),
            jax.ShapeDtypeStruct((length, width), bf16),
            jax.ShapeDtypeStruct((32, width), f32),
            jax.ShapeDtypeStruct((8, width), f32),
            jax.ShapeDtypeStruct((8, width), f32),
        ),
        grid_spec=pltpu.PrefetchScalarGridSpec(
            num_scalar_prefetch=2,
            grid=(pairs // group, blocks),
            in_specs=[
                pl.BlockSpec((group, 1, 2 * BQ, padded), lambda p, i, *_: (p, i, 0, 0)),
                tile, tile, tile, tile, tile, tile, whole, whole, small(32), small(2), fixed(BQ, 128), fixed(512, 128),
            ],
            out_specs=[tile, whole, whole, small(32), small(8), small(8)],
            scratch_shapes=[
                pltpu.VMEM((group, padded, 128), bf16),
                pltpu.VMEM((group, padded, 128), bf16),
                pltpu.VMEM((group, 256, 256), bf16),
                pltpu.VMEM((group, 128, padded), f32),
                pltpu.VMEM((group, 128, padded), f32),
                pltpu.VMEM((group, 2 * BQ, 128), f32),
                pltpu.VMEM((group, 2, 2 * BQ, 128), f32),
                pltpu.VMEM((group, 2 * BQ, 512), bf16),
                pltpu.VMEM((group, 256, 256), f32),
                pltpu.VMEM((8, wide), f32),
            ],
        ),
        compiler_params=pltpu.CompilerParams(dimension_semantics=("arbitrary", "arbitrary"), vmem_limit_bytes=62 << 20),
        cost_estimate=pl.CostEstimate(flops=80 * 10**9, bytes_accessed=70 * 10**6, transcendentals=0),
    )(behind, ahead, probs, grad, mixed, inverse, content, position, ordering, keys, values, relative, order,
      jnp.asarray(turn, jnp.int32), jnp.asarray(bucket_onehot(), bf16))


MESH = pl.DeviceIdType.MESH


class Place:
    def __init__(self, replicas, shards):
        self.replicas, self.shards = replicas, shards
        self.cores = 2 if shards % 2 == 0 else 1
        chips = shards // self.cores
        self.across = 2 if chips % 2 == 0 else 1
        self.line = chips // self.across
        self.replica = lax.axis_index("rep")
        own = lax.axis_index("shard")
        self.own = own
        self.core = lax.rem(own, self.cores)
        self.column = lax.rem(own // self.cores, self.across)
        self.spot = own // (self.cores * self.across)

    def shard(self, spot, column, core):
        return (spot * self.across + column) * self.cores + core

    def other_column(self, step):
        return lax.rem(self.column + step, self.across)

    def other_replica(self, step):
        return lax.rem(self.replica + step, self.replicas)

    def device(self, spot=None, column=None, core=None, replica=None):
        spot = self.spot if spot is None else spot
        column = self.column if column is None else column
        core = self.core if core is None else core
        replica = self.replica if replica is None else replica
        return (replica, self.shard(spot, column, core))

    def meet(self):
        barrier = pltpu.get_barrier_semaphore()

        def greet(device):
            pl.semaphore_signal(barrier, inc=1, device_id=device, device_id_type=MESH)

        fixed = 0
        if self.cores > 1:
            greet(self.device(core=1 - self.core))
            fixed += 1
        for step in range(1, self.across):
            greet(self.device(column=self.other_column(step)))
            fixed += 1
        for step in range(1, self.replicas):
            greet(self.device(replica=self.other_replica(step)))
            fixed += 1
        for step, there in ((1, self.spot < self.line - 1), (-1, self.spot > 0)):

            @pl.when(there)
            def _():
                greet(self.device(spot=self.spot + step))

        lined = (self.spot < self.line - 1).astype(jnp.int32) + (self.spot > 0).astype(jnp.int32)
        pl.semaphore_wait(barrier, fixed + lined)


def parts_of(columns, replicas):
    return replicas if columns % (128 * replicas) == 0 else 1


def columns_of(part, parts, columns):
    size = columns // parts
    return pl.ds(pl.multiple_of(part * size, 128), size)


def when(condition, action):
    if condition is True:
        action()
    else:
        pl.when(condition)(action)


def gather_kernel(replicas, shards, count, *refs):
    here = Place(replicas, shards)
    sources, wholes = refs[:count], refs[count : 2 * count]
    line_send, line_recv, cross_send, cross_recv, rep_send, rep_recv, core_send, core_recv = refs[2 * count :]
    here.meet()
    pending = []

    def send(source, whole_view, send_sem, recv_sem, device, condition=True):
        copy = pltpu.make_async_remote_copy(
            src_ref=source, dst_ref=whole_view, send_sem=send_sem, recv_sem=recv_sem, device_id=device, device_id_type=MESH
        )
        when(condition, copy.start)
        pending.append((condition, copy.wait_send))

    def arrived(view, recv_sem, condition=True):
        copy = pltpu.make_async_remote_copy(
            src_ref=view, dst_ref=view, send_sem=recv_sem, recv_sem=recv_sem, device_id=here.device(), device_id_type=MESH
        )
        when(condition, copy.wait_recv)

    def view(k, spot, column, core, part=None):
        whole = wholes[k].at[here.shard(spot, column, core)]
        if part is None:
            return whole
        columns = whole.shape[1]
        return whole.at[:, columns_of(part, parts_of(columns, replicas), columns)]

    def spread(k, spot, condition, own=False):
        columns = wholes[k].shape[2]
        parts = parts_of(columns, replicas)
        part = here.replica if parts > 1 else 0
        target = view(k, spot, here.column, here.core)
        source = sources[k] if own else target
        for step in range(1, here.across):
            cut = columns_of(part, parts, columns)
            send(source.at[:, cut], target.at[:, cut], cross_send.at[k, step, spot], cross_recv.at[k, here.column, spot],
                 here.device(column=here.other_column(step)), condition)
        if here.cores > 1:
            send(source, target, core_send.at[k, 0, here.column, spot], core_recv.at[k, 0, here.column, spot],
                 here.device(core=1 - here.core), condition)

    def crossed(k, spot, condition):
        columns = wholes[k].shape[2]
        parts = parts_of(columns, replicas)
        part = here.replica if parts > 1 else 0
        for step in range(1, here.across):
            column = here.other_column(step)
            piece = view(k, spot, column, here.core, part)
            arrived(piece, cross_recv.at[k, column, spot], condition)
            if parts > 1:
                for hop in range(1, replicas):
                    send(piece, piece, rep_send.at[k, hop, column, spot], rep_recv.at[k, here.replica, column, spot],
                         here.device(replica=here.other_replica(hop)), condition)
            if here.cores > 1:
                send(piece, piece, core_send.at[k, 1, column, spot], core_recv.at[k, 1, column, spot],
                     here.device(core=1 - here.core), condition)

    def replicated(k, spot, condition):
        parts = parts_of(wholes[k].shape[2], replicas)
        if parts == 1:
            return
        for step in range(1, here.across):
            column = here.other_column(step)
            for hop in range(1, replicas):
                replica = here.other_replica(hop)
                piece = view(k, spot, column, here.core, replica)
                arrived(piece, rep_recv.at[k, replica, column, spot], condition)
                if here.cores > 1:
                    send(piece, piece, core_send.at[k, 1 + hop, column, spot], core_recv.at[k, 1 + hop, column, spot],
                         here.device(core=1 - here.core), condition)

    def at(distance, action):
        for k in range(count):
            if distance == 0:
                action(k, here.spot, True)
            else:
                action(k, here.spot - distance, here.spot >= distance)
                action(k, here.spot + distance, here.spot + distance < here.line)

    for k in range(count):
        own = view(k, here.spot, here.column, here.core)
        send(sources[k], own, line_send.at[k, 0, here.spot], line_recv.at[k, here.spot],
             here.device(spot=here.spot + 1), here.spot < here.line - 1)
        send(sources[k], own, line_send.at[k, 1, here.spot], line_recv.at[k, here.spot],
             here.device(spot=here.spot - 1), here.spot > 0)
        spread(k, here.spot, True, own=True)
    for k in range(count):
        wholes[k][here.own] = sources[k][...]

    def along(distance):
        for k in range(count):
            for sign in (-1, 1):
                spot = here.spot + sign * distance
                condition = (spot >= 0) & (spot < here.line)
                piece = view(k, spot, here.column, here.core)
                arrived(piece, line_recv.at[k, spot], condition)
                onward = here.spot - sign
                send(piece, piece, line_send.at[k, 0 if sign < 0 else 1, spot], line_recv.at[k, spot],
                     here.device(spot=onward), condition & (onward >= 0) & (onward < here.line))
                spread(k, spot, condition)

    for distance in range(here.line + 2):
        if 1 <= distance < here.line:
            along(distance)
        if 1 <= distance <= here.line:
            at(distance - 1, crossed)
        if 2 <= distance:
            at(distance - 2, replicated)
    if here.cores > 1:
        for k in range(count):
            columns = wholes[k].shape[2]
            parts = parts_of(columns, replicas)
            for spot in range(here.line):
                other = 1 - here.core
                arrived(view(k, spot, here.column, other), core_recv.at[k, 0, here.column, spot])
                for step in range(1, here.across):
                    column = here.other_column(step)
                    part = here.replica if parts > 1 else 0
                    arrived(view(k, spot, column, other, part), core_recv.at[k, 1, column, spot])
                    for hop in range(1, replicas if parts > 1 else 1):
                        arrived(view(k, spot, column, other, here.other_replica(hop)), core_recv.at[k, 1 + hop, column, spot])
    for condition, wait in pending:
        when(condition, wait)


def gather(mesh, arrays, collective_id):
    replicas, shards = mesh.shape["rep"], mesh.shape["shard"]
    count = len(arrays)
    line = shards // 4
    dma = pltpu.SemaphoreType.DMA
    vmem = pl.BlockSpec(memory_space=pltpu.VMEM)
    moved = sum(a.size * 2 * shards for a in arrays)
    return pl.pallas_call(
        functools.partial(gather_kernel, replicas, shards, count),
        name="gather",
        out_shape=[jax.ShapeDtypeStruct((shards,) + a.shape, a.dtype) for a in arrays],
        in_specs=[vmem] * count,
        out_specs=[vmem] * count,
        scratch_shapes=[
            dma((count, 2, line)), dma((count, line)),
            dma((count, 2, line)), dma((count, 2, line)),
            dma((count, replicas, 2, line)), dma((count, replicas, 2, line)),
            dma((count, replicas + 1, 2, line)), dma((count, replicas + 1, 2, line)),
        ],
        compiler_params=pltpu.CompilerParams(collective_id=collective_id, has_side_effects=True, vmem_limit_bytes=56 << 20),
        cost_estimate=pl.CostEstimate(flops=0, bytes_accessed=moved * 4, transcendentals=0),
    )(*arrays)


WORK_INPUTS = ("key_low", "value_low", "query_low", "sum_grad", "mix", "weight")


def scatter_kernel(replicas, shards, count, chunks, extra, work, *refs):
    here = Place(replicas, shards)
    take = lambda number: [refs_left.pop(0) for _ in range(number)]
    refs_left = list(refs)
    sources, extras, work_in = take(count), take(extra), take(len(WORK_INPUTS))
    outs, extra_outs, (tokens_grad,) = take(count), take(extra), take(1)
    own_bufs, core_bufs, rep_bufs, cross_bufs, line_bufs, last_bufs = (take(count) for _ in range(6))
    extra_bufs = take(extra)
    work_bufs, (block_buf, own_sems, work_sems, block_sems) = take(len(WORK_INPUTS)), take(4)
    (core_send, core_recv, rep_send, rep_recv, cross_send, cross_recv, line_send, line_recv, last_send, last_recv) = refs_left
    local = []
    for j, (k, low, size) in enumerate(chunks):
        for column in range(here.across):
            cut = pl.ds(low, size)
            local.append(pltpu.make_async_copy(
                sources[k].at[:, column, here.core, :, cut], own_bufs[k].at[column, :, :, cut], own_sems.at[j, column]
            ))
    here.meet()
    pending = []

    def send(source, target, send_sem, recv_sem, device, condition=True):
        copy = pltpu.make_async_remote_copy(
            src_ref=source, dst_ref=target, send_sem=send_sem, recv_sem=recv_sem, device_id=device, device_id_type=MESH
        )
        when(condition, copy.start)
        pending.append((condition, copy.wait_send))

    def arrived(view, recv_sem, condition=True):
        copy = pltpu.make_async_remote_copy(
            src_ref=view, dst_ref=view, send_sem=recv_sem, recv_sem=recv_sem, device_id=here.device(), device_id_type=MESH
        )
        when(condition, copy.wait_recv)

    def add(target, source):
        target[...] = target[...] + source[...]

    steps = range(1, here.across)
    hops = range(1, replicas)

    def split(j):
        return parts_of(chunks[j][2], replicas)

    def columns(j, part=None):
        _, low, size = chunks[j]
        if part is None or split(j) == 1:
            return pl.ds(low, size)
        size = size // replicas
        return pl.ds(pl.multiple_of(low + part * size, 128), size)

    def compact(j):
        _, low, size = chunks[j]
        return pl.ds(low // split(j), size // split(j))

    def mixed(j, column):
        k = chunks[j][0]
        mine = core_bufs[k].at[column, :, :, columns(j)]
        own = own_bufs[k].at[column, :, :, columns(j)]
        _, low, size = chunks[j]
        cut = pl.ds(low, size)
        pltpu.make_async_copy(
            sources[k].at[:, column, here.core, :, cut], own_bufs[k].at[column, :, :, cut], own_sems.at[j, column]
        ).wait()
        if here.cores > 1:
            arrived(mine, core_recv.at[j, column])
            add(mine, own)
        else:
            mine[...] = own[...]

    def stage_rep(j):
        k = chunks[j][0]
        for step in steps:
            column = here.other_column(step)
            mixed(j, column)
            if split(j) > 1:
                for hop in hops:
                    replica = here.other_replica(hop)
                    send(core_bufs[k].at[column, :, :, columns(j, replica)], rep_bufs[k].at[hop - 1, step - 1, :, :, compact(j)],
                         rep_send.at[j, hop, step], rep_recv.at[j, hop, step], here.device(replica=replica))

    def stage_cross(j):
        k = chunks[j][0]
        for step in steps:
            column = here.other_column(step)
            mine = core_bufs[k].at[column, :, :, columns(j, here.replica)]
            if split(j) > 1:
                for hop in hops:
                    piece = rep_bufs[k].at[hop - 1, step - 1, :, :, compact(j)]
                    arrived(piece, rep_recv.at[j, hop, step])
                    add(mine, piece)
            send(mine, cross_bufs[k].at[step - 1, :, :, compact(j)], cross_send.at[j, step], cross_recv.at[j, step],
                 here.device(column=column))
        mixed(j, here.column)

    def stage_line(distance, j):
        k = chunks[j][0]
        if distance == here.line - 1:
            for step in steps:
                piece = cross_bufs[k].at[step - 1, :, :, compact(j)]
                arrived(piece, cross_recv.at[j, step])
                add(core_bufs[k].at[here.column, :, :, columns(j, here.replica)], piece)
        for sign, way in ((1, 0), (-1, 1)):
            target = here.spot + sign * distance
            inside = (target >= 0) & (target < here.line)
            before = here.spot - sign
            fed = inside & (before >= 0) & (before < here.line)
            mine = core_bufs[k].at[here.column, target, :, columns(j)]
            piece = line_bufs[k].at[way, target, :, columns(j)]
            arrived(piece, line_recv.at[j, way, target], fed)
            when(fed, functools.partial(add, mine, piece))
            send(mine, piece, line_send.at[j, way, target], line_recv.at[j, way, target],
                 here.device(spot=here.spot + sign), inside)

    def stage_last(j):
        k = chunks[j][0]
        mine = core_bufs[k].at[here.column, here.spot, :, columns(j)]
        for sign, way in ((1, 0), (-1, 1)):
            before = here.spot - sign
            fed = (before >= 0) & (before < here.line)
            piece = line_bufs[k].at[way, here.spot, :, columns(j)]
            arrived(piece, line_recv.at[j, way, here.spot], fed)
            when(fed, functools.partial(add, mine, piece))
        for hop in hops:
            send(mine, last_bufs[k].at[here.replica, :, columns(j)], last_send.at[j, hop], last_recv.at[j, here.replica],
                 here.device(replica=here.other_replica(hop)))

    def finish(own, buffer, out, semaphore, cut):
        for hop in hops:
            replica = here.other_replica(hop)
            arrived(buffer.at[replica, :, cut], semaphore.at[replica])
        result = None
        for replica in range(replicas):
            term = jnp.where(here.replica == replica, own[...].astype(f32), buffer[replica, :, cut].astype(f32))
            result = term if result is None else result + term
        out[:, cut] = result

    def stage_finish(j):
        k = chunks[j][0]
        finish(core_bufs[k].at[here.column, here.spot, :, columns(j)], last_bufs[k], outs[k], last_recv.at[j], columns(j))

    if here.cores > 1:
        for j, (k, _, _) in enumerate(chunks):
            for step in (*steps, 0):
                column = here.other_column(step)
                send(sources[k].at[:, column, 1 - here.core, :, columns(j)], core_bufs[k].at[column, :, :, columns(j)],
                     core_send.at[j, column], core_recv.at[j, column], here.device(core=1 - here.core))
    for copy in local:
        copy.start()
    loads = [pltpu.make_async_copy(ref, buf, work_sems.at[i]) for i, (ref, buf) in enumerate(zip(work_in, work_bufs))]
    for copy in loads:
        copy.start()
    size = block_buf.shape[1]
    blocks = tokens_grad.shape[0] // size

    def stored(b, slot):
        return pltpu.make_async_copy(block_buf.at[slot], tokens_grad.at[pl.ds(pl.multiple_of(b * size, size), size)], block_sems.at[slot])

    def pair(turn):
        if turn == 0:
            for copy in loads:
                copy.wait()

        @pl.loop(0, 2)
        def _(slot):
            b = 2 * turn + slot
            if turn > 0:
                stored(b - 2, slot).wait()
            block_buf[slot] = work(b, *work_bufs)
            stored(b, slot).start()

    stages = [stage_rep, stage_cross]
    stages += [functools.partial(stage_line, distance) for distance in range(here.line - 1, 0, -1)]
    stages += [stage_last, stage_finish]
    total = len(chunks)
    for time in range(total + len(stages) - 1):
        for place in reversed(range(len(stages))):
            if 0 <= time - place < total:
                stages[place](time - place)
        if time == 0:
            for e in range(extra):
                for hop in hops:
                    send(extras[e], extra_bufs[e].at[here.replica], last_send.at[total + e, hop],
                         last_recv.at[total + e, here.replica], here.device(replica=here.other_replica(hop)))
        elif time % 2 == 1 and time < blocks:
            pair(time // 2)
    for turn in range((total + len(stages) - 1) // 2, blocks // 2):
        pair(turn)
    for slot in range(2):
        stored(blocks - 2 + slot, slot).wait()
    for e in range(extra):
        finish(extras[e], extra_bufs[e], extra_outs[e], last_recv.at[total + e], pl.ds(0, extras[e].shape[1]))
    for condition, wait in pending:
        when(condition, wait)


def scatter(mesh, arrays, widths, extras, inputs, work, collective_id):
    replicas, shards = mesh.shape["rep"], mesh.shape["shard"]
    count, extra = len(arrays), len(extras)
    dma = pltpu.SemaphoreType.DMA
    vmem = pl.BlockSpec(memory_space=pltpu.VMEM)
    cores = across = 2
    line = shards // (cores * across)
    shapes = [a.shape[1:] for a in arrays]
    chunks = [
        (k, low, min(width, shapes[k][1])) for k, width in enumerate(widths) for low in range(0, shapes[k][1], min(width, shapes[k][1]))
    ]
    cuts = [(shapes[k][0], shapes[k][1] // parts_of(min(width, shapes[k][1]), replicas)) for k, width in enumerate(widths)]
    moved = sum(a.size * 2 for a in arrays)
    number = len(chunks)
    rows = inputs[0].shape[0]
    size = min(rows, 256)
    anywhere = pl.BlockSpec(memory_space=pl.ANY)
    buffers = (
        [pltpu.VMEM((across, line) + s, bf16) for s in shapes]
        + [pltpu.VMEM((across, line) + s, bf16) for s in shapes]
        + [pltpu.VMEM((replicas - 1, across - 1, line) + s, bf16) for s in cuts]
        + [pltpu.VMEM((across - 1, line) + s, bf16) for s in cuts]
        + [pltpu.VMEM((2, line) + s, bf16) for s in shapes]
        + [pltpu.VMEM((replicas,) + s, bf16) for s in shapes]
        + [pltpu.VMEM((replicas,) + e.shape, bf16) for e in extras]
        + [pltpu.VMEM(i.shape, i.dtype) for i in inputs]
        + [pltpu.VMEM((2, size, inputs[0].shape[1]), f32), dma((number, across)), dma((len(inputs),)), dma((2,))]
    )
    return pl.pallas_call(
        functools.partial(scatter_kernel, replicas, shards, count, chunks, extra, work),
        name="scatter",
        out_shape=(
            [jax.ShapeDtypeStruct(s, f32) for s in shapes]
            + [jax.ShapeDtypeStruct(e.shape, f32) for e in extras]
            + [jax.ShapeDtypeStruct(inputs[0].shape, f32)]
        ),
        in_specs=[anywhere] * count + [vmem] * extra + [anywhere] * len(inputs),
        out_specs=[vmem] * (count + extra) + [anywhere],
        scratch_shapes=buffers + [
            dma((number, across)), dma((number, across)),
            dma((number, replicas, across)), dma((number, replicas, across)),
            dma((number, across)), dma((number, across)),
            dma((number, 2, line)), dma((number, 2, line)),
            dma((number + extra, replicas)), dma((number + extra, replicas)),
        ],
        compiler_params=pltpu.CompilerParams(collective_id=collective_id, has_side_effects=True, vmem_limit_bytes=62 << 20),
        cost_estimate=pl.CostEstimate(flops=0, bytes_accessed=moved * 4, transcendentals=0),
    )(*[a.reshape((line, across, cores) + a.shape[1:]) for a in arrays], *extras, *inputs)


FIRST_VECTOR = 34
VMEM_ALL = 62 << 20


def place_of(rows):
    return lax.broadcasted_iota(jnp.int32, (rows, 2 * rows), 1) - 2 * lax.broadcasted_iota(jnp.int32, (rows, 2 * rows), 0)


def mixing(own, rest):
    place = place_of(own.shape[0])
    return jnp.where(place == 0, own, jnp.where(place == 1, rest, 0.0)).astype(bf16)


def project_kernel(
    tokens_ref, hot_ref, weight_ref, small_ref,
    pooled_ref, content_ref, position_ref, ordering_ref, key_ref, value_ref, document_ref, mix_ref,
):
    width = tokens_ref.shape[1]
    rows = pooled_ref.shape[0]
    tokens = tokens_ref[...]
    place = place_of(rows)
    first, second = (nn(jnp.where(place == j, 1.0, 0.0).astype(bf16), hot_ref[...]) for j in range(2))
    document_ref[...] = first.astype(bf16)
    own = 1.0 / (1.0 + jnp.sum(first * second, axis=1, keepdims=True))
    mix_ref[...] = jnp.broadcast_to(own, mix_ref.shape)
    pooled = nn(mixing(own, 1.0 - own), tokens)
    pooled_ref[...] = pooled
    key_ref[...] = nn(tokens, weight_ref[:, width : 2 * width]).astype(bf16)
    value_ref[...] = nn(tokens, weight_ref[:, 2 * width :]).astype(bf16)
    queries = nn(pooled.astype(bf16), weight_ref[:, :width])
    bias = small_ref[2:5, :].astype(f32)
    content_ref[...] = ((queries + bias[0:1]) * (0.125 * LOG2E)).astype(bf16)
    position_ref[...] = (queries + bias[1:2]).astype(bf16)
    ordering_ref[...] = (queries + bias[2:3]).astype(bf16)


def project(tokens, hot, weight, small):
    length, width = tokens.shape
    block = 256
    steps = length // block
    whole = lambda n: pl.BlockSpec((block, n), lambda i: (i, 0))
    half = lambda n: pl.BlockSpec((block // 2, n), lambda i: (i, 0))
    rows = jax.ShapeDtypeStruct((length // 2, width), bf16)
    full = jax.ShapeDtypeStruct((length, width), bf16)
    narrow = lambda kind: jax.ShapeDtypeStruct((length // 2, 128), kind)
    return pl.pallas_call(
        project_kernel,
        name="project",
        grid=(steps,),
        out_shape=(jax.ShapeDtypeStruct((length // 2, width), f32), rows, rows, rows, full, full, narrow(bf16), narrow(f32)),
        in_specs=[whole(width), whole(128), fixed(*weight.shape), fixed(*small.shape)],
        out_specs=[half(width)] * 4 + [whole(width)] * 2 + [half(128)] * 2,
        compiler_params=pltpu.CompilerParams(vmem_limit_bytes=VMEM_ALL),
        cost_estimate=pl.CostEstimate(flops=5 * length * width * width, bytes_accessed=10 * length * width, transcendentals=0),
    )(tokens, hot, weight, small)


def mean(values):
    return jnp.mean(values, axis=1, keepdims=True)


def normalize(values):
    centered = values - mean(values)
    inverse = lax.rsqrt(mean(centered * centered) + 1e-05)
    return centered * inverse, inverse


def norm_back(grad, normed, inverse):
    return inverse * (grad - mean(grad) - normed * mean(grad * normed))


def column_sum(values):
    return jnp.sum(values, axis=0, keepdims=True)


def middle_kernel(
    blocks, context_ref, pooled_ref, cotangent_ref, wide_ref, outer_ref, small_ref, bias_ref,
    layer_ref, sum_ref, context_grad_ref, sums_ref, inner_sums_ref, output_out, inner_out, outer_out,
    act, back, slope, first_all, outer_all, attended_all, context_all,
):
    step = pl.program_id(0)
    size, width = pooled_ref.shape
    hidden = bias_ref.shape[1]
    chunks = [slice(c * width, (c + 1) * width) for c in range(hidden // width)]

    @pl.when(step == 0)
    def _():
        sums_ref[...] = jnp.zeros(sums_ref.shape, f32)
        inner_sums_ref[...] = jnp.zeros(inner_sums_ref.shape, f32)

    @pl.when(step < blocks)
    def _():
        rows = pl.ds(pl.multiple_of(step * size, size), size)

        def vector(j):
            return small_ref[2 + j : 3 + j, :].astype(f32)

        context = context_ref[...]
        context_all[rows, :] = context
        first_norm, first_inverse = normalize(pooled_ref[...] + nn(context, wide_ref[:, :width]))
        first = first_norm * vector(3) + vector(4)
        first_low = first.astype(bf16)
        first_all[rows, :] = first_low
        outer = None
        for cut in chunks:
            inner = nn(first_low, wide_ref[:, width + cut.start : width + cut.stop]) + bias_ref[:, cut].astype(f32)
            cumulative = 0.5 * (1.0 + lax.erf(inner * math.sqrt(0.5)))
            act_low = (inner * cumulative).astype(bf16)
            act[rows, cut] = act_low
            slope[:, cut] = cumulative + inner * (jnp.exp(-0.5 * inner * inner) * (1.0 / math.sqrt(2.0 * math.pi)))
            part = nn(act_low, outer_ref[cut, :])
            outer = part if outer is None else outer + part
        second_norm, second_inverse = normalize(first + outer + vector(5))
        layer_ref[...] = (second_norm * vector(6) + vector(7)).astype(bf16)
        cotangent = cotangent_ref[...].astype(f32)
        mid_grad = norm_back(cotangent * vector(6), second_norm, second_inverse)
        outer_low = mid_grad.astype(bf16)
        outer_all[rows, :] = outer_low
        first_grad = mid_grad
        for cut in chunks:
            inner_grad = nt(outer_low, outer_ref[cut, :]) * slope[:, cut]
            inner_low = inner_grad.astype(bf16)
            back[rows, cut] = inner_low
            inner_sums_ref[0:1, cut] += column_sum(inner_low.astype(f32))
            first_grad = first_grad + nt(inner_low, wide_ref[:, width + cut.start : width + cut.stop])
        sum_grad = norm_back(first_grad * vector(3), first_norm, first_inverse)
        sum_ref[...] = sum_grad
        attended_low = sum_grad.astype(bf16)
        attended_all[rows, :] = attended_low
        context_grad_ref[...] = nt(attended_low, wide_ref[:, :width]).astype(bf16)
        for j, term in enumerate(
            (first_grad * first_norm, first_grad, outer_low.astype(f32), cotangent * second_norm, cotangent)
        ):
            sums_ref[j : j + 1, :] += column_sum(term)

    @pl.when((step >= blocks) & (step < blocks + len(chunks)))
    def _():
        cut = pl.ds(pl.multiple_of((step - blocks) * width, width), width)
        outer_out[...] = tn(act[:, cut], outer_all[...]).astype(bf16)
        inner_out[...] = tn(first_all[...], back[:, cut]).astype(bf16)

    @pl.when(step == blocks + len(chunks))
    def _():
        output_out[...] = tn(context_all[...], attended_all[...]).astype(bf16)


def middle(context, pooled, cotangent, wide, outer, small, bias):
    rows, width = context.shape
    hidden = bias.shape[1]
    size = 256
    blocks, chunks = rows // size, hidden // width
    block = pl.BlockSpec((size, width), lambda i: (jnp.minimum(i, blocks - 1), 0))
    chunk = lambda i: jnp.clip(i - blocks, 0, chunks - 1)
    low = jax.ShapeDtypeStruct((rows, width), bf16)
    flops = 18 * rows * width * hidden
    return pl.pallas_call(
        functools.partial(middle_kernel, blocks),
        name="middle",
        grid=(blocks + chunks + 1,),
        out_shape=(
            low,
            jax.ShapeDtypeStruct((rows, width), f32),
            low,
            jax.ShapeDtypeStruct((8, width), f32),
            jax.ShapeDtypeStruct((8, hidden), f32),
            jax.ShapeDtypeStruct((width, width), bf16),
            jax.ShapeDtypeStruct((width, hidden), bf16),
            jax.ShapeDtypeStruct((hidden, width), bf16),
        ),
        in_specs=[block, block, block, fixed(*wide.shape), fixed(*outer.shape), fixed(*small.shape), fixed(*bias.shape)],
        out_specs=[
            block, block, block, fixed(8, width), fixed(8, hidden), fixed(width, width),
            pl.BlockSpec((width, width), lambda i: (0, chunk(i))),
            pl.BlockSpec((width, width), lambda i: (chunk(i), 0)),
        ],
        scratch_shapes=[
            pltpu.VMEM((rows, hidden), bf16),
            pltpu.VMEM((rows, hidden), bf16),
            pltpu.VMEM((size, hidden), f32),
            pltpu.VMEM((rows, width), bf16),
            pltpu.VMEM((rows, width), bf16),
            pltpu.VMEM((rows, width), bf16),
            pltpu.VMEM((rows, width), bf16),
        ],
        compiler_params=pltpu.CompilerParams(vmem_limit_bytes=60 << 20),
        cost_estimate=pl.CostEstimate(flops=flops, bytes_accessed=40 * rows * width, transcendentals=2 * rows * hidden),
    )(context, pooled, cotangent, wide, outer, small, bias)


def tail_kernel(tokens_ref, key_ref, value_ref, query_ref, pooled_ref, weight_grad_ref, total):
    step = pl.program_id(0)
    width = tokens_ref.shape[1]

    @pl.when(step == 0)
    def _():
        total[...] = jnp.zeros(total.shape, f32)

    tokens = tokens_ref[...]
    total[:, :width] += tn(pooled_ref[...].astype(bf16), query_ref[...])
    total[:, width : 2 * width] += tn(tokens, key_ref[...])
    total[:, 2 * width :] += tn(tokens, value_ref[...])

    @pl.when(step == pl.num_programs(0) - 1)
    def _():
        weight_grad_ref[...] = total[...].astype(bf16)


def tail(tokens, key_low, value_low, query_low, pooled):
    length, width = tokens.shape
    block = 512
    whole = pl.BlockSpec((block, width), lambda i: (i, 0))
    half = pl.BlockSpec((block // 2, width), lambda i: (i, 0))
    return pl.pallas_call(
        tail_kernel,
        name="tail",
        grid=(length // block,),
        out_shape=jax.ShapeDtypeStruct((width, 3 * width), bf16),
        in_specs=[whole, whole, whole, half, half],
        out_specs=fixed(width, 3 * width),
        scratch_shapes=[pltpu.VMEM((width, 3 * width), f32)],
        compiler_params=pltpu.CompilerParams(vmem_limit_bytes=VMEM_ALL),
        cost_estimate=pl.CostEstimate(flops=5 * length * width * width, bytes_accessed=8 * length * width, transcendentals=0),
    )(tokens, key_low, value_low, query_low, pooled)


def tokens_block(block, key_ref, value_ref, query_ref, sum_ref, mix_ref, weight_ref):
    width = key_ref.shape[1]
    whole, half = (pl.ds(pl.multiple_of(block * rows, rows), rows) for rows in (256, 128))
    pooled_grad = sum_ref[half, :] + nt(query_ref[half, :], weight_ref[:, :width])
    coarse = pooled_grad.astype(bf16)
    fine = (pooled_grad - coarse.astype(f32)).astype(bf16)
    own = mix_ref[half, :1]
    mix = mixing(own, 1.0 - own)
    return (
        tn(mix, coarse) + tn(mix, fine)
        + nt(key_ref[whole, :], weight_ref[:, width : 2 * width])
        + nt(value_ref[whole, :], weight_ref[:, 2 * width :])
    )


def pack_kernel(count, folds, *refs):
    squares, (output_ref, inner_ref, relative_ref, order_ref) = refs[:3], refs[3:7]
    vectors, bias_ref = refs[7 : 7 + count], refs[7 + count]
    wide_ref, small_ref, projections_ref = refs[8 + count :]
    width = output_ref.shape[1]
    each = relative_ref.shape[1]
    for j, ref in enumerate(squares):
        projections_ref[:, j * width : (j + 1) * width] = ref[...]
    wide_ref[:, :width] = output_ref[...]
    wide_ref[:, width:] = inner_ref[...]
    small_ref[...] = jnp.zeros(small_ref.shape, bf16)
    rows = [relative_ref[...].astype(f32), order_ref[...].astype(f32)]
    rows += [ref[...].astype(f32).reshape(1, each) for ref in vectors]
    bias = bias_ref[...].astype(f32).reshape(1, folds * each)
    rows += [bias[:, j * each : (j + 1) * each] for j in range(folds)]
    small_ref[: FIRST_VECTOR + count + folds, :each] = jnp.concatenate(rows, 0).astype(bf16)


def pack(squares, output, inner, relative, order, vectors, bias, folds):
    rows = -(-(FIRST_VECTOR + len(vectors) + folds) // 16) * 16
    return pl.pallas_call(
        functools.partial(pack_kernel, len(vectors), folds),
        name="pack",
        out_shape=(
            jax.ShapeDtypeStruct((output.shape[0], output.shape[1] + inner.shape[1]), bf16),
            jax.ShapeDtypeStruct((rows, 128), bf16),
            jax.ShapeDtypeStruct((output.shape[0], 3 * output.shape[1]), bf16),
        ),
        cost_estimate=pl.CostEstimate(flops=0, bytes_accessed=4 * inner.size, transcendentals=0),
    )(*squares, output, inner, relative, order, *vectors, bias)


def finish_kernel(count, folds, projection_ref, output_ref, inner_ref, outer_ref, small_ref, *outs):
    width = output_ref.shape[1]
    squares, (output_out, inner_out, outer_out, relative_out, order_out) = outs[:3], outs[3:8]
    vectors, bias_out = outs[8 : 8 + count], outs[8 + count]
    each = relative_out.shape[1]
    for j, ref in enumerate(squares):
        ref[...] = projection_ref[:, j * width : (j + 1) * width]
    output_out[...] = output_ref[...]
    inner_out[...] = inner_ref[...]
    outer_out[...] = outer_ref[...]
    small = small_ref[...]
    relative_out[...] = small[:32, :each]
    order_out[...] = small[32:34, :each]
    for j, ref in enumerate(vectors):
        ref[...] = small[FIRST_VECTOR + j, :each]
    start = FIRST_VECTOR + count
    bias_out[...] = jnp.concatenate([small[start + j : start + j + 1, :each] for j in range(folds)], 1).reshape(folds * each)


def finish(projection, output, inner, outer, small, count, folds):
    each, width = small.shape[0], output.shape[1]
    rows = output.shape[0]
    shape = lambda *s: jax.ShapeDtypeStruct(s, f32)
    return pl.pallas_call(
        functools.partial(finish_kernel, count, folds),
        name="finish",
        out_shape=(
            [shape(rows, width)] * 4 + [shape(*inner.shape), shape(*outer.shape), shape(32, rows), shape(2, rows)]
            + [shape(rows)] * count + [shape(folds * rows)]
        ),
        cost_estimate=pl.CostEstimate(flops=0, bytes_accessed=8 * inner.size, transcendentals=0),
    )(projection, output, inner, outer, small)


def unpack_kernel(shards, folds, start, small_ref, segment_ref, relative_out, order_out, vectors_out, bias_out, hot_out, away_out, behind_out, ahead_out):
    each = relative_out.shape[1] // shards
    length = segment_ref.shape[1]
    own = [small_ref[s].astype(f32) for s in range(shards)]
    whole = jnp.concatenate([piece[:start, :each] for piece in own], 1).astype(bf16)
    relative_out[...] = whole[:32]
    order_out[...] = whole[32:34]
    vectors_out[: start - 32, :] = whole[32:]
    bias_out[...] = jnp.concatenate(
        [piece[start + j : start + j + 1, :each] for piece in own for j in range(folds)], 1
    ).astype(bf16)
    document = lax.broadcasted_iota(jnp.int32, (128, length), 0)
    same = jnp.where(segment_ref[...] == document, 1.0, 0.0).T
    counted = lax.broadcasted_iota(jnp.int32, same.shape, 1) < 8
    hot_out[...] = same.astype(bf16)
    away_out[256 : 256 + length, :] = jnp.where(counted, -BIG * (1.0 - same), 0.0).astype(bf16)
    pad = jnp.where(counted[:256], -BIG, 0.0).astype(bf16)
    away_out[:256, :] = pad
    away_out[256 + length :, :] = pad
    blocks = behind_out.shape[0]
    own_row = jnp.broadcast_to(segment_ref[...], (blocks, length))
    lane = lax.broadcasted_iota(jnp.int32, (blocks, length), 1)
    start = 2 * BQ * lax.broadcasted_iota(jnp.int32, (blocks, length), 0)
    total = lambda values: jnp.sum(values, axis=1, keepdims=True)
    at = lambda place: total(jnp.where(lane == place, own_row, 0))
    first = total(jnp.where(own_row < at(start), 1, 0))
    last = total(jnp.where(own_row <= at(start + 2 * BQ - 2), 1, 0))
    chunks = lambda rest: lax.shift_right_logical(jnp.maximum(rest + CHUNK - 1, 0), CHUNK.bit_length() - 1)
    behind_out[...] = chunks(start[:, :128] - 256 - first)
    ahead_out[...] = chunks(last - (start[:, :128] - 256 + NEAR))


def unpack(small, segments, width, count, folds):
    shards = small.shape[0]
    length = segments.shape[1]
    start = FIRST_VECTOR + count
    shape = lambda *s: jax.ShapeDtypeStruct(s, bf16)
    return pl.pallas_call(
        functools.partial(unpack_kernel, shards, folds, start),
        name="unpack",
        out_shape=(shape(32, width), shape(2, width), shape(16, width), shape(1, folds * width), shape(length, 128), shape(length + 512, 128))
        + (jax.ShapeDtypeStruct((length // (2 * BQ), 128), jnp.int32),) * 2,
        compiler_params=pltpu.CompilerParams(vmem_limit_bytes=VMEM_ALL),
        cost_estimate=pl.CostEstimate(flops=0, bytes_accessed=1 << 20, transcendentals=0),
    )(small, segments)


def collect_kernel(folds, relative_ref, order_ref, bias_ref, sums_ref, inner_ref, out_ref):
    shards, rows, _ = out_ref.shape
    width = relative_ref.shape[1]
    each = width // shards
    whole = jnp.concatenate([relative_ref[...], order_ref[:2], bias_ref[:3], sums_ref[:5]], 0)
    inner = inner_ref[0:1, :]
    out_ref[...] = jnp.zeros(out_ref.shape, bf16)
    for s in range(shards):
        cut = slice(s * each, s * each + each)
        own = [inner[:, (s * folds + j) * each : (s * folds + j + 1) * each] for j in range(folds)]
        piece = jnp.concatenate([whole[:, cut], *own], 0)
        out_ref[s, : piece.shape[0], :each] = piece.astype(bf16)


def collect(relative, order, bias, sums, inner, shards, count, folds):
    rows = -(-(FIRST_VECTOR + count + folds) // 16) * 16
    return pl.pallas_call(
        functools.partial(collect_kernel, folds),
        name="collect",
        out_shape=jax.ShapeDtypeStruct((shards, rows, 128), bf16),
        compiler_params=pltpu.CompilerParams(vmem_limit_bytes=VMEM_ALL),
        cost_estimate=pl.CostEstimate(flops=0, bytes_accessed=1 << 19, transcendentals=0),
    )(relative, order, bias, sums, inner)


def body(
    mesh,
    tokens,
    segment_ids,
    query_weight,
    key_weight,
    value_weight,
    output_weight,
    relative_table,
    order_table,
    content_bias,
    position_bias,
    order_bias,
    first_gain,
    first_shift,
    inner_weight,
    inner_bias,
    outer_weight,
    outer_bias,
    second_gain,
    second_shift,
    cotangent,
):
    shards = mesh.shape["shard"]
    width = tokens.shape[1]
    hidden = inner_weight.shape[1]
    each = width // shards
    folds = hidden // width
    vectors = (content_bias, position_bias, order_bias, first_gain, first_shift, outer_bias, second_gain, second_shift)
    wide_own, small, projections_own = pack(
        (query_weight, key_weight, value_weight), output_weight, inner_weight, relative_table, order_table, vectors, inner_bias, folds
    )
    projections, small_all = gather(mesh, [projections_own, small], 0)
    projections = projections.reshape(width, 3 * width)
    weight_relative, weight_order, small_all, bias_inner, hot, away, behind, ahead = unpack(
        small_all, segment_ids, width, len(vectors), folds
    )
    wide = lax.all_gather(wide_own, "shard", axis=0, tiled=True)
    weight_outer = lax.all_gather(outer_weight, "shard", axis=0, tiled=True)

    pooled, content, position, ordering, keys, values, document, mix = project(tokens, hot, projections, small_all)
    probs, context, mixed, inverse = attend(
        behind, ahead, content, position, ordering, keys, values, weight_relative, weight_order, away, document
    )
    layer_out, sum_grad, context_grad, sums, inner_sums, output_grad, inner_grad, outer_grad = middle(
        context, pooled, cotangent, wide, weight_outer, small_all, bias_inner
    )
    query_low, key_low, value_low, relative_grad, order_grad, bias_sums = attend_back(
        behind, ahead, probs, context_grad, mixed, inverse, content, position, ordering,
        keys, values, weight_relative, weight_order,
    )
    projection_grad = tail(tokens, key_low, value_low, query_low, pooled)
    small_grad = collect(relative_grad, order_grad, bias_sums, sums, inner_sums, shards, len(vectors), folds)
    outer_part = lax.psum_scatter(outer_grad, "shard", scatter_dimension=0, tiled=True)
    inner_sum, output_sum, projection_sum, small_sum, outer_sum, tokens_grad = scatter(
        mesh,
        [
            inner_grad.reshape(shards, each, hidden),
            output_grad.reshape(shards, each, width),
            projection_grad.reshape(shards, each, 3 * width),
            small_grad,
        ],
        [width, width, width, 128],
        [outer_part],
        [key_low, value_low, query_low, sum_grad, mix, projections],
        tokens_block,
        1,
    )
    parts = finish(projection_sum, output_sum, inner_sum, outer_sum, small_sum, len(vectors), folds)
    squares, (inner_sum, outer_sum, relative_sum, order_sum) = parts[:4], parts[4:8]
    own, bias_sum = parts[8:-1], parts[-1]
    return (
        layer_out, tokens_grad, *squares, relative_sum, order_sum, *own[:5],
        inner_sum, bias_sum, outer_sum, *own[5:],
    )


def solution(mesh):
    placed = (
        P(("rep", "shard"), None),
        P(("rep", "shard"), None),
        P("shard", None),
        P("shard", None),
        P("shard", None),
        P("shard", None),
        P(None, "shard"),
        P(None, "shard"),
        P("shard"),
        P("shard"),
        P("shard"),
        P("shard"),
        P("shard"),
        P("shard", None),
        P("shard"),
        P("shard", None),
        P("shard"),
        P("shard"),
        P("shard"),
        P(("rep", "shard"), None),
    )
    return jax.shard_map(
        functools.partial(body, mesh),
        mesh=mesh,
        in_specs=placed,
        out_specs=(
            P(("rep", "shard"), None),
            P(("rep", "shard"), None),
            P("shard", None),
            P("shard", None),
            P("shard", None),
            P("shard", None),
            P(None, "shard"),
            P(None, "shard"),
            P("shard"),
            P("shard"),
            P("shard"),
            P("shard"),
            P("shard"),
            P("shard", None),
            P("shard"),
            P("shard", None),
            P("shard"),
            P("shard"),
            P("shard"),
        ),
        check_vma=False,
    )
```

```python
import functools
import math

import jax
import jax.numpy as jnp
import numpy as np
from jax import lax
from jax.experimental import pallas as pl
from jax.experimental.pallas import tpu as pltpu
from jax.sharding import PartitionSpec as P

LIMITS = (1, 2, 3, 4, 5, 6, 7, 8, 12, 16, 24, 32, 48, 64, 128)
BQ = 128
NEAR = 640
CHUNK = 256
LOG2E = math.log2(math.e)
LN2 = math.log(2.0)
BIG = 1e30
f32 = jnp.float32
bf16 = jnp.bfloat16


def bucket_of(offset):
    distance = np.abs(offset)
    passed = sum((distance >= limit).astype(np.int32) for limit in LIMITS)
    return np.where(offset < 0, 15 + passed + (distance >= 256), passed).astype(np.int32)


def bucket_onehot():
    out = np.zeros((4 * 128, 128), np.float32)
    offsets = np.concatenate([np.arange(-256, 128), np.full(64, -300), np.full(64, 300)])
    out[np.arange(512), bucket_of(offsets)] = 1
    out[:, 32] = offsets >= 0
    out[:, 33] = offsets < 0
    return out


def nt(left, right):
    return lax.dot_general(left, right, (((1,), (1,)), ((), ())), preferred_element_type=f32)


def nn(left, right):
    return lax.dot_general(left, right, (((1,), (0,)), ((), ())), preferred_element_type=f32)


def tn(left, right):
    return lax.dot_general(left, right, (((0,), (0,)), ((), ())), preferred_element_type=f32)


def halves(array):
    low = lax.broadcasted_iota(jnp.int32, array.shape, 1) < 64
    zero = jnp.zeros_like(array)
    return jnp.where(low, array, zero), jnp.where(low, zero, array)


def pick(array):
    half = array.shape[0] // 2
    low = lax.broadcasted_iota(jnp.int32, (half, 128), 1) < 64
    return jnp.where(low, array[:half], array[half:])


def take(table, index):
    numbers = lax.GatherDimensionNumbers(
        offset_dims=(), collapsed_slice_dims=(1,), start_index_map=(1,),
        operand_batching_dims=(0,), start_indices_batching_dims=(0,),
    )
    return lax.gather(table, index[:, :, None], numbers, (1, 1), mode=lax.GatherScatterMode.PROMISE_IN_BOUNDS)


def lanes_of(p):
    return slice(128 * p, 128 * p + 128)


def far_start(chunk, behind, far, near):
    start = jnp.where(chunk < behind, near - CHUNK * (chunk + 1), near + NEAR + CHUNK * (chunk - behind))
    return pl.multiple_of(jnp.where(chunk < far, start, 0), 128)


def forward_kernel(
    group, behind_ref, ahead_ref, content_ref, position_ref, ordering_ref, key_ref, value_ref,
    relative_ref, order_ref, away_ref, document_ref,
    probs_ref, context_ref, mixed_ref, inverse_ref,
    index_ref, keys, values, table, bias, scores, peak, total,
):
    step = pl.program_id(1)
    length = key_ref.shape[0]

    rows_each = 256
    pieces = length // rows_each

    @pl.when((step == 0) & (pl.program_id(0) == 0))
    def _():
        @pl.loop(0, NEAR // 128)
        def _(tile):
            lane = lax.broadcasted_iota(jnp.int32, (BQ, 128), 1)
            row = lax.broadcasted_iota(jnp.int32, (BQ, 128), 0)
            offset = 128 * (tile - 2) + lane - 2 * row
            distance = jnp.abs(offset)
            passed = jnp.zeros_like(offset)
            for limit in LIMITS:
                passed = passed + jnp.where(distance >= limit, 1, 0)
            index_ref[tile] = jnp.where(offset < 0, 15 + passed + jnp.where(distance >= 256, 1, 0), passed)

        @pl.loop(0, group)
        def _(p):
            for scratch in (keys, values):
                scratch[p, :256, :128] = jnp.zeros((256, 128), bf16)
                scratch[p, 256 + length :, :128] = jnp.zeros((256, 128), bf16)

            @pl.loop(0, pieces + 2)
            def _(piece):
                rows = pl.ds(pl.multiple_of(piece * rows_each, rows_each), rows_each)
                keys[p, rows, 128:] = away_ref[rows, :]
                values[p, rows, 128:] = jnp.ones((rows_each, 128), bf16)

    @pl.when(step == 0)
    def _():
        @pl.loop(0, pieces)
        def _(piece):
            source = pl.ds(pl.multiple_of(piece * rows_each, rows_each), rows_each)
            target = pl.ds(pl.multiple_of((piece + 1) * rows_each, rows_each), rows_each)
            for p in range(group):
                keys[p, target, :128] = key_ref[source, lanes_of(p)]
                values[p, target, :128] = value_ref[source, lanes_of(p)]

        after = lax.broadcasted_iota(jnp.int32, (32, 128), 0) < 16
        table[...] = jnp.zeros(table.shape, bf16)
        for p in range(group):
            lanes = lanes_of(p)
            orders = jnp.where(after, order_ref[0:1, lanes].astype(f32), order_ref[1:2, lanes].astype(f32)).astype(bf16)
            for half, (relative, order) in enumerate(zip(halves(relative_ref[:, lanes]), halves(orders))):
                both = jnp.concatenate([relative, order], 1)
                table[p, 128 * half : 128 * half + 32, :] = both
                for side, bucket in ((0, 31), (1, 15)):
                    start = 256 + 256 * side + 128 * half
                    table[p, start : start + 128, :] = jnp.broadcast_to(both[bucket : bucket + 1].astype(f32), (128, 256)).astype(bf16)

    document = document_ref[...]
    near = pl.multiple_of(step * 256, 256)
    queries = []
    for p in range(group):
        even, odd = halves(content_ref[:, lanes_of(p)])
        queries.append(jnp.concatenate(
            [jnp.concatenate([even, document], 1), jnp.concatenate([odd, document], 1)], 0
        ))
    for p in range(group):
        lanes = lanes_of(p)
        places = nt(jnp.concatenate([position_ref[:, lanes], ordering_ref[:, lanes]], 1), table[p]) * (0.125 * LOG2E)
        place = (places[:, :128], places[:, 128:256])
        near_scores = nt(queries[p], keys[p, pl.ds(near, NEAR), :])
        for half in range(2):
            rows = slice(BQ * half, BQ * half + BQ)
            for side in range(2):
                start = 256 + 256 * side + 128 * half
                bias[p, rows, 128 * side : 128 * side + 128] = places[:, start : start + 128]
            for quarter in range(2):
                own = slice(64 * quarter, 64 * quarter + 64)
                rows = slice(BQ * half + 64 * quarter, BQ * half + 64 * quarter + 64)
                best = None
                for tile in range(NEAR // 128):
                    if tile == 4 - 4 * quarter:
                        extra = bias[p, rows, 128 - 128 * quarter : 256 - 128 * quarter]
                    else:
                        extra = take(place[half][own], index_ref[tile, own])
                    part = near_scores[rows, 128 * tile : 128 * tile + 128] + extra
                    scores[p, rows, pl.ds(near + 128 * tile, 128)] = part
                    best = part if best is None else jnp.maximum(best, part)
                peak[p, rows, :] = best
    behind = behind_ref[step, 0]
    far = behind + ahead_ref[step, 0]

    def start_of(chunk):
        return far_start(chunk, behind, far, near)

    @pl.loop(0, (far + 1) // 2)
    def _(two):
        for chunk in (2 * two, 2 * two + 1):
            start = start_of(chunk)
            place = pl.multiple_of(jnp.where(chunk < behind, 0, 128), 128)
            for p in range(group):
                part = nt(queries[p], keys[p, pl.ds(start, CHUNK), :])
                extra = bias[p, :, pl.ds(place, 128)]
                left, right = part[:, :128] + extra, part[:, 128:] + extra
                scores[p, :, pl.ds(start, 128)] = left
                scores[p, :, pl.ds(start + 128, 128)] = right
                peak[p] = jnp.maximum(peak[p], jnp.maximum(left, right))

    tops = [jnp.max(peak[p], axis=1, keepdims=True) for p in range(group)]
    for p in range(group):
        peak[p] = jnp.broadcast_to(tops[p], (2 * BQ, 128))
        probs = jnp.exp2(scores[p, :, pl.ds(near, NEAR)] - tops[p]).astype(bf16)
        probs_ref[p, 0, :, pl.ds(near, NEAR)] = probs
        total[p] = nn(probs, values[p, pl.ds(near, NEAR), :])

    @pl.loop(0, (far + 1) // 2)
    def _(two):
        starts = [start_of(2 * two), start_of(2 * two + 1)]
        for p in range(group):
            top = peak[p]
            parts = []
            for start in starts:
                left = jnp.exp2(scores[p, :, pl.ds(start, 128)] - top).astype(bf16)
                right = jnp.exp2(scores[p, :, pl.ds(start + 128, 128)] - top).astype(bf16)
                probs = jnp.concatenate([left, right], 1)
                probs_ref[p, 0, :, pl.ds(start, CHUNK)] = probs
                parts.append(nn(probs, values[p, pl.ds(start, CHUNK), :]))
            total[p] += parts[0] + parts[1]

    for p in range(group):
        lanes = lanes_of(p)
        inverse = 1.0 / total[p, :, 128:]
        mixed = pick(total[p, :, :128] * inverse)
        inverse_ref[:, lanes] = pick(inverse)
        mixed_ref[:, lanes] = mixed
        context_ref[:, lanes] = mixed.astype(bf16)


def backward_kernel(
    group, behind_ref, ahead_ref, probs_ref, grad_ref, mixed_ref, inverse_ref, content_ref, position_ref, ordering_ref,
    key_ref, value_ref, relative_ref, order_ref, turn_ref, onehot_ref,
    query_ref, key_low_ref, value_low_ref, relative_out, order_out, sums_out,
    keys, values, table, key_total, value_total, query_total, far_total, bucket, table_total, sums,
):
    step = pl.program_id(1)
    length = key_ref.shape[0]

    @pl.when(step == 0)
    def _():
        slot = lax.broadcasted_iota(jnp.int32, (32, 128), 0)
        table[...] = jnp.zeros(table.shape, bf16)
        for p in range(group):
            lanes = lanes_of(p)
            even, odd = halves(relative_ref[:, lanes])
            table[p, 0:32, :128] = even
            table[p, 128:160, :128] = odd
            orders = jnp.where(slot == 0, order_ref[0:1, lanes].astype(f32), order_ref[1:2, lanes].astype(f32))
            even, odd = halves(jnp.where(slot < 2, orders, 0.0))
            table[p, 32:64, 128:] = even.astype(bf16)
            table[p, 160:192, 128:] = odd.astype(bf16)

        @pl.loop(0, length // 256 + 2)
        def _(piece):
            rows = pl.ds(pl.multiple_of(piece * 256, 256), 256)
            for p in range(group):
                for total in (key_total, value_total):
                    total[p, :, rows] = jnp.zeros((128, 256), f32)

        for scratch in (keys, values):
            scratch[:, :256, :] = jnp.zeros((group, 256, 128), bf16)
            scratch[:, 256 + length :, :] = jnp.zeros((group, 256, 128), bf16)

        @pl.loop(0, length // 256)
        def _(piece):
            source = pl.ds(pl.multiple_of(piece * 256, 256), 256)
            target = pl.ds(pl.multiple_of((piece + 1) * 256, 256), 256)
            for p in range(group):
                for scratch, ref in ((keys, key_ref), (values, value_ref)):
                    scratch[p, target, :] = ref[source, lanes_of(p)]

        table_total[...] = jnp.zeros(table_total.shape, f32)
        sums[...] = jnp.zeros(sums.shape, f32)

    near = pl.multiple_of(step * 256, 256)
    grads, grads_t, content_t, deltas = [], [], [], []
    for p in range(group):
        lanes = lanes_of(p)
        scaled = (grad_ref[:, lanes].astype(f32) * inverse_ref[:, lanes]).astype(bf16)
        both = jnp.concatenate(halves(scaled), 0)
        even, odd = halves(scaled.astype(f32) * mixed_ref[:, lanes])
        deltas.append(jnp.concatenate(
            [jnp.sum(even, axis=1, keepdims=True), jnp.sum(odd, axis=1, keepdims=True)], 0
        ))
        grads.append(both)
        grads_t.append(both.T)
        content_t.append(jnp.concatenate(halves(content_ref[:, lanes]), 0).T)

    def visit(p, start, size):
        probs = probs_ref[p, 0, :, pl.ds(start, size)]
        prob_grad = nt(grads[p], values[p, pl.ds(start, size), :])
        score = probs.astype(f32) * (prob_grad - deltas[p])
        score_low = score.astype(bf16)
        value_total[p, :, pl.ds(start, size)] += nn(grads_t[p], probs)
        key_total[p, :, pl.ds(start, size)] += nn(content_t[p], score_low)
        return score, nn(score_low, keys[p, pl.ds(start, size), :])

    turn = turn_ref[...]
    turns = jnp.concatenate([turn, turn], 0)
    lane = lax.broadcasted_iota(jnp.int32, (64, 128), 1)
    row = lax.broadcasted_iota(jnp.int32, (64, 128), 0)
    first = lane + 2 * row < 128
    zero = jnp.zeros((64, 128), f32)
    for p in range(group):
        score, query_total[p] = visit(p, near, NEAR)
        parts = [score[:, 128 * t : 128 * t + 128] for t in range(5)]
        tiles = [take(part, turns) for part in parts]
        for quarter in range(4):
            rows = slice(64 * quarter, 64 * quarter + 64)
            own = [tile[rows] for tile in tiles]
            if quarter % 2 == 0:
                near_parts = [jnp.where(first, own[t], own[t + 1]) for t in range(3)]
                far_total[p, 0, rows] = jnp.where(first, zero, own[0])
                far_total[p, 1, rows] = jnp.where(first, own[3], zero) + parts[4][rows]
            else:
                near_parts = [jnp.where(first, own[t + 1], own[t + 2]) for t in range(3)]
                far_total[p, 0, rows] = parts[0][rows] + jnp.where(first, zero, own[1])
                far_total[p, 1, rows] = jnp.where(first, own[4], zero)
            for t in range(3):
                bucket[p, rows, 128 * t : 128 * t + 128] = near_parts[t].astype(bf16)
    behind = behind_ref[step, 0]

    far = behind + ahead_ref[step, 0]

    @pl.loop(0, (far + 1) // 2)
    def _(two):
        for chunk in (2 * two, 2 * two + 1):
            start = far_start(chunk, behind, far, near)
            side = jnp.where(chunk < behind, 0, 1)
            for p in range(group):
                score, part = visit(p, start, CHUNK)
                query_total[p] += part
                far_total[p, side] += score[:, :128] + score[:, 128:]

    for p in range(group):
        lanes = lanes_of(p)
        folded = [far_total[p, side] + pltpu.roll(far_total[p, side], 64, 1) for side in range(2)]
        low_lane = lax.broadcasted_iota(jnp.int32, folded[0].shape, 1) < 64
        bucket[p, :, 384:] = jnp.where(low_lane, *folded).astype(bf16)
        low = (nn(bucket[p], onehot_ref[...]) * 0.125).astype(bf16)
        low = jnp.concatenate([low[:BQ], low[BQ:]], 1)
        placed = nn(low, table[p])
        content_grad = pick(query_total[p]) * 0.125
        query_ref[:, lanes] = (content_grad + placed[:, :128] + placed[:, 128:]).astype(bf16)
        table_total[p] += tn(low, jnp.concatenate([position_ref[:, lanes], ordering_ref[:, lanes]], 1))
        for j, term in enumerate((content_grad, placed[:, :128], placed[:, 128:])):
            sums[j : j + 1, lanes] += jnp.sum(term, axis=0, keepdims=True)

    @pl.when(step == pl.num_programs(1) - 1)
    def _():
        low_lane = lax.broadcasted_iota(jnp.int32, (32, 128), 1) < 64
        for p in range(group):
            lanes = lanes_of(p)
            relative_out[:, lanes] = jnp.where(low_lane, table_total[p, 0:32, :128], table_total[p, 128:160, :128])
            order_out[:, lanes] = jnp.where(low_lane[:8], table_total[p, 32:40, 128:], table_total[p, 160:168, 128:])
        sums_out[...] = sums[...]

        @pl.loop(0, length // 512)
        def _(piece):
            rows = pl.ds(pl.multiple_of(piece * 512, 512), 512)
            columns = pl.ds(pl.multiple_of(piece * 512 + 256, 256), 512)
            for p in range(group):
                key_low_ref[rows, lanes_of(p)] = (key_total[p, :, columns] * LN2).T.astype(bf16)
                value_low_ref[rows, lanes_of(p)] = value_total[p, :, columns].T.astype(bf16)


def fixed(*shape):
    return pl.BlockSpec(shape, lambda *_: (0,) * len(shape), pipeline_mode=pl.Buffered(1))


GROUP = 3


def attend(behind, ahead, content, position, ordering, keys, values, relative, order, away, document):
    rows, width = content.shape
    length = keys.shape[0]
    padded = length + 512
    pairs, blocks, group = width // 128, rows // BQ, GROUP
    wide = 128 * group
    tile = pl.BlockSpec((BQ, wide), lambda p, i, *_: (i, p))
    whole = pl.BlockSpec((length, wide), lambda p, i, *_: (0, p), pipeline_mode=pl.Buffered(1))
    return pl.pallas_call(
        functools.partial(forward_kernel, group),
        name="attend",
        out_shape=(
            jax.ShapeDtypeStruct((pairs, blocks, 2 * BQ, padded), bf16),
            jax.ShapeDtypeStruct((rows, width), bf16),
            jax.ShapeDtypeStruct((rows, width), f32),
            jax.ShapeDtypeStruct((rows, width), f32),
        ),
        grid_spec=pltpu.PrefetchScalarGridSpec(
            num_scalar_prefetch=2,
            grid=(pairs // group, blocks),
            in_specs=[
                tile, tile, tile, whole, whole,
                pl.BlockSpec((32, wide), lambda p, i, *_: (0, p)),
                pl.BlockSpec((2, wide), lambda p, i, *_: (0, p)),
                fixed(padded, 128),
                pl.BlockSpec((BQ, 128), lambda p, i, *_: (i, 0)),
            ],
            out_specs=[pl.BlockSpec((group, 1, 2 * BQ, padded), lambda p, i, *_: (p, i, 0, 0)), tile, tile, tile],
            scratch_shapes=[
                pltpu.VMEM((NEAR // 128, BQ, 128), jnp.int32),
                pltpu.VMEM((group, padded, 256), bf16),
                pltpu.VMEM((group, padded, 256), bf16),
                pltpu.VMEM((group, 768, 256), bf16),
                pltpu.VMEM((group, 2 * BQ, 256), f32),
                pltpu.VMEM((group, 2 * BQ, padded), f32),
                pltpu.VMEM((group, 2 * BQ, 128), f32),
                pltpu.VMEM((group, 2 * BQ, 256), f32),
            ],
        ),
        compiler_params=pltpu.CompilerParams(dimension_semantics=("arbitrary", "arbitrary"), vmem_limit_bytes=62 << 20),
        cost_estimate=pl.CostEstimate(flops=40 * 10**9, bytes_accessed=70 * 10**6, transcendentals=10**7),
    )(behind, ahead, content, position, ordering, keys, values, relative, order, away, document)


def attend_back(behind, ahead, probs, grad, mixed, inverse, content, position, ordering, keys, values, relative, order):
    rows, width = content.shape
    length = keys.shape[0]
    padded = length + 512
    pairs, blocks, group = width // 128, rows // BQ, GROUP
    wide = 128 * group
    tile = pl.BlockSpec((BQ, wide), lambda p, i, *_: (i, p))
    whole = pl.BlockSpec((length, wide), lambda p, i, *_: (0, p), pipeline_mode=pl.Buffered(1))
    small = lambda n: pl.BlockSpec((n, wide), lambda p, i, *_: (0, p))
    turn = (np.arange(128)[None, :] + 2 * np.arange(BQ)[:, None]) % 128
    return pl.pallas_call(
        functools.partial(backward_kernel, group),
        name="attend_back",
        out_shape=(
            jax.ShapeDtypeStruct((rows, width), bf16),
            jax.ShapeDtypeStruct((length, width), bf16),
            jax.ShapeDtypeStruct((length, width), bf16),
            jax.ShapeDtypeStruct((32, width), f32),
            jax.ShapeDtypeStruct((8, width), f32),
            jax.ShapeDtypeStruct((8, width), f32),
        ),
        grid_spec=pltpu.PrefetchScalarGridSpec(
            num_scalar_prefetch=2,
            grid=(pairs // group, blocks),
            in_specs=[
                pl.BlockSpec((group, 1, 2 * BQ, padded), lambda p, i, *_: (p, i, 0, 0)),
                tile, tile, tile, tile, tile, tile, whole, whole, small(32), small(2), fixed(BQ, 128), fixed(512, 128),
            ],
            out_specs=[tile, whole, whole, small(32), small(8), small(8)],
            scratch_shapes=[
                pltpu.VMEM((group, padded, 128), bf16),
                pltpu.VMEM((group, padded, 128), bf16),
                pltpu.VMEM((group, 256, 256), bf16),
                pltpu.VMEM((group, 128, padded), f32),
                pltpu.VMEM((group, 128, padded), f32),
                pltpu.VMEM((group, 2 * BQ, 128), f32),
                pltpu.VMEM((group, 2, 2 * BQ, 128), f32),
                pltpu.VMEM((group, 2 * BQ, 512), bf16),
                pltpu.VMEM((group, 256, 256), f32),
                pltpu.VMEM((8, wide), f32),
            ],
        ),
        compiler_params=pltpu.CompilerParams(dimension_semantics=("arbitrary", "arbitrary"), vmem_limit_bytes=62 << 20),
        cost_estimate=pl.CostEstimate(flops=80 * 10**9, bytes_accessed=70 * 10**6, transcendentals=0),
    )(behind, ahead, probs, grad, mixed, inverse, content, position, ordering, keys, values, relative, order,
      jnp.asarray(turn, jnp.int32), jnp.asarray(bucket_onehot(), bf16))


MESH = pl.DeviceIdType.MESH


class Place:
    def __init__(self, replicas, shards):
        self.replicas, self.shards = replicas, shards
        self.cores = 2 if shards % 2 == 0 else 1
        chips = shards // self.cores
        self.across = 2 if chips % 2 == 0 else 1
        self.line = chips // self.across
        self.replica = lax.axis_index("rep")
        own = lax.axis_index("shard")
        self.own = own
        self.core = lax.rem(own, self.cores)
        self.column = lax.rem(own // self.cores, self.across)
        self.spot = own // (self.cores * self.across)

    def shard(self, spot, column, core):
        return (spot * self.across + column) * self.cores + core

    def other_column(self, step):
        return lax.rem(self.column + step, self.across)

    def other_replica(self, step):
        return lax.rem(self.replica + step, self.replicas)

    def device(self, spot=None, column=None, core=None, replica=None):
        spot = self.spot if spot is None else spot
        column = self.column if column is None else column
        core = self.core if core is None else core
        replica = self.replica if replica is None else replica
        return (replica, self.shard(spot, column, core))

    def meet(self):
        barrier = pltpu.get_barrier_semaphore()

        def greet(device):
            pl.semaphore_signal(barrier, inc=1, device_id=device, device_id_type=MESH)

        fixed = 0
        if self.cores > 1:
            greet(self.device(core=1 - self.core))
            fixed += 1
        for step in range(1, self.across):
            greet(self.device(column=self.other_column(step)))
            fixed += 1
        for step in range(1, self.replicas):
            greet(self.device(replica=self.other_replica(step)))
            fixed += 1
        for step, there in ((1, self.spot < self.line - 1), (-1, self.spot > 0)):

            @pl.when(there)
            def _():
                greet(self.device(spot=self.spot + step))

        lined = (self.spot < self.line - 1).astype(jnp.int32) + (self.spot > 0).astype(jnp.int32)
        pl.semaphore_wait(barrier, fixed + lined)


def parts_of(columns, replicas):
    return replicas if columns % (128 * replicas) == 0 else 1


def columns_of(part, parts, columns):
    size = columns // parts
    return pl.ds(pl.multiple_of(part * size, 128), size)


def when(condition, action):
    if condition is True:
        action()
    else:
        pl.when(condition)(action)


def gather_kernel(replicas, shards, count, *refs):
    here = Place(replicas, shards)
    sources, wholes = refs[:count], refs[count : 2 * count]
    line_send, line_recv, cross_send, cross_recv, rep_send, rep_recv, core_send, core_recv = refs[2 * count :]
    here.meet()
    pending = []

    def send(source, whole_view, send_sem, recv_sem, device, condition=True):
        copy = pltpu.make_async_remote_copy(
            src_ref=source, dst_ref=whole_view, send_sem=send_sem, recv_sem=recv_sem, device_id=device, device_id_type=MESH
        )
        when(condition, copy.start)
        pending.append((condition, copy.wait_send))

    def arrived(view, recv_sem, condition=True):
        copy = pltpu.make_async_remote_copy(
            src_ref=view, dst_ref=view, send_sem=recv_sem, recv_sem=recv_sem, device_id=here.device(), device_id_type=MESH
        )
        when(condition, copy.wait_recv)

    def view(k, spot, column, core, part=None):
        whole = wholes[k].at[here.shard(spot, column, core)]
        if part is None:
            return whole
        columns = whole.shape[1]
        return whole.at[:, columns_of(part, parts_of(columns, replicas), columns)]

    def spread(k, spot, condition, own=False):
        columns = wholes[k].shape[2]
        parts = parts_of(columns, replicas)
        part = here.replica if parts > 1 else 0
        target = view(k, spot, here.column, here.core)
        source = sources[k] if own else target
        for step in range(1, here.across):
            cut = columns_of(part, parts, columns)
            send(source.at[:, cut], target.at[:, cut], cross_send.at[k, step, spot], cross_recv.at[k, here.column, spot],
                 here.device(column=here.other_column(step)), condition)
        if here.cores > 1:
            send(source, target, core_send.at[k, 0, here.column, spot], core_recv.at[k, 0, here.column, spot],
                 here.device(core=1 - here.core), condition)

    def crossed(k, spot, condition):
        columns = wholes[k].shape[2]
        parts = parts_of(columns, replicas)
        part = here.replica if parts > 1 else 0
        for step in range(1, here.across):
            column = here.other_column(step)
            piece = view(k, spot, column, here.core, part)
            arrived(piece, cross_recv.at[k, column, spot], condition)
            if parts > 1:
                for hop in range(1, replicas):
                    send(piece, piece, rep_send.at[k, hop, column, spot], rep_recv.at[k, here.replica, column, spot],
                         here.device(replica=here.other_replica(hop)), condition)
            if here.cores > 1:
                send(piece, piece, core_send.at[k, 1, column, spot], core_recv.at[k, 1, column, spot],
                     here.device(core=1 - here.core), condition)

    def replicated(k, spot, condition):
        parts = parts_of(wholes[k].shape[2], replicas)
        if parts == 1:
            return
        for step in range(1, here.across):
            column = here.other_column(step)
            for hop in range(1, replicas):
                replica = here.other_replica(hop)
                piece = view(k, spot, column, here.core, replica)
                arrived(piece, rep_recv.at[k, replica, column, spot], condition)
                if here.cores > 1:
                    send(piece, piece, core_send.at[k, 1 + hop, column, spot], core_recv.at[k, 1 + hop, column, spot],
                         here.device(core=1 - here.core), condition)

    def at(distance, action):
        for k in range(count):
            if distance == 0:
                action(k, here.spot, True)
            else:
                action(k, here.spot - distance, here.spot >= distance)
                action(k, here.spot + distance, here.spot + distance < here.line)

    for k in range(count):
        own = view(k, here.spot, here.column, here.core)
        send(sources[k], own, line_send.at[k, 0, here.spot], line_recv.at[k, here.spot],
             here.device(spot=here.spot + 1), here.spot < here.line - 1)
        send(sources[k], own, line_send.at[k, 1, here.spot], line_recv.at[k, here.spot],
             here.device(spot=here.spot - 1), here.spot > 0)
        spread(k, here.spot, True, own=True)
    for k in range(count):
        wholes[k][here.own] = sources[k][...]

    def along(distance):
        for k in range(count):
            for sign in (-1, 1):
                spot = here.spot + sign * distance
                condition = (spot >= 0) & (spot < here.line)
                piece = view(k, spot, here.column, here.core)
                arrived(piece, line_recv.at[k, spot], condition)
                onward = here.spot - sign
                send(piece, piece, line_send.at[k, 0 if sign < 0 else 1, spot], line_recv.at[k, spot],
                     here.device(spot=onward), condition & (onward >= 0) & (onward < here.line))
                spread(k, spot, condition)

    for distance in range(here.line + 2):
        if 1 <= distance < here.line:
            along(distance)
        if 1 <= distance <= here.line:
            at(distance - 1, crossed)
        if 2 <= distance:
            at(distance - 2, replicated)
    if here.cores > 1:
        for k in range(count):
            columns = wholes[k].shape[2]
            parts = parts_of(columns, replicas)
            for spot in range(here.line):
                other = 1 - here.core
                arrived(view(k, spot, here.column, other), core_recv.at[k, 0, here.column, spot])
                for step in range(1, here.across):
                    column = here.other_column(step)
                    part = here.replica if parts > 1 else 0
                    arrived(view(k, spot, column, other, part), core_recv.at[k, 1, column, spot])
                    for hop in range(1, replicas if parts > 1 else 1):
                        arrived(view(k, spot, column, other, here.other_replica(hop)), core_recv.at[k, 1 + hop, column, spot])
    for condition, wait in pending:
        when(condition, wait)


def gather(mesh, arrays, collective_id):
    replicas, shards = mesh.shape["rep"], mesh.shape["shard"]
    count = len(arrays)
    line = shards // 4
    dma = pltpu.SemaphoreType.DMA
    vmem = pl.BlockSpec(memory_space=pltpu.VMEM)
    moved = sum(a.size * 2 * shards for a in arrays)
    return pl.pallas_call(
        functools.partial(gather_kernel, replicas, shards, count),
        name="gather",
        out_shape=[jax.ShapeDtypeStruct((shards,) + a.shape, a.dtype) for a in arrays],
        in_specs=[vmem] * count,
        out_specs=[vmem] * count,
        scratch_shapes=[
            dma((count, 2, line)), dma((count, line)),
            dma((count, 2, line)), dma((count, 2, line)),
            dma((count, replicas, 2, line)), dma((count, replicas, 2, line)),
            dma((count, replicas + 1, 2, line)), dma((count, replicas + 1, 2, line)),
        ],
        compiler_params=pltpu.CompilerParams(collective_id=collective_id, has_side_effects=True, vmem_limit_bytes=56 << 20),
        cost_estimate=pl.CostEstimate(flops=0, bytes_accessed=moved * 4, transcendentals=0),
    )(*arrays)


WORK_INPUTS = ("key_low", "value_low", "query_low", "sum_grad", "mix", "weight")


def scatter_kernel(replicas, shards, count, chunks, extra, work, *refs):
    here = Place(replicas, shards)
    take = lambda number: [refs_left.pop(0) for _ in range(number)]
    refs_left = list(refs)
    sources, extras, work_in = take(count), take(extra), take(len(WORK_INPUTS))
    outs, extra_outs, (tokens_grad,) = take(count), take(extra), take(1)
    own_bufs, core_bufs, rep_bufs, cross_bufs, line_bufs, last_bufs = (take(count) for _ in range(6))
    extra_bufs = take(extra)
    work_bufs, (block_buf, own_sems, work_sems, block_sems) = take(len(WORK_INPUTS)), take(4)
    (core_send, core_recv, rep_send, rep_recv, cross_send, cross_recv, line_send, line_recv, last_send, last_recv) = refs_left
    local = []
    for j, (k, low, size) in enumerate(chunks):
        for column in range(here.across):
            cut = pl.ds(low, size)
            local.append(pltpu.make_async_copy(
                sources[k].at[:, column, here.core, :, cut], own_bufs[k].at[column, :, :, cut], own_sems.at[j, column]
            ))
    for copy in local:
        copy.start()
    here.meet()
    pending = []

    def send(source, target, send_sem, recv_sem, device, condition=True):
        copy = pltpu.make_async_remote_copy(
            src_ref=source, dst_ref=target, send_sem=send_sem, recv_sem=recv_sem, device_id=device, device_id_type=MESH
        )
        when(condition, copy.start)
        pending.append((condition, copy.wait_send))

    def arrived(view, recv_sem, condition=True):
        copy = pltpu.make_async_remote_copy(
            src_ref=view, dst_ref=view, send_sem=recv_sem, recv_sem=recv_sem, device_id=here.device(), device_id_type=MESH
        )
        when(condition, copy.wait_recv)

    def add(target, source):
        target[...] = target[...] + source[...]

    steps = range(1, here.across)
    hops = range(1, replicas)

    def split(j):
        return parts_of(chunks[j][2], replicas)

    def columns(j, part=None):
        _, low, size = chunks[j]
        if part is None or split(j) == 1:
            return pl.ds(low, size)
        size = size // replicas
        return pl.ds(pl.multiple_of(low + part * size, 128), size)

    def compact(j):
        _, low, size = chunks[j]
        return pl.ds(low // split(j), size // split(j))

    def mixed(j, column):
        k = chunks[j][0]
        mine = core_bufs[k].at[column, :, :, columns(j)]
        own = own_bufs[k].at[column, :, :, columns(j)]
        _, low, size = chunks[j]
        cut = pl.ds(low, size)
        pltpu.make_async_copy(
            sources[k].at[:, column, here.core, :, cut], own_bufs[k].at[column, :, :, cut], own_sems.at[j, column]
        ).wait()
        if here.cores > 1:
            arrived(mine, core_recv.at[j, column])
            add(mine, own)
        else:
            mine[...] = own[...]

    def stage_rep(j):
        k = chunks[j][0]
        for step in steps:
            column = here.other_column(step)
            mixed(j, column)
            if split(j) > 1:
                for hop in hops:
                    replica = here.other_replica(hop)
                    send(core_bufs[k].at[column, :, :, columns(j, replica)], rep_bufs[k].at[hop - 1, step - 1, :, :, compact(j)],
                         rep_send.at[j, hop, step], rep_recv.at[j, hop, step], here.device(replica=replica))

    def stage_cross(j):
        k = chunks[j][0]
        for step in steps:
            column = here.other_column(step)
            mine = core_bufs[k].at[column, :, :, columns(j, here.replica)]
            if split(j) > 1:
                for hop in hops:
                    piece = rep_bufs[k].at[hop - 1, step - 1, :, :, compact(j)]
                    arrived(piece, rep_recv.at[j, hop, step])
                    add(mine, piece)
            send(mine, cross_bufs[k].at[step - 1, :, :, compact(j)], cross_send.at[j, step], cross_recv.at[j, step],
                 here.device(column=column))
        mixed(j, here.column)

    def stage_line(distance, j):
        k = chunks[j][0]
        if distance == here.line - 1:
            for step in steps:
                piece = cross_bufs[k].at[step - 1, :, :, compact(j)]
                arrived(piece, cross_recv.at[j, step])
                add(core_bufs[k].at[here.column, :, :, columns(j, here.replica)], piece)
        for sign, way in ((1, 0), (-1, 1)):
            target = here.spot + sign * distance
            inside = (target >= 0) & (target < here.line)
            before = here.spot - sign
            fed = inside & (before >= 0) & (before < here.line)
            mine = core_bufs[k].at[here.column, target, :, columns(j)]
            piece = line_bufs[k].at[way, target, :, columns(j)]
            arrived(piece, line_recv.at[j, way, target], fed)
            when(fed, functools.partial(add, mine, piece))
            send(mine, piece, line_send.at[j, way, target], line_recv.at[j, way, target],
                 here.device(spot=here.spot + sign), inside)

    def stage_last(j):
        k = chunks[j][0]
        mine = core_bufs[k].at[here.column, here.spot, :, columns(j)]
        for sign, way in ((1, 0), (-1, 1)):
            before = here.spot - sign
            fed = (before >= 0) & (before < here.line)
            piece = line_bufs[k].at[way, here.spot, :, columns(j)]
            arrived(piece, line_recv.at[j, way, here.spot], fed)
            when(fed, functools.partial(add, mine, piece))
        for hop in hops:
            send(mine, last_bufs[k].at[here.replica, :, columns(j)], last_send.at[j, hop], last_recv.at[j, here.replica],
                 here.device(replica=here.other_replica(hop)))

    def finish(own, buffer, out, semaphore, cut):
        for hop in hops:
            replica = here.other_replica(hop)
            arrived(buffer.at[replica, :, cut], semaphore.at[replica])
        result = None
        for replica in range(replicas):
            term = jnp.where(here.replica == replica, own[...].astype(f32), buffer[replica, :, cut].astype(f32))
            result = term if result is None else result + term
        out[:, cut] = result

    def stage_finish(j):
        k = chunks[j][0]
        finish(core_bufs[k].at[here.column, here.spot, :, columns(j)], last_bufs[k], outs[k], last_recv.at[j], columns(j))

    if here.cores > 1:
        for j, (k, _, _) in enumerate(chunks):
            for step in (*steps, 0):
                column = here.other_column(step)
                send(sources[k].at[:, column, 1 - here.core, :, columns(j)], core_bufs[k].at[column, :, :, columns(j)],
                     core_send.at[j, column], core_recv.at[j, column], here.device(core=1 - here.core))
    loads = [pltpu.make_async_copy(ref, buf, work_sems.at[i]) for i, (ref, buf) in enumerate(zip(work_in, work_bufs))]
    for copy in loads:
        copy.start()
    size = block_buf.shape[1]
    blocks = tokens_grad.shape[0] // size

    def stored(b, slot):
        return pltpu.make_async_copy(block_buf.at[slot], tokens_grad.at[pl.ds(pl.multiple_of(b * size, size), size)], block_sems.at[slot])

    def pair(turn):
        if turn == 0:
            for copy in loads:
                copy.wait()

        @pl.loop(0, 2)
        def _(slot):
            b = 2 * turn + slot
            if turn > 0:
                stored(b - 2, slot).wait()
            block_buf[slot] = work(b, *work_bufs)
            stored(b, slot).start()

    stages = [stage_rep, stage_cross]
    stages += [functools.partial(stage_line, distance) for distance in range(here.line - 1, 0, -1)]
    stages += [stage_last, stage_finish]
    total = len(chunks)
    for time in range(total + len(stages) - 1):
        for place in reversed(range(len(stages))):
            if 0 <= time - place < total:
                stages[place](time - place)
        if time == 0:
            for e in range(extra):
                for hop in hops:
                    send(extras[e], extra_bufs[e].at[here.replica], last_send.at[total + e, hop],
                         last_recv.at[total + e, here.replica], here.device(replica=here.other_replica(hop)))
        elif time % 2 == 1 and time < blocks:
            pair(time // 2)
    for turn in range((total + len(stages) - 1) // 2, blocks // 2):
        pair(turn)
    for slot in range(2):
        stored(blocks - 2 + slot, slot).wait()
    for e in range(extra):
        finish(extras[e], extra_bufs[e], extra_outs[e], last_recv.at[total + e], pl.ds(0, extras[e].shape[1]))
    for condition, wait in pending:
        when(condition, wait)


def scatter(mesh, arrays, widths, extras, inputs, work, collective_id):
    replicas, shards = mesh.shape["rep"], mesh.shape["shard"]
    count, extra = len(arrays), len(extras)
    dma = pltpu.SemaphoreType.DMA
    vmem = pl.BlockSpec(memory_space=pltpu.VMEM)
    cores = across = 2
    line = shards // (cores * across)
    shapes = [a.shape[1:] for a in arrays]
    chunks = [
        (k, low, min(width, shapes[k][1])) for k, width in enumerate(widths) for low in range(0, shapes[k][1], min(width, shapes[k][1]))
    ]
    cuts = [(shapes[k][0], shapes[k][1] // parts_of(min(width, shapes[k][1]), replicas)) for k, width in enumerate(widths)]
    moved = sum(a.size * 2 for a in arrays)
    number = len(chunks)
    rows = inputs[0].shape[0]
    size = min(rows, 256)
    anywhere = pl.BlockSpec(memory_space=pl.ANY)
    buffers = (
        [pltpu.VMEM((across, line) + s, bf16) for s in shapes]
        + [pltpu.VMEM((across, line) + s, bf16) for s in shapes]
        + [pltpu.VMEM((replicas - 1, across - 1, line) + s, bf16) for s in cuts]
        + [pltpu.VMEM((across - 1, line) + s, bf16) for s in cuts]
        + [pltpu.VMEM((2, line) + s, bf16) for s in shapes]
        + [pltpu.VMEM((replicas,) + s, bf16) for s in shapes]
        + [pltpu.VMEM((replicas,) + e.shape, bf16) for e in extras]
        + [pltpu.VMEM(i.shape, i.dtype) for i in inputs]
        + [pltpu.VMEM((2, size, inputs[0].shape[1]), f32), dma((number, across)), dma((len(inputs),)), dma((2,))]
    )
    return pl.pallas_call(
        functools.partial(scatter_kernel, replicas, shards, count, chunks, extra, work),
        name="scatter",
        out_shape=(
            [jax.ShapeDtypeStruct(s, f32) for s in shapes]
            + [jax.ShapeDtypeStruct(e.shape, f32) for e in extras]
            + [jax.ShapeDtypeStruct(inputs[0].shape, f32)]
        ),
        in_specs=[anywhere] * count + [vmem] * extra + [anywhere] * len(inputs),
        out_specs=[vmem] * (count + extra) + [anywhere],
        scratch_shapes=buffers + [
            dma((number, across)), dma((number, across)),
            dma((number, replicas, across)), dma((number, replicas, across)),
            dma((number, across)), dma((number, across)),
            dma((number, 2, line)), dma((number, 2, line)),
            dma((number + extra, replicas)), dma((number + extra, replicas)),
        ],
        compiler_params=pltpu.CompilerParams(collective_id=collective_id, has_side_effects=True, vmem_limit_bytes=62 << 20),
        cost_estimate=pl.CostEstimate(flops=0, bytes_accessed=moved * 4, transcendentals=0),
    )(*[a.reshape((line, across, cores) + a.shape[1:]) for a in arrays], *extras, *inputs)


FIRST_VECTOR = 34
VMEM_ALL = 62 << 20


def place_of(rows):
    return lax.broadcasted_iota(jnp.int32, (rows, 2 * rows), 1) - 2 * lax.broadcasted_iota(jnp.int32, (rows, 2 * rows), 0)


def mixing(own, rest):
    place = place_of(own.shape[0])
    return jnp.where(place == 0, own, jnp.where(place == 1, rest, 0.0)).astype(bf16)


def project_kernel(
    tokens_ref, hot_ref, weight_ref, small_ref,
    pooled_ref, content_ref, position_ref, ordering_ref, key_ref, value_ref, document_ref, mix_ref,
):
    width = tokens_ref.shape[1]
    rows = pooled_ref.shape[0]
    tokens = tokens_ref[...]
    place = place_of(rows)
    first, second = (nn(jnp.where(place == j, 1.0, 0.0).astype(bf16), hot_ref[...]) for j in range(2))
    document_ref[...] = first.astype(bf16)
    own = 1.0 / (1.0 + jnp.sum(first * second, axis=1, keepdims=True))
    mix_ref[...] = jnp.broadcast_to(own, mix_ref.shape)
    pooled = nn(mixing(own, 1.0 - own), tokens)
    pooled_ref[...] = pooled
    key_ref[...] = nn(tokens, weight_ref[:, width : 2 * width]).astype(bf16)
    value_ref[...] = nn(tokens, weight_ref[:, 2 * width :]).astype(bf16)
    queries = nn(pooled.astype(bf16), weight_ref[:, :width])
    bias = small_ref[2:5, :].astype(f32)
    content_ref[...] = ((queries + bias[0:1]) * (0.125 * LOG2E)).astype(bf16)
    position_ref[...] = (queries + bias[1:2]).astype(bf16)
    ordering_ref[...] = (queries + bias[2:3]).astype(bf16)


def project(tokens, hot, weight, small):
    length, width = tokens.shape
    block = 256
    steps = length // block
    whole = lambda n: pl.BlockSpec((block, n), lambda i: (i, 0))
    half = lambda n: pl.BlockSpec((block // 2, n), lambda i: (i, 0))
    rows = jax.ShapeDtypeStruct((length // 2, width), bf16)
    full = jax.ShapeDtypeStruct((length, width), bf16)
    narrow = lambda kind: jax.ShapeDtypeStruct((length // 2, 128), kind)
    return pl.pallas_call(
        project_kernel,
        name="project",
        grid=(steps,),
        out_shape=(jax.ShapeDtypeStruct((length // 2, width), f32), rows, rows, rows, full, full, narrow(bf16), narrow(f32)),
        in_specs=[whole(width), whole(128), fixed(*weight.shape), fixed(*small.shape)],
        out_specs=[half(width)] * 4 + [whole(width)] * 2 + [half(128)] * 2,
        compiler_params=pltpu.CompilerParams(vmem_limit_bytes=VMEM_ALL),
        cost_estimate=pl.CostEstimate(flops=5 * length * width * width, bytes_accessed=10 * length * width, transcendentals=0),
    )(tokens, hot, weight, small)


def mean(values):
    return jnp.mean(values, axis=1, keepdims=True)


def normalize(values):
    centered = values - mean(values)
    inverse = lax.rsqrt(mean(centered * centered) + 1e-05)
    return centered * inverse, inverse


def norm_back(grad, normed, inverse):
    return inverse * (grad - mean(grad) - normed * mean(grad * normed))


def column_sum(values):
    return jnp.sum(values, axis=0, keepdims=True)


def middle_kernel(
    blocks, context_ref, pooled_ref, cotangent_ref, wide_ref, outer_ref, small_ref, bias_ref,
    layer_ref, sum_ref, context_grad_ref, sums_ref, inner_sums_ref, output_out, inner_out, outer_out,
    act, back, slope, first_all, outer_all, attended_all, context_all,
):
    step = pl.program_id(0)
    size, width = pooled_ref.shape
    hidden = bias_ref.shape[1]
    chunks = [slice(c * width, (c + 1) * width) for c in range(hidden // width)]

    @pl.when(step == 0)
    def _():
        sums_ref[...] = jnp.zeros(sums_ref.shape, f32)
        inner_sums_ref[...] = jnp.zeros(inner_sums_ref.shape, f32)

    @pl.when(step < blocks)
    def _():
        rows = pl.ds(pl.multiple_of(step * size, size), size)

        def vector(j):
            return small_ref[2 + j : 3 + j, :].astype(f32)

        context = context_ref[...]
        context_all[rows, :] = context
        first_norm, first_inverse = normalize(pooled_ref[...] + nn(context, wide_ref[:, :width]))
        first = first_norm * vector(3) + vector(4)
        first_low = first.astype(bf16)
        first_all[rows, :] = first_low
        outer = None
        for cut in chunks:
            inner = nn(first_low, wide_ref[:, width + cut.start : width + cut.stop]) + bias_ref[:, cut].astype(f32)
            cumulative = 0.5 * (1.0 + lax.erf(inner * math.sqrt(0.5)))
            act_low = (inner * cumulative).astype(bf16)
            act[rows, cut] = act_low
            slope[:, cut] = cumulative + inner * (jnp.exp(-0.5 * inner * inner) * (1.0 / math.sqrt(2.0 * math.pi)))
            part = nn(act_low, outer_ref[cut, :])
            outer = part if outer is None else outer + part
        second_norm, second_inverse = normalize(first + outer + vector(5))
        layer_ref[...] = (second_norm * vector(6) + vector(7)).astype(bf16)
        cotangent = cotangent_ref[...].astype(f32)
        mid_grad = norm_back(cotangent * vector(6), second_norm, second_inverse)
        outer_low = mid_grad.astype(bf16)
        outer_all[rows, :] = outer_low
        first_grad = mid_grad
        for cut in chunks:
            inner_grad = nt(outer_low, outer_ref[cut, :]) * slope[:, cut]
            inner_low = inner_grad.astype(bf16)
            back[rows, cut] = inner_low
            inner_sums_ref[0:1, cut] += column_sum(inner_low.astype(f32))
            first_grad = first_grad + nt(inner_low, wide_ref[:, width + cut.start : width + cut.stop])
        sum_grad = norm_back(first_grad * vector(3), first_norm, first_inverse)
        sum_ref[...] = sum_grad
        attended_low = sum_grad.astype(bf16)
        attended_all[rows, :] = attended_low
        context_grad_ref[...] = nt(attended_low, wide_ref[:, :width]).astype(bf16)
        for j, term in enumerate(
            (first_grad * first_norm, first_grad, outer_low.astype(f32), cotangent * second_norm, cotangent)
        ):
            sums_ref[j : j + 1, :] += column_sum(term)

    @pl.when((step >= blocks) & (step < blocks + len(chunks)))
    def _():
        cut = pl.ds(pl.multiple_of((step - blocks) * width, width), width)
        outer_out[...] = tn(act[:, cut], outer_all[...]).astype(bf16)
        inner_out[...] = tn(first_all[...], back[:, cut]).astype(bf16)

    @pl.when(step == blocks + len(chunks))
    def _():
        output_out[...] = tn(context_all[...], attended_all[...]).astype(bf16)


def middle(context, pooled, cotangent, wide, outer, small, bias):
    rows, width = context.shape
    hidden = bias.shape[1]
    size = 256
    blocks, chunks = rows // size, hidden // width
    block = pl.BlockSpec((size, width), lambda i: (jnp.minimum(i, blocks - 1), 0))
    chunk = lambda i: jnp.clip(i - blocks, 0, chunks - 1)
    low = jax.ShapeDtypeStruct((rows, width), bf16)
    flops = 18 * rows * width * hidden
    return pl.pallas_call(
        functools.partial(middle_kernel, blocks),
        name="middle",
        grid=(blocks + chunks + 1,),
        out_shape=(
            low,
            jax.ShapeDtypeStruct((rows, width), f32),
            low,
            jax.ShapeDtypeStruct((8, width), f32),
            jax.ShapeDtypeStruct((8, hidden), f32),
            jax.ShapeDtypeStruct((width, width), bf16),
            jax.ShapeDtypeStruct((width, hidden), bf16),
            jax.ShapeDtypeStruct((hidden, width), bf16),
        ),
        in_specs=[block, block, block, fixed(*wide.shape), fixed(*outer.shape), fixed(*small.shape), fixed(*bias.shape)],
        out_specs=[
            block, block, block, fixed(8, width), fixed(8, hidden), fixed(width, width),
            pl.BlockSpec((width, width), lambda i: (0, chunk(i))),
            pl.BlockSpec((width, width), lambda i: (chunk(i), 0)),
        ],
        scratch_shapes=[
            pltpu.VMEM((rows, hidden), bf16),
            pltpu.VMEM((rows, hidden), bf16),
            pltpu.VMEM((size, hidden), f32),
            pltpu.VMEM((rows, width), bf16),
            pltpu.VMEM((rows, width), bf16),
            pltpu.VMEM((rows, width), bf16),
            pltpu.VMEM((rows, width), bf16),
        ],
        compiler_params=pltpu.CompilerParams(vmem_limit_bytes=60 << 20),
        cost_estimate=pl.CostEstimate(flops=flops, bytes_accessed=40 * rows * width, transcendentals=2 * rows * hidden),
    )(context, pooled, cotangent, wide, outer, small, bias)


def tail_kernel(tokens_ref, key_ref, value_ref, query_ref, pooled_ref, weight_grad_ref, total):
    step = pl.program_id(0)
    width = tokens_ref.shape[1]

    @pl.when(step == 0)
    def _():
        total[...] = jnp.zeros(total.shape, f32)

    tokens = tokens_ref[...]
    total[:, :width] += tn(pooled_ref[...].astype(bf16), query_ref[...])
    total[:, width : 2 * width] += tn(tokens, key_ref[...])
    total[:, 2 * width :] += tn(tokens, value_ref[...])

    @pl.when(step == pl.num_programs(0) - 1)
    def _():
        weight_grad_ref[...] = total[...].astype(bf16)


def tail(tokens, key_low, value_low, query_low, pooled):
    length, width = tokens.shape
    block = 512
    whole = pl.BlockSpec((block, width), lambda i: (i, 0))
    half = pl.BlockSpec((block // 2, width), lambda i: (i, 0))
    return pl.pallas_call(
        tail_kernel,
        name="tail",
        grid=(length // block,),
        out_shape=jax.ShapeDtypeStruct((width, 3 * width), bf16),
        in_specs=[whole, whole, whole, half, half],
        out_specs=fixed(width, 3 * width),
        scratch_shapes=[pltpu.VMEM((width, 3 * width), f32)],
        compiler_params=pltpu.CompilerParams(vmem_limit_bytes=VMEM_ALL),
        cost_estimate=pl.CostEstimate(flops=5 * length * width * width, bytes_accessed=8 * length * width, transcendentals=0),
    )(tokens, key_low, value_low, query_low, pooled)


def tokens_block(block, key_ref, value_ref, query_ref, sum_ref, mix_ref, weight_ref):
    width = key_ref.shape[1]
    whole, half = (pl.ds(pl.multiple_of(block * rows, rows), rows) for rows in (256, 128))
    pooled_grad = sum_ref[half, :] + nt(query_ref[half, :], weight_ref[:, :width])
    coarse = pooled_grad.astype(bf16)
    fine = (pooled_grad - coarse.astype(f32)).astype(bf16)
    own = mix_ref[half, :1]
    mix = mixing(own, 1.0 - own)
    return (
        tn(mix, coarse) + tn(mix, fine)
        + nt(key_ref[whole, :], weight_ref[:, width : 2 * width])
        + nt(value_ref[whole, :], weight_ref[:, 2 * width :])
    )


def pack_kernel(count, folds, *refs):
    squares, (output_ref, inner_ref, relative_ref, order_ref) = refs[:3], refs[3:7]
    vectors, bias_ref = refs[7 : 7 + count], refs[7 + count]
    wide_ref, small_ref, projections_ref = refs[8 + count :]
    width = output_ref.shape[1]
    each = relative_ref.shape[1]
    for j, ref in enumerate(squares):
        projections_ref[:, j * width : (j + 1) * width] = ref[...]
    wide_ref[:, :width] = output_ref[...]
    wide_ref[:, width:] = inner_ref[...]
    small_ref[...] = jnp.zeros(small_ref.shape, bf16)
    rows = [relative_ref[...].astype(f32), order_ref[...].astype(f32)]
    rows += [ref[...].astype(f32).reshape(1, each) for ref in vectors]
    bias = bias_ref[...].astype(f32).reshape(1, folds * each)
    rows += [bias[:, j * each : (j + 1) * each] for j in range(folds)]
    small_ref[: FIRST_VECTOR + count + folds, :each] = jnp.concatenate(rows, 0).astype(bf16)


def pack(squares, output, inner, relative, order, vectors, bias, folds):
    rows = -(-(FIRST_VECTOR + len(vectors) + folds) // 16) * 16
    return pl.pallas_call(
        functools.partial(pack_kernel, len(vectors), folds),
        name="pack",
        out_shape=(
            jax.ShapeDtypeStruct((output.shape[0], output.shape[1] + inner.shape[1]), bf16),
            jax.ShapeDtypeStruct((rows, 128), bf16),
            jax.ShapeDtypeStruct((output.shape[0], 3 * output.shape[1]), bf16),
        ),
        cost_estimate=pl.CostEstimate(flops=0, bytes_accessed=4 * inner.size, transcendentals=0),
    )(*squares, output, inner, relative, order, *vectors, bias)


def finish_kernel(count, folds, projection_ref, output_ref, inner_ref, outer_ref, small_ref, *outs):
    width = output_ref.shape[1]
    squares, (output_out, inner_out, outer_out, relative_out, order_out) = outs[:3], outs[3:8]
    vectors, bias_out = outs[8 : 8 + count], outs[8 + count]
    each = relative_out.shape[1]
    for j, ref in enumerate(squares):
        ref[...] = projection_ref[:, j * width : (j + 1) * width]
    output_out[...] = output_ref[...]
    inner_out[...] = inner_ref[...]
    outer_out[...] = outer_ref[...]
    small = small_ref[...]
    relative_out[...] = small[:32, :each]
    order_out[...] = small[32:34, :each]
    for j, ref in enumerate(vectors):
        ref[...] = small[FIRST_VECTOR + j, :each]
    start = FIRST_VECTOR + count
    bias_out[...] = jnp.concatenate([small[start + j : start + j + 1, :each] for j in range(folds)], 1).reshape(folds * each)


def finish(projection, output, inner, outer, small, count, folds):
    each, width = small.shape[0], output.shape[1]
    rows = output.shape[0]
    shape = lambda *s: jax.ShapeDtypeStruct(s, f32)
    return pl.pallas_call(
        functools.partial(finish_kernel, count, folds),
        name="finish",
        out_shape=(
            [shape(rows, width)] * 4 + [shape(*inner.shape), shape(*outer.shape), shape(32, rows), shape(2, rows)]
            + [shape(rows)] * count + [shape(folds * rows)]
        ),
        cost_estimate=pl.CostEstimate(flops=0, bytes_accessed=8 * inner.size, transcendentals=0),
    )(projection, output, inner, outer, small)


def unpack_kernel(shards, folds, start, small_ref, segment_ref, relative_out, order_out, vectors_out, bias_out, hot_out, away_out, behind_out, ahead_out):
    each = relative_out.shape[1] // shards
    length = segment_ref.shape[1]
    own = [small_ref[s].astype(f32) for s in range(shards)]
    whole = jnp.concatenate([piece[:start, :each] for piece in own], 1).astype(bf16)
    relative_out[...] = whole[:32]
    order_out[...] = whole[32:34]
    vectors_out[: start - 32, :] = whole[32:]
    bias_out[...] = jnp.concatenate(
        [piece[start + j : start + j + 1, :each] for piece in own for j in range(folds)], 1
    ).astype(bf16)
    document = lax.broadcasted_iota(jnp.int32, (128, length), 0)
    same = jnp.where(segment_ref[...] == document, 1.0, 0.0).T
    counted = lax.broadcasted_iota(jnp.int32, same.shape, 1) < 8
    hot_out[...] = same.astype(bf16)
    away_out[256 : 256 + length, :] = jnp.where(counted, -BIG * (1.0 - same), 0.0).astype(bf16)
    pad = jnp.where(counted[:256], -BIG, 0.0).astype(bf16)
    away_out[:256, :] = pad
    away_out[256 + length :, :] = pad
    blocks = behind_out.shape[0]
    own_row = jnp.broadcast_to(segment_ref[...], (blocks, length))
    lane = lax.broadcasted_iota(jnp.int32, (blocks, length), 1)
    start = 2 * BQ * lax.broadcasted_iota(jnp.int32, (blocks, length), 0)
    total = lambda values: jnp.sum(values, axis=1, keepdims=True)
    at = lambda place: total(jnp.where(lane == place, own_row, 0))
    first = total(jnp.where(own_row < at(start), 1, 0))
    last = total(jnp.where(own_row <= at(start + 2 * BQ - 2), 1, 0))
    chunks = lambda rest: lax.shift_right_logical(jnp.maximum(rest + CHUNK - 1, 0), CHUNK.bit_length() - 1)
    behind_out[...] = chunks(start[:, :128] - 256 - first)
    ahead_out[...] = chunks(last - (start[:, :128] - 256 + NEAR))


def unpack(small, segments, width, count, folds):
    shards = small.shape[0]
    length = segments.shape[1]
    start = FIRST_VECTOR + count
    shape = lambda *s: jax.ShapeDtypeStruct(s, bf16)
    return pl.pallas_call(
        functools.partial(unpack_kernel, shards, folds, start),
        name="unpack",
        out_shape=(shape(32, width), shape(2, width), shape(16, width), shape(1, folds * width), shape(length, 128), shape(length + 512, 128))
        + (jax.ShapeDtypeStruct((length // (2 * BQ), 128), jnp.int32),) * 2,
        compiler_params=pltpu.CompilerParams(vmem_limit_bytes=VMEM_ALL),
        cost_estimate=pl.CostEstimate(flops=0, bytes_accessed=1 << 20, transcendentals=0),
    )(small, segments)


def collect_kernel(folds, relative_ref, order_ref, bias_ref, sums_ref, inner_ref, out_ref):
    shards, rows, _ = out_ref.shape
    width = relative_ref.shape[1]
    each = width // shards
    whole = jnp.concatenate([relative_ref[...], order_ref[:2], bias_ref[:3], sums_ref[:5]], 0)
    inner = inner_ref[0:1, :]
    out_ref[...] = jnp.zeros(out_ref.shape, bf16)
    for s in range(shards):
        cut = slice(s * each, s * each + each)
        own = [inner[:, (s * folds + j) * each : (s * folds + j + 1) * each] for j in range(folds)]
        piece = jnp.concatenate([whole[:, cut], *own], 0)
        out_ref[s, : piece.shape[0], :each] = piece.astype(bf16)


def collect(relative, order, bias, sums, inner, shards, count, folds):
    rows = -(-(FIRST_VECTOR + count + folds) // 16) * 16
    return pl.pallas_call(
        functools.partial(collect_kernel, folds),
        name="collect",
        out_shape=jax.ShapeDtypeStruct((shards, rows, 128), bf16),
        compiler_params=pltpu.CompilerParams(vmem_limit_bytes=VMEM_ALL),
        cost_estimate=pl.CostEstimate(flops=0, bytes_accessed=1 << 19, transcendentals=0),
    )(relative, order, bias, sums, inner)


def body(
    mesh,
    tokens,
    segment_ids,
    query_weight,
    key_weight,
    value_weight,
    output_weight,
    relative_table,
    order_table,
    content_bias,
    position_bias,
    order_bias,
    first_gain,
    first_shift,
    inner_weight,
    inner_bias,
    outer_weight,
    outer_bias,
    second_gain,
    second_shift,
    cotangent,
):
    shards = mesh.shape["shard"]
    width = tokens.shape[1]
    hidden = inner_weight.shape[1]
    each = width // shards
    folds = hidden // width
    vectors = (content_bias, position_bias, order_bias, first_gain, first_shift, outer_bias, second_gain, second_shift)
    wide_own, small, projections_own = pack(
        (query_weight, key_weight, value_weight), output_weight, inner_weight, relative_table, order_table, vectors, inner_bias, folds
    )
    projections, small_all = gather(mesh, [projections_own, small], 0)
    projections = projections.reshape(width, 3 * width)
    weight_relative, weight_order, small_all, bias_inner, hot, away, behind, ahead = unpack(
        small_all, segment_ids, width, len(vectors), folds
    )
    wide = lax.all_gather(wide_own, "shard", axis=0, tiled=True)
    weight_outer = lax.all_gather(outer_weight, "shard", axis=0, tiled=True)

    pooled, content, position, ordering, keys, values, document, mix = project(tokens, hot, projections, small_all)
    probs, context, mixed, inverse = attend(
        behind, ahead, content, position, ordering, keys, values, weight_relative, weight_order, away, document
    )
    layer_out, sum_grad, context_grad, sums, inner_sums, output_grad, inner_grad, outer_grad = middle(
        context, pooled, cotangent, wide, weight_outer, small_all, bias_inner
    )
    query_low, key_low, value_low, relative_grad, order_grad, bias_sums = attend_back(
        behind, ahead, probs, context_grad, mixed, inverse, content, position, ordering,
        keys, values, weight_relative, weight_order,
    )
    projection_grad = tail(tokens, key_low, value_low, query_low, pooled)
    small_grad = collect(relative_grad, order_grad, bias_sums, sums, inner_sums, shards, len(vectors), folds)
    outer_part = lax.psum_scatter(outer_grad, "shard", scatter_dimension=0, tiled=True)
    inner_sum, output_sum, projection_sum, small_sum, outer_sum, tokens_grad = scatter(
        mesh,
        [
            inner_grad.reshape(shards, each, hidden),
            output_grad.reshape(shards, each, width),
            projection_grad.reshape(shards, each, 3 * width),
            small_grad,
        ],
        [width, width, width, 128],
        [outer_part],
        [key_low, value_low, query_low, sum_grad, mix, projections],
        tokens_block,
        1,
    )
    parts = finish(projection_sum, output_sum, inner_sum, outer_sum, small_sum, len(vectors), folds)
    squares, (inner_sum, outer_sum, relative_sum, order_sum) = parts[:4], parts[4:8]
    own, bias_sum = parts[8:-1], parts[-1]
    return (
        layer_out, tokens_grad, *squares, relative_sum, order_sum, *own[:5],
        inner_sum, bias_sum, outer_sum, *own[5:],
    )


def solution(mesh):
    placed = (
        P(("rep", "shard"), None),
        P(("rep", "shard"), None),
        P("shard", None),
        P("shard", None),
        P("shard", None),
        P("shard", None),
        P(None, "shard"),
        P(None, "shard"),
        P("shard"),
        P("shard"),
        P("shard"),
        P("shard"),
        P("shard"),
        P("shard", None),
        P("shard"),
        P("shard", None),
        P("shard"),
        P("shard"),
        P("shard"),
        P(("rep", "shard"), None),
    )
    return jax.shard_map(
        functools.partial(body, mesh),
        mesh=mesh,
        in_specs=placed,
        out_specs=(
            P(("rep", "shard"), None),
            P(("rep", "shard"), None),
            P("shard", None),
            P("shard", None),
            P("shard", None),
            P("shard", None),
            P(None, "shard"),
            P(None, "shard"),
            P("shard"),
            P("shard"),
            P("shard"),
            P("shard"),
            P("shard"),
            P("shard", None),
            P("shard"),
            P("shard", None),
            P("shard"),
            P("shard"),
            P("shard"),
        ),
        check_vma=False,
    )
```
